32 devices in a mesh: seq: 2 (over x), shard: 16 (over z, y, core).
Axes of the slice: x: 2, y: 2, z: 4, core: 2. Of those that a mesh axis runs over, the one named last changes fastest.
Arguments:
- tokens: bfloat16 [2, 16, 1024, 768], P(None, 'shard', 'seq'), may hold values from -6 to 6
- kinds: int32 [2, 16, 1024], P(None, 'shard', 'seq'), may hold values 0 or 1
- groups: int32 [2, 16, 1024], P(None, 'shard', 'seq'), may hold values from 0 to 7, never falling along the last dimension, each value on 1 to 512 neighbouring positions
- query_weight: bfloat16 [768, 3072], P('shard'), may hold values from -0.21875 to 0.21875
- query_bias: bfloat16 [3072], P('shard'), may hold values from -3 to 3
- key_weight: bfloat16 [768, 768], P('shard'), may hold values from -0.21875 to 0.21875
- key_bias: bfloat16 [768], P('shard'), may hold values from -3 to 3
- value_weight: bfloat16 [768, 768], P('shard'), may hold values from -0.21875 to 0.21875
- value_bias: bfloat16 [768], P('shard'), may hold values from -3 to 3
- output_weight: bfloat16 [768, 768], P('shard'), may hold values from -0.875 to 0.875
- output_bias: bfloat16 [768], P('shard'), may hold values from -2 to 2
- norm1_gain: bfloat16 [768], P('shard'), may hold values from 0.5 to 1.5
- norm1_shift: bfloat16 [768], P('shard'), may hold values from -2 to 2
- up_weight: bfloat16 [768, 3072], P('shard'), may hold values from -0.21875 to 0.21875
- up_bias: bfloat16 [3072], P('shard'), may hold values from -3 to 3
- down_weight: bfloat16 [3072, 768], P('shard'), may hold values from -0.109375 to 0.109375
- down_bias: bfloat16 [768], P('shard'), may hold values from -2 to 2
- norm2_gain: bfloat16 [768], P('shard'), may hold values from 0.5 to 1.5
- norm2_shift: bfloat16 [768], P('shard'), may hold values from -2 to 2
- cotangent: bfloat16 [2, 16, 1024, 768], P(None, 'shard', 'seq'), may hold values from -6 to 6
Outputs:
- mixed: bfloat16 [2, 16, 1024, 768], P(None, 'shard', 'seq')
- input_grad: float32 [2, 16, 1024, 768], P(None, 'shard', 'seq')
- query_weight_grad: float32 [768, 3072], P('shard')
- query_bias_grad: float32 [3072], P('shard')
- key_weight_grad: float32 [768, 768], P('shard')
- key_bias_grad: float32 [768], P('shard')
- value_weight_grad: float32 [768, 768], P('shard')
- value_bias_grad: float32 [768], P('shard')
- output_weight_grad: float32 [768, 768], P('shard')
- output_bias_grad: float32 [768], P('shard')
- norm1_gain_grad: float32 [768], P('shard')
- norm1_shift_grad: float32 [768], P('shard')
- up_weight_grad: float32 [768, 3072], P('shard')
- up_bias_grad: float32 [3072], P('shard')
- down_weight_grad: float32 [3072, 768], P('shard')
- down_bias_grad: float32 [768], P('shard')
- norm2_gain_grad: float32 [768], P('shard')
- norm2_shift_grad: float32 [768], P('shard')
The draws below stay inside these ranges and needn't reach their ends.
Inputs may be any that keep to these rules, and one draw needn't show every extreme that they name: `kinds`: 1 marks an entity token, 0 a word token. `groups`: document numbers never fall along a sequence; every document holds 1 to 512 tokens.
All inputs are finite; a program needn't handle non-finite values. No bound on the sum of `kinds` on one device may be relied on, other than what follows from the above.
Results may differ from the reference program's by a relative error of at most 0.02.
Values may be sent and summed in bfloat16 or wider, within the bound.
A program may use at most 192 MiB of HBM per device.

```python
import math
import jax
import jax.numpy as jnp
import numpy as np
from jax import lax

D = 768
HEADS = 12
FF = 3072
MICRO = 2
DOCS = 8
LEN = 1024
SEQS = 16


def plant(result, rng, smallest, high):
    index_at = [jax.random.randint(jax.random.fold_in(rng, axis), (), 0, length) for axis, length in enumerate(result.shape)]
    longest = result.shape.index(max(result.shape))
    beside = index_at[:longest] + [(index_at[longest] + 1) % result.shape[longest]] + index_at[longest + 1:]
    return result.at[tuple(index_at)].set(smallest).at[tuple(beside)].set(high)


def spiked(values, stream_key, source, target, parts, factor):
    def block_of(axis_at):
        return (jnp.arange(values.shape[axis_at]) // (values.shape[axis_at] // parts)).reshape((-1,) + (1,) * (values.ndim - 1 - axis_at))

    one_side = jax.random.permutation(stream_key, parts)[block_of(target)]
    second = (block_of(target) + parts // 2) % parts
    return jnp.where((block_of(source) == one_side) | (block_of(source) == second), factor * values, values)


def level_of(stream_key, extent, split, smallest, top_value):
    level, own = 1.0, jax.random.fold_in(stream_key, 6)
    for axis_at, blocks in split:
        heights = jnp.exp(jax.random.uniform(jax.random.fold_in(own, axis_at), (blocks,), jnp.float32, smallest / len(split), top_value / len(split)))
        level = level * jnp.repeat(heights, extent[axis_at] // blocks).reshape([-1 if axis == axis_at else 1 for axis in range(len(extent))])
    return level


def split_up(number_of, total, most, slope):
    portions = [(1 << 20) // math.isqrt(standing ** slope) + 1 for standing in range(2, number_of + 1)]
    spare, holding = total - most - (number_of - 1), [1] * (number_of - 1)
    while spare > 0:
        free = [i for i in range(number_of - 1) if holding[i] < most]
        pool, budget = sum([portions[i] for i in free]), spare
        for i in free:
            addition = min(most - holding[i], max(1, budget * portions[i] // pool), spare)
            holding[i] = holding[i] + addition
            spare = spare - addition
    return np.array([most] + holding)


def ragged(own_key, count, total, most, slope):
    if count == 2:
        one = jax.random.randint(own_key, (), max(1, total - most), min(most, total - 1) + 1)
        return jnp.stack([one, total - one])
    sizes = jnp.asarray(split_up(count, total, most, slope), jnp.int32)
    twos = (count - 1) // 2
    source_of, sink = sizes[1:1 + 2 * twos:2], sizes[2:2 + 2 * twos:2]
    margin = jnp.minimum(source_of - 1, most - sink)
    moved = jax.random.randint(jax.random.fold_in(own_key, 1), (twos,), 0, 1 << 20) % (margin + 1)
    sizes = sizes.at[1:1 + 2 * twos:2].set(source_of - moved).at[2:2 + 2 * twos:2].set(sink + moved)
    return sizes[jax.random.permutation(jax.random.fold_in(own_key, 2), count)]


def centred(own_key, dims, width, most, cuts=(), kind=jnp.bfloat16):
    gain = level_of(own_key, dims, cuts, -0.22, 0.18) if cuts else 1.0
    drawn = jax.random.normal(own_key, dims, jnp.float32) * width * gain
    return jnp.minimum(jnp.maximum(drawn, -most), most).astype(kind)


def gaussian_with(stream_key, dims, width, limit, split, heavy, dtype=jnp.bfloat16):
    drawn = width * jax.random.normal(stream_key, dims, jnp.float32)
    if split:
        drawn = drawn * level_of(stream_key, dims, split, -0.22, 0.18)
    return jnp.clip(spiked(drawn, jax.random.fold_in(stream_key, 3), *heavy), -limit, limit).astype(dtype)


def setup_inputs(seed: int = 0) -> dict:
    seeds = jax.random.split(jax.random.key(seed), 21)
    tokens = centred(seeds[0], (MICRO, SEQS, LEN, D), 1.0, 6.0, ((1, 16), (2, 2)))
    kinds = plant((jax.random.randint(seeds[1], (MICRO, SEQS, LEN), 0, 4) < 1).astype(jnp.int32), jax.random.fold_in(seeds[1], 1), 0, 1)
    groups = jax.vmap(lambda own: jnp.searchsorted(jnp.cumsum(ragged(own, DOCS, LEN, LEN // 2, 2)), jnp.arange(LEN), side="right"))(jax.random.split(seeds[2], MICRO * SEQS)).reshape((MICRO, SEQS, LEN)).astype(jnp.int32)
    query_weight = centred(seeds[3], (D, 4 * D), D ** -0.5, 0.21875, ((0, 16),))
    query_bias = centred(seeds[4], (4 * D,), 0.5, 3.0, ((0, 16),))
    key_weight = centred(seeds[5], (D, D), D ** -0.5, 0.21875, ((0, 16),))
    key_bias = centred(seeds[6], (D,), 0.5, 3.0, ((0, 16),))
    value_weight = centred(seeds[7], (D, D), D ** -0.5, 0.21875, ((0, 16),))
    value_bias = centred(seeds[8], (D,), 0.5, 3.0, ((0, 16),))
    output_weight = centred(seeds[9], (D, D), (D // 16) ** -0.5, 0.875, ((0, 16),))
    output_bias = centred(seeds[10], (D,), 0.3, 2.0, ((0, 16),))
    norm1_gain = jnp.clip(1.0 + 0.1 * jax.random.normal(seeds[11], (D,), jnp.float32), 0.5, 1.5).astype(jnp.bfloat16)
    norm1_shift = centred(seeds[12], (D,), 0.3, 2.0, ((0, 16),))
    up_weight = centred(seeds[13], (D, FF), D ** -0.5, 0.21875, ((0, 16),))
    up_bias = centred(seeds[14], (FF,), 0.5, 3.0, ((0, 16),))
    down_weight = centred(seeds[15], (FF, D), FF ** -0.5, 0.109375, ((0, 16),))
    down_bias = centred(seeds[16], (D,), 0.3, 2.0, ((0, 16),))
    norm2_gain = jnp.clip(1.0 + 0.1 * jax.random.normal(seeds[17], (D,), jnp.float32), 0.5, 1.5).astype(jnp.bfloat16)
    norm2_shift = centred(seeds[18], (D,), 0.3, 2.0, ((0, 16),))
    cotangent = gaussian_with(seeds[19], (MICRO, SEQS, LEN, D), 1.0, 6.0, ((1, 16), (2, 2)), (1, 3, 16, 2.0))
    return dict(tokens=tokens, kinds=kinds, groups=groups, query_weight=query_weight, query_bias=query_bias, key_weight=key_weight, key_bias=key_bias, value_weight=value_weight, value_bias=value_bias, output_weight=output_weight, output_bias=output_bias, norm1_gain=norm1_gain, norm1_shift=norm1_shift, up_weight=up_weight, up_bias=up_bias, down_weight=down_weight, down_bias=down_bias, norm2_gain=norm2_gain, norm2_shift=norm2_shift, cotangent=cotangent)


@jax.custom_vjp
def low(v):
    return lax.optimization_barrier(v.astype(jnp.bfloat16)).astype(jnp.float32)

@jax.custom_vjp
def low_back(v):
    return v

def low_keep(v):
    return (low(v), None)

def low_pass(kept, grad):
    return (grad,)

def back_keep(v):
    return (v, None)

def back_low(kept, grad):
    return (low(grad),)
low.defvjp(low_keep, low_pass)
low_back.defvjp(back_keep, back_low)

def matmul(left_side, right_side):
    return jnp.dot(left_side, right_side, precision=lax.Precision.HIGHEST)

def layer_norm(hidden, norm_gain, norm_shift):
    center = hidden - lax.optimization_barrier(jnp.mean(hidden, axis=-1, keepdims=True))
    variance = lax.optimization_barrier(jnp.mean(center * center, axis=-1, keepdims=True))
    return center * lax.rsqrt(variance + 1e-12) * norm_gain + norm_shift

def one_sequence(params, seq_tokens, seq_kinds, seq_groups):
    query_weight, query_bias, key_weight, key_bias, value_weight, value_bias, output_weight, output_bias, norm1_gain, norm1_shift, up_weight, up_bias, down_weight, down_bias, norm2_gain, norm2_shift = params
    length = seq_tokens.shape[0]
    head_dim = D // HEADS
    entity = (seq_kinds == 1)[:, None]
    queries = matmul(seq_tokens, query_weight) + query_bias
    query_word = low(low_back(jnp.where(entity, queries[:, 2 * D:3 * D], queries[:, :D])))
    query_entity = low(low_back(jnp.where(entity, queries[:, 3 * D:], queries[:, D:2 * D])))
    keys = low(low_back(matmul(seq_tokens, key_weight) + key_bias))
    values = low(low_back(matmul(seq_tokens, value_weight) + value_bias))

    def by_heads(array):
        return array.reshape(length, HEADS, head_dim).transpose(1, 0, 2)
    word_scores = jnp.einsum('hqd,hkd->hqk', by_heads(query_word), by_heads(keys), precision=lax.Precision.HIGHEST)
    entity_scores = jnp.einsum('hqd,hkd->hqk', by_heads(query_entity), by_heads(keys), precision=lax.Precision.HIGHEST)
    raw_scores = jnp.where((seq_kinds == 1)[None, None, :], entity_scores, word_scores) * head_dim ** (-0.5)
    scores = low_back(raw_scores)
    same_doc = (seq_groups[:, None] == seq_groups[None, :])[None]
    scores = jnp.where(same_doc, scores, -1e+30)
    weights = low(jax.nn.softmax(scores, axis=-1))
    context = jnp.einsum('hqk,hkd->hqd', weights, by_heads(values), precision=lax.Precision.HIGHEST)
    context = low(low_back(context.transpose(1, 0, 2).reshape(length, D)))
    attended = low_back(matmul(context, output_weight) + output_bias)
    first_out = layer_norm(seq_tokens + attended, norm1_gain, norm1_shift)
    up_out = low_back(matmul(low(first_out), up_weight) + up_bias)
    activated = low(jax.nn.gelu(up_out, approximate=False))
    down_out = low_back(matmul(activated, down_weight) + down_bias)
    return layer_norm(first_out + down_out, norm2_gain, norm2_shift)

def reference(tokens, kinds, groups, query_weight, query_bias, key_weight, key_bias, value_weight, value_bias, output_weight, output_bias, norm1_gain, norm1_shift, up_weight, up_bias, down_weight, down_bias, norm2_gain, norm2_shift, cotangent):
    params = (query_weight.astype(jnp.float32), query_bias.astype(jnp.float32), key_weight.astype(jnp.float32), key_bias.astype(jnp.float32), value_weight.astype(jnp.float32), value_bias.astype(jnp.float32), output_weight.astype(jnp.float32), output_bias.astype(jnp.float32), norm1_gain.astype(jnp.float32), norm1_shift.astype(jnp.float32), up_weight.astype(jnp.float32), up_bias.astype(jnp.float32), down_weight.astype(jnp.float32), down_bias.astype(jnp.float32), norm2_gain.astype(jnp.float32), norm2_shift.astype(jnp.float32))
    flat_tokens = tokens.astype(jnp.float32).reshape(-1, LEN, D)
    flat_kinds = kinds.reshape(-1, LEN)
    flat_groups = groups.reshape(-1, LEN)

    def forward(weights, inputs):

        def one_step(sequence_items):
            return one_sequence(weights, sequence_items[0], sequence_items[1], sequence_items[2])
        return lax.map(jax.checkpoint(one_step), (inputs, flat_kinds, flat_groups))
    mixed, pullback = jax.vjp(forward, params, flat_tokens)
    param_grads, input_grad = pullback(cotangent.astype(jnp.float32).reshape(mixed.shape))
    return (mixed.astype(jnp.bfloat16).reshape(tokens.shape), input_grad.reshape(tokens.shape), param_grads[0], param_grads[1], param_grads[2], param_grads[3], param_grads[4], param_grads[5], param_grads[6], param_grads[7], param_grads[8], param_grads[9], param_grads[10], param_grads[11], param_grads[12], param_grads[13], param_grads[14], param_grads[15])
```

```python
import functools

import jax
import jax.numpy as jnp
from jax import lax
from jax.experimental import pallas as pl
from jax.experimental.pallas import tpu as pltpu
from jax.sharding import PartitionSpec as P

HEADS = 12
GROUPS = 16
BLOCK = 256
masked_score = -1e30
layer_eps = 1e-12
bf16 = jnp.bfloat16
f32 = jnp.float32
VMEM_LIMIT = 60 * 1024 * 1024


def nn(a, b):
    return lax.dot_general(a, b, (((1,), (0,)), ((), ())), preferred_element_type=f32)


def nt(a, b):
    return lax.dot_general(a, b, (((1,), (1,)), ((), ())), preferred_element_type=f32)


def tn(a, b):
    return lax.dot_general(a, b, (((0,), (0,)), ((), ())), preferred_element_type=f32)


def swap(value):
    return lax.ppermute(value, "seq", [(0, 1), (1, 0)])


def cost(flops, moved, trans=0):
    return pl.CostEstimate(flops=flops, bytes_accessed=moved, transcendentals=trans)


def low_lanes(shape):
    return lax.broadcasted_iota(jnp.int32, shape, len(shape) - 1) % 128 < 64


def pack_kernel(side_ref, q_ref, k_ref, v_ref, vec_ref, out_ref):
    rows, width = k_ref.shape
    half = width // 2
    first = side_ref[0] == 0

    def own(ref, base):
        return jnp.where(
            first,
            ref[:, base : base + half].astype(f32),
            ref[:, base + half : base + width].astype(f32),
        )

    lo = low_lanes((rows, 128))
    for e in range(2):
        word = own(q_ref, 2 * e * width)
        entity = own(q_ref, (2 * e + 1) * width)
        for t in range(half // 128):
            a = word[:, 128 * t : 128 * t + 128]
            b = entity[:, 128 * t : 128 * t + 128]
            even = jnp.where(lo, a, pltpu.roll(b, 64, 1))
            odd = jnp.where(lo, pltpu.roll(a, 64, 1), b)
            out_ref[e * rows : e * rows + rows, 256 * t : 256 * t + 128] = even.astype(bf16)
            out_ref[e * rows : e * rows + rows, 256 * t + 128 : 256 * t + 256] = odd.astype(bf16)
    out_ref[2 * rows : 3 * rows, :half] = own(k_ref, 0).astype(bf16)
    out_ref[2 * rows : 3 * rows, half:] = own(v_ref, 0).astype(bf16)
    out_ref[3 * rows :, :] = jnp.broadcast_to(vec_ref[...], (16, width))


def pair_columns(columns, side, head_dim):
    lead = columns.shape[:-1]
    per = columns.shape[-1] // (8 * head_dim)
    view = columns.reshape(lead + (2, 2, 2, per, head_dim))
    view = jnp.where(side == 0, view[..., 0, :, :], view[..., 1, :, :])
    return jnp.swapaxes(view, -3, -2).reshape(lead + (2, -1))


def unpair_columns(pairs, head_dim):
    lead = pairs.shape[:-2]
    per = pairs.shape[-1] // (2 * head_dim)
    view = pairs.reshape(lead + (2, per, 2, head_dim))
    return jnp.swapaxes(view, -3, -2).reshape(lead + (2, 2, per * head_dim))


def own_half(columns, side):
    half = columns.shape[-1] // 2
    return jnp.where(side == 0, columns[..., :half], columns[..., half:])


def pack_attention(query_weight, key_weight, value_weight, vector, side, head_dim):
    rows, width = key_weight.shape
    if rows % 16 == 0:
        return pl.pallas_call(
            pack_kernel,
            out_shape=jax.ShapeDtypeStruct((3 * rows + 16, width), bf16),
            in_specs=[pl.BlockSpec(memory_space=pltpu.SMEM)]
            + [pl.BlockSpec(memory_space=pltpu.VMEM)] * 4,
            out_specs=pl.BlockSpec(memory_space=pltpu.VMEM),
            name="pack",
        )(side[None], query_weight, key_weight, value_weight, vector)
    pairs = pair_columns(query_weight, side, head_dim)
    key_value = jnp.concatenate([own_half(key_weight, side), own_half(value_weight, side)], axis=1)
    return jnp.concatenate(
        [pairs[:, 0], pairs[:, 1], key_value, jnp.broadcast_to(vector, (16, width))], axis=0
    )


def regroup(gathered, sizes):
    devices, _, width = gathered.shape
    pieces = []
    start = 0
    for size in sizes:
        piece = gathered[:, start : start + size].reshape(GROUPS, -1, width)
        pieces.append(piece)
        start += size
    return jnp.concatenate(pieces, axis=1)


def ungroup(grouped, sizes, devices):
    _, _, width = grouped.shape
    pieces = []
    start = 0
    for size in sizes:
        wide = size * devices // GROUPS
        pieces.append(grouped[:, start : start + wide].reshape(devices, size, width))
        start += wide
    return jnp.concatenate(pieces, axis=1)


def project_kernel(x_ref, w_ref, bias_ref, kind_ref, qp_ref, km_ref, kmt_ref, v_ref, vt_ref):
    width = x_ref.shape[1]
    half = width // 2
    rows = width // GROUPS
    x = x_ref[...]
    kind = kind_ref[...]
    wa = w_ref[:, 0:rows, :].reshape(width, width)
    wb = w_ref[:, rows : 2 * rows, :].reshape(width, width)
    wkv = w_ref[:, 2 * rows : 3 * rows, :].reshape(width, width)
    qa = nn(x, wa) + bias_ref[0:1, :]
    qb = nn(x, wb) + bias_ref[1:2, :]
    qp_ref[...] = (jnp.where(kind == 1, qb, qa) * 0.125).astype(bf16)
    kv = nn(x, wkv) + bias_ref[2:3, :]
    lane_high = (lax.broadcasted_iota(jnp.int32, (BLOCK, 128), 1) >= 64).astype(jnp.int32)
    keep = lane_high == kind
    lo = lane_high == 0
    for t in range(half // 128):
        k = kv[:, 128 * t : 128 * t + 128]
        r = pltpu.roll(k, 64, 1)
        even = jnp.where(keep, jnp.where(lo, k, r), 0.0)
        odd = jnp.where(keep, jnp.where(lo, r, k), 0.0)
        km_ref[:, 256 * t : 256 * t + 128] = even.astype(bf16)
        km_ref[:, 256 * t + 128 : 256 * t + 256] = odd.astype(bf16)
        kmt_ref[256 * t : 256 * t + 128, :] = even.T.astype(bf16)
        kmt_ref[256 * t + 128 : 256 * t + 256, :] = odd.T.astype(bf16)
    v = kv[:, half:]
    v_ref[...] = v.astype(bf16)
    vt_ref[...] = v.T.astype(bf16)


def project(xs, weights, bias_rows, kind_col):
    halves, micro, local, width = xs.shape
    half = width // 2
    sub = local // BLOCK

    def rows_spec(cols):
        return pl.BlockSpec((None, None, BLOCK, cols), lambda a, m, i: (a, m, i, 0))

    def cols_spec(count):
        return pl.BlockSpec((None, None, count, BLOCK), lambda a, m, i: (a, m, 0, i))

    def shape(*dims):
        return jax.ShapeDtypeStruct((halves, micro) + dims, bf16)

    tokens = halves * micro * local
    return pl.pallas_call(
        project_kernel,
        grid=(halves, micro, sub),
        in_specs=[
            rows_spec(width),
            pl.BlockSpec(weights.shape, lambda a, m, i: (0, 0, 0)),
            pl.BlockSpec(bias_rows.shape, lambda a, m, i: (0, 0)),
            rows_spec(1),
        ],
        out_specs=[rows_spec(width), rows_spec(width), cols_spec(width), rows_spec(half), cols_spec(half)],
        out_shape=[
            shape(local, width),
            shape(local, width),
            shape(width, local),
            shape(local, half),
            shape(half, local),
        ],
        compiler_params=pltpu.CompilerParams(vmem_limit_bytes=VMEM_LIMIT),
        cost_estimate=cost(2 * tokens * width * 3 * width, tokens * width * 10),
        name="project",
    )(xs, weights, bias_rows, kind_col)


def place(block, per):
    return block // per, pl.multiple_of(lax.rem(block, per) * BLOCK, BLOCK)


def attend_kernel(
    low_ref, high_ref, qp_ref, km_ref, vt_ref, gk_ref, gq_ref, c_ref, ct_ref, lse_ref, m_sc, l_sc, acc_sc
):
    micro_at = pl.program_id(0)
    local = qp_ref.shape[1]
    per = local // BLOCK
    blocks = 2 * per
    heads = qp_ref.shape[2] // 128
    base = micro_at * blocks

    @pl.loop(0, blocks)
    def _(qb):
        qh, qo = place(qb, per)
        m_sc[...] = jnp.full_like(m_sc, masked_score)
        l_sc[...] = jnp.zeros_like(l_sc)
        acc_sc[...] = jnp.zeros_like(acc_sc)
        q_low, q_high = low_ref[base + qb], high_ref[base + qb]

        @pl.loop(0, blocks)
        def _(kb):
            @pl.when((q_low <= high_ref[base + kb]) & (low_ref[base + kb] <= q_high))
            def _():
                kh, ko = place(kb, per)
                same = gk_ref[kh, pl.ds(ko, BLOCK), :] == gq_ref[qh, :, pl.ds(qo, BLOCK)]
                bias = jnp.where(same, 0.0, masked_score)
                for h in range(heads):
                    at = slice(128 * h, 128 * h + 128)
                    vat = slice(64 * h, 64 * h + 64)
                    s = nt(km_ref[kh, pl.ds(ko, BLOCK), at], qp_ref[qh, pl.ds(qo, BLOCK), at]) + bias
                    m_old = m_sc[h : h + 1, :]
                    m_new = jnp.maximum(m_old, jnp.max(s, axis=0, keepdims=True))
                    alpha = jnp.exp(m_old - m_new)
                    p = jnp.exp(s - m_new)
                    m_sc[h : h + 1, :] = m_new
                    l_sc[h : h + 1, :] = alpha * l_sc[h : h + 1, :] + jnp.sum(p, axis=0, keepdims=True)
                    acc_sc[vat, :] = alpha * acc_sc[vat, :] + nn(
                        vt_ref[kh, vat, pl.ds(ko, BLOCK)], p.astype(bf16)
                    )

        cols = pl.ds(pl.multiple_of(qb * BLOCK, BLOCK), BLOCK)
        for h in range(heads):
            vat = slice(64 * h, 64 * h + 64)
            total = l_sc[h : h + 1, :]
            ct_ref[vat, cols] = acc_sc[vat, :] / total
            lse_ref[h : h + 1, cols] = m_sc[h : h + 1, :] + jnp.log(total)
        c_ref[qh, pl.ds(qo, BLOCK), :] = ct_ref[:, cols].T.astype(bf16)


def whole_micro(array):
    rest = array.shape[2:]
    return pl.BlockSpec((array.shape[0], None) + rest, lambda m, *_: (0, m) + (0,) * len(rest))


def attend(low, high, qp, km, vt, gk, gq):
    halves, micro, local, width = qp.shape
    half = width // 2
    heads = width // 128
    length = halves * local
    return pl.pallas_call(
        attend_kernel,
        grid_spec=pltpu.PrefetchScalarGridSpec(
            num_scalar_prefetch=2,
            grid=(micro,),
            in_specs=[whole_micro(a) for a in (qp, km, vt, gk, gq)],
            out_specs=[
                pl.BlockSpec((halves, None, local, half), lambda m, *_: (0, m, 0, 0)),
                pl.BlockSpec((None, half, length), lambda m, *_: (m, 0, 0)),
                pl.BlockSpec((None, 8, length), lambda m, *_: (m, 0, 0)),
            ],
            scratch_shapes=[
                pltpu.VMEM((8, BLOCK), f32),
                pltpu.VMEM((8, BLOCK), f32),
                pltpu.VMEM((half, BLOCK), f32),
            ],
        ),
        out_shape=[
            jax.ShapeDtypeStruct((halves, micro, local, half), bf16),
            jax.ShapeDtypeStruct((micro, half, length), f32),
            jax.ShapeDtypeStruct((micro, 8, length), f32),
        ],
        compiler_params=pltpu.CompilerParams(vmem_limit_bytes=VMEM_LIMIT),
        cost_estimate=cost(
            micro * heads * length * length * 512, micro * length * width * 8, micro * heads * length * length
        ),
        name="attend",
    )(low, high, qp, km, vt, gk, gq)


def attend_back_kernel(
    low_ref,
    high_ref,
    qp_ref,
    km_ref,
    kmt_ref,
    v_ref,
    dc_ref,
    ct_ref,
    lse_ref,
    gk_ref,
    gq_ref,
    kind_ref,
    d_ref,
    db_ref,
    dqt_sc,
    dk_sc,
    dv_sc,
    delta_sc,
):
    micro_at = pl.program_id(0)
    local, width = qp_ref.shape[1], qp_ref.shape[2]
    half = width // 2
    per = local // BLOCK
    blocks = 2 * per
    tiles = half // 128
    base = micro_at * blocks
    dk_sc[...] = jnp.zeros_like(dk_sc)
    dv_sc[...] = jnp.zeros_like(dv_sc)

    @pl.when(micro_at == 0)
    def _():
        db_ref[...] = jnp.zeros_like(db_ref)

    lo = low_lanes((BLOCK, 128))

    @pl.loop(0, blocks)
    def _(qb):
        qh, qo = place(qb, per)
        qrows = pl.ds(qo, BLOCK)
        cols = pl.ds(pl.multiple_of(qb * BLOCK, BLOCK), BLOCK)
        dct = dc_ref[qh, qrows, :].astype(f32).T
        inner = dct * ct_ref[:, cols]
        for h in range(2 * tiles):
            delta_sc[h : h + 1, :] = jnp.sum(inner[64 * h : 64 * h + 64, :], axis=0, keepdims=True)
        dqt_sc[...] = jnp.zeros_like(dqt_sc)
        q_low, q_high = low_ref[base + qb], high_ref[base + qb]

        @pl.loop(0, blocks)
        def _(kb):
            @pl.when((q_low <= high_ref[base + kb]) & (low_ref[base + kb] <= q_high))
            def _():
                kh, ko = place(kb, per)
                krows = pl.ds(ko, BLOCK)
                drows = pl.ds(pl.multiple_of(kb * BLOCK, BLOCK), BLOCK)
                same = gk_ref[kh, krows, :] == gq_ref[qh, :, qrows]
                bias = jnp.where(same, 0.0, masked_score)
                for t in range(tiles):
                    tat = slice(128 * t, 128 * t + 128)
                    v = v_ref[kh, krows, tat]
                    dc = dc_ref[qh, qrows, tat]
                    from_pair = []
                    for side in range(2):
                        h = 2 * t + side
                        at = slice(128 * h, 128 * h + 128)
                        q = qp_ref[qh, qrows, at]
                        s = nt(km_ref[kh, krows, at], q) + bias
                        p = jnp.exp(s - lse_ref[h : h + 1, cols])
                        zero = jnp.zeros_like(v)
                        vm = jnp.where(lo, v, zero) if side == 0 else jnp.where(lo, zero, v)
                        dp = nt(vm, dc)
                        ds = (p * (dp - delta_sc[h : h + 1, :])).astype(bf16)
                        dk_sc[drows, at] += nn(ds, q)
                        dqt_sc[at, :] += nn(kmt_ref[kh, at, krows], ds)
                        from_pair.append(nn(p.astype(bf16), dc))
                    dv_sc[drows, tat] += jnp.where(lo, from_pair[0], from_pair[1])

        dq = dqt_sc[...].T * 0.125
        entity = kind_ref[qh, qrows, :] == 1
        d_ref[qh, qrows, 0:width] = jnp.where(entity, 0.0, dq).astype(bf16)
        d_ref[qh, qrows, width : 2 * width] = jnp.where(entity, dq, 0.0).astype(bf16)

    @pl.loop(0, blocks)
    def _(kb):
        kh, ko = place(kb, per)
        krows = pl.ds(ko, BLOCK)
        drows = pl.ds(pl.multiple_of(kb * BLOCK, BLOCK), BLOCK)
        entity = kind_ref[kh, krows, :] == 1
        for t in range(tiles):
            even = dk_sc[drows, 256 * t : 256 * t + 128]
            odd = dk_sc[drows, 256 * t + 128 : 256 * t + 256]
            left = jnp.where(entity, pltpu.roll(even, 64, 1), even)
            right = jnp.where(entity, odd, pltpu.roll(odd, 64, 1))
            d_ref[kh, krows, 2 * width + 128 * t : 2 * width + 128 * t + 128] = jnp.where(
                lo, left, right
            ).astype(bf16)
        d_ref[kh, krows, 2 * width + half : 3 * width] = dv_sc[drows, :].astype(bf16)
        db_ref[0:1, :] += jnp.sum(d_ref[kh, krows, :].astype(f32), axis=0, keepdims=True)


def attend_back(low, high, qp, km, kmt, v, dc, ct, lse, gk, gq, kind_col):
    halves, micro, local, width = qp.shape
    half = width // 2
    heads = width // 128
    length = halves * local
    return pl.pallas_call(
        attend_back_kernel,
        grid_spec=pltpu.PrefetchScalarGridSpec(
            num_scalar_prefetch=2,
            grid=(micro,),
            in_specs=[whole_micro(a) for a in (qp, km, kmt, v, dc)]
            + [
                pl.BlockSpec((None, half, length), lambda m, *_: (m, 0, 0)),
                pl.BlockSpec((None, 8, length), lambda m, *_: (m, 0, 0)),
            ]
            + [whole_micro(a) for a in (gk, gq, kind_col)],
            out_specs=[
                pl.BlockSpec((halves, None, local, 3 * width), lambda m, *_: (0, m, 0, 0)),
                pl.BlockSpec((8, 3 * width), lambda m, *_: (0, 0)),
            ],
            scratch_shapes=[
                pltpu.VMEM((width, BLOCK), f32),
                pltpu.VMEM((length, width), f32),
                pltpu.VMEM((length, half), f32),
                pltpu.VMEM((8, BLOCK), f32),
            ],
        ),
        out_shape=[
            jax.ShapeDtypeStruct((halves, micro, local, 3 * width), bf16),
            jax.ShapeDtypeStruct((8, 3 * width), f32),
        ],
        compiler_params=pltpu.CompilerParams(vmem_limit_bytes=VMEM_LIMIT),
        cost_estimate=cost(
            micro * heads * length * length * 1280, micro * length * width * 16, micro * heads * length * length
        ),
        name="attend_back",
    )(low, high, qp, km, kmt, v, dc, ct, lse, gk, gq, kind_col)


def norm_forward(hidden):
    center = hidden - jnp.mean(hidden, axis=-1, keepdims=True)
    rescale = lax.rsqrt(jnp.mean(center * center, axis=-1, keepdims=True) + layer_eps)
    return center * rescale, rescale


def norm_backward(upstream, normed, rescale, gain):
    scaled = upstream * gain
    return rescale * (
        scaled
        - jnp.mean(scaled, axis=-1, keepdims=True)
        - normed * jnp.mean(scaled * normed, axis=-1, keepdims=True)
    )


def column_sum(values):
    return jnp.sum(values.astype(f32), axis=0, keepdims=True)


def chain_kernel(
    side_ref,
    x_ref,
    own_ref,
    other_ref,
    cot_ref,
    w_ref,
    vec_ref,
    mixed_ref,
    dh_ref,
    left_ref,
    right_ref,
    dco_ref,
    dcx_ref,
    sums_ref,
    slope_sc,
    z_sc,
):
    width = x_ref.shape[1]
    half = width // 2
    rows = width // GROUPS
    chunks = 4
    first = side_ref[0] == 0

    @pl.when(pl.program_id(0) == 0)
    def _():
        sums_ref[...] = jnp.zeros_like(sums_ref)

    def vector(at):
        return vec_ref[at : at + 1, :]

    def up_chunk(j):
        at = pl.multiple_of(5 * rows + j * rows, 16)
        return w_ref[:, pl.ds(at, rows), :].reshape(width, width)

    def down_chunk(j):
        return w_ref[pl.ds(j * (GROUPS // chunks), GROUPS // chunks), 0 : 4 * rows, :].reshape(width, width)

    def out_weight():
        return w_ref[:, 4 * rows : 5 * rows, :].reshape(width, width)

    own = own_ref[...].astype(f32)
    other = other_ref[...].astype(f32)
    context = jnp.concatenate(
        [jnp.where(first, own, other), jnp.where(first, other, own)], axis=1
    ).astype(bf16)
    left_ref[:, 0:width] = context
    hidden = x_ref[...].astype(f32) + (nn(context, out_weight()) + vector(0))
    n1, r1 = norm_forward(hidden)
    y1 = n1 * vector(1) + vector(2)
    left_ref[:, width : 2 * width] = y1.astype(bf16)
    z_sc[...] = y1 + vector(7)

    @pl.loop(0, chunks)
    def _(j):
        u = nn(left_ref[:, width : 2 * width], up_chunk(j)) + vec_ref[pl.ds(j + 3, 1), :]
        cumulative = 0.5 * (1.0 + lax.erf(u * 0.7071067811865476))
        at = pl.multiple_of(j * width, 128)
        slope_sc[:, pl.ds(at, width)] = (
            cumulative + u * jnp.exp(-0.5 * u * u) * 0.3989422804014327
        )
        g = (u * cumulative).astype(bf16)
        left_ref[:, pl.ds(pl.multiple_of(at + 2 * width, 128), width)] = g
        z_sc[...] += nn(g, down_chunk(j))

    n2, r2 = norm_forward(z_sc[...])
    mixed_ref[...] = (n2 * vector(8) + vector(9)).astype(bf16)
    upstream = cot_ref[...].astype(f32)
    sums_ref[0:1, :] += column_sum(upstream * n2)
    sums_ref[1:2, :] += column_sum(upstream)
    dh2 = norm_backward(upstream, n2, r2, vector(8))
    dz = dh2.astype(bf16)
    right_ref[:, 5 * width :] = dz
    sums_ref[2:3, :] += column_sum(dz)
    z_sc[...] = dh2

    @pl.loop(0, chunks)
    def _(j):
        at = pl.multiple_of(j * width, 128)
        du = (
            nt(right_ref[:, 5 * width :], down_chunk(j)) * slope_sc[:, pl.ds(at, width)]
        ).astype(bf16)
        right_ref[:, pl.ds(pl.multiple_of(at + width, 128), width)] = du
        sums_ref[pl.ds(j + 8, 1), :] += column_sum(du)
        z_sc[...] += nt(du, up_chunk(j))

    dy1 = z_sc[...]
    hidden = x_ref[...].astype(f32) + (nn(left_ref[:, 0:width], out_weight()) + vector(0))
    n1, r1 = norm_forward(hidden)
    sums_ref[3:4, :] += column_sum(dy1 * n1)
    sums_ref[4:5, :] += column_sum(dy1)
    dh1 = norm_backward(dy1, n1, r1, vector(1))
    dh_ref[...] = dh1
    da = dh1.astype(bf16)
    right_ref[:, 0:width] = da
    sums_ref[5:6, :] += column_sum(da)
    dc = nt(da, out_weight())
    dco_ref[...] = jnp.where(first, dc[:, :half], dc[:, half:]).astype(bf16)
    dcx_ref[...] = jnp.where(first, dc[:, half:], dc[:, :half]).astype(bf16)


def chain(side, x, c_own, c_other, cot, weights, vectors):
    tokens, width = x.shape
    half = width // 2

    def rows_spec(cols):
        return pl.BlockSpec((BLOCK, cols), lambda i, *_: (i, 0))

    def shape(cols, kind):
        return jax.ShapeDtypeStruct((tokens, cols), kind)

    return pl.pallas_call(
        chain_kernel,
        grid_spec=pltpu.PrefetchScalarGridSpec(
            num_scalar_prefetch=1,
            grid=(tokens // BLOCK,),
            in_specs=[
                rows_spec(width),
                rows_spec(half),
                rows_spec(half),
                rows_spec(width),
                pl.BlockSpec(weights.shape, lambda i, *_: (0, 0, 0), pipeline_mode=pl.Buffered(1)),
                pl.BlockSpec(vectors.shape, lambda i, *_: (0, 0)),
            ],
            out_specs=[
                rows_spec(width),
                rows_spec(width),
                rows_spec(6 * width),
                rows_spec(6 * width),
                rows_spec(half),
                rows_spec(half),
                pl.BlockSpec((16, width), lambda i, *_: (0, 0)),
            ],
            scratch_shapes=[pltpu.VMEM((BLOCK, 4 * width), f32), pltpu.VMEM((BLOCK, width), f32)],
        ),
        out_shape=[
            shape(width, bf16),
            shape(width, f32),
            shape(6 * width, bf16),
            shape(6 * width, bf16),
            shape(half, bf16),
            shape(half, bf16),
            jax.ShapeDtypeStruct((16, width), f32),
        ],
        compiler_params=pltpu.CompilerParams(vmem_limit_bytes=VMEM_LIMIT),
        cost_estimate=cost(2 * tokens * width * width * 19, tokens * width * 36 + weights.size * 2),
        name="chain",
    )(side[None], x, c_own, c_other, cot, weights, vectors)


def feed_grad_kernel(l_ref, r_ref, out_ref):
    width = l_ref.shape[1]
    rows = width // GROUPS
    at = pl.program_id(0)
    grad = tn(l_ref[...], r_ref[...]).astype(bf16)

    @pl.when(at == 0)
    def _():
        out_ref[:, 4 * rows : 5 * rows, :] = grad.reshape(GROUPS, rows, width)

    @pl.when((at >= 1) & (at < 5))
    def _():
        start = pl.multiple_of(5 * rows + (at - 1) * rows, 16)
        out_ref[:, pl.ds(start, rows), :] = grad.reshape(GROUPS, rows, width)

    @pl.when(at >= 5)
    def _():
        out_ref[pl.ds((at - 5) * 4, 4), 0 : 4 * rows, :] = grad.reshape(4, 4 * rows, width)


def feed_grad(left, right):
    tokens = left.shape[0]
    width = left.shape[1] // 6
    rows = width // GROUPS

    def left_at(i):
        return (0, jnp.where(i == 0, 0, jnp.where(i < 5, 1, i - 3)))

    def right_at(i):
        return (0, jnp.minimum(i, 5))

    return pl.pallas_call(
        feed_grad_kernel,
        grid=(9,),
        in_specs=[
            pl.BlockSpec((tokens, width), left_at),
            pl.BlockSpec((tokens, width), right_at),
        ],
        out_specs=pl.BlockSpec((GROUPS, 9 * rows, width), lambda i: (0, 0, 0)),
        out_shape=jax.ShapeDtypeStruct((GROUPS, 9 * rows, width), bf16),
        compiler_params=pltpu.CompilerParams(vmem_limit_bytes=VMEM_LIMIT),
        cost_estimate=cost(2 * tokens * width * width * 9, tokens * width * 24 + width * width * 18),
        name="feed_grad",
    )(left, right)


def attn_grad_kernel(x_ref, d_ref, vec_ref, out_ref):
    width = x_ref.shape[1]
    rows = width // GROUPS
    at = pl.program_id(0)
    grad = tn(x_ref[...], d_ref[...]).astype(bf16)
    start = pl.multiple_of(at * rows, 16)
    out_ref[:, pl.ds(start, rows), :] = grad.reshape(GROUPS, rows, width)
    out_ref[:, 3 * rows :, :] = vec_ref[...]


def attn_grad(x, d, vectors):
    tokens, width = x.shape
    rows = width // GROUPS
    return pl.pallas_call(
        attn_grad_kernel,
        grid=(3,),
        in_specs=[
            pl.BlockSpec((tokens, width), lambda i: (0, 0)),
            pl.BlockSpec((tokens, width), lambda i: (0, i)),
            pl.BlockSpec((GROUPS, 16, width), lambda i: (0, 0, 0)),
        ],
        out_specs=pl.BlockSpec((GROUPS, 3 * rows + 16, width), lambda i: (0, 0, 0)),
        out_shape=jax.ShapeDtypeStruct((GROUPS, 3 * rows + 16, width), bf16),
        compiler_params=pltpu.CompilerParams(vmem_limit_bytes=VMEM_LIMIT),
        cost_estimate=cost(2 * tokens * width * width * 3, tokens * width * 8 + width * width * 6),
        name="attn_grad",
    )(x, d, vectors)


def input_grad_kernel(d_ref, w_ref, out_ref):
    width = out_ref.shape[1]
    rows = width // GROUPS
    total = None
    for i in range(3):
        part = nt(
            d_ref[:, i * width : i * width + width],
            w_ref[:, i * rows : i * rows + rows, :].reshape(width, width),
        )
        total = part if total is None else total + part
    out_ref[...] = total.astype(out_ref.dtype)


def input_grad_part(d, weights, side_at, kind):
    _, micro, local, wide = d.shape
    width = wide // 3
    sub = local // BLOCK
    return pl.pallas_call(
        input_grad_kernel,
        grid=(micro, sub),
        in_specs=[
            pl.BlockSpec((None, None, BLOCK, wide), lambda m, i: (side_at, m, i, 0)),
            pl.BlockSpec(weights.shape, lambda m, i: (0, 0, 0)),
        ],
        out_specs=pl.BlockSpec((None, BLOCK, width), lambda m, i: (m, i, 0)),
        out_shape=jax.ShapeDtypeStruct((micro, local, width), kind),
        compiler_params=pltpu.CompilerParams(vmem_limit_bytes=VMEM_LIMIT),
        cost_estimate=cost(2 * micro * local * wide * width, micro * local * wide * 2 + weights.size * 2),
        name="input_grad",
    )(d, weights)


def on_device(
    tokens,
    kinds,
    groups,
    query_weight,
    query_bias,
    key_weight,
    key_bias,
    value_weight,
    value_bias,
    output_weight,
    output_bias,
    norm1_gain,
    norm1_shift,
    up_weight,
    up_bias,
    down_weight,
    down_bias,
    norm2_gain,
    norm2_shift,
    cotangent,
):
    micro, _, local, width = tokens.shape
    half = width // 2
    head_dim = width // HEADS
    devices = lax.axis_size("shard")
    rows = width // devices
    side = lax.axis_index("seq").astype(jnp.int32)
    per = local // BLOCK

    vector = jnp.concatenate(
        [
            query_bias,
            key_bias,
            value_bias,
            output_bias,
            norm1_gain,
            norm1_shift,
            up_bias,
            down_bias,
            norm2_gain,
            norm2_shift,
        ]
    )
    piece = vector.shape[0]
    vector_row = jnp.pad(vector, (0, width - piece))[None]
    attn_sizes = (rows, rows, rows)
    feed_sizes = (4 * rows,) + (rows,) * 5
    packed = pack_attention(query_weight, key_weight, value_weight, vector_row, side, head_dim)
    attn_gathered = lax.all_gather(packed[None], "shard", axis=0, tiled=True)
    feed_local = jnp.concatenate(
        [down_weight, output_weight] + [up_weight[:, j * width : j * width + width] for j in range(4)],
        axis=0,
    )
    feed_gathered = lax.all_gather(feed_local[None], "shard", axis=0, tiled=True)
    vectors = attn_gathered[:, 3 * rows, :piece]
    if devices == GROUPS:
        attn_w, feed_w = attn_gathered, feed_gathered
    else:
        attn_w = regroup(attn_gathered, attn_sizes)
        feed_w = regroup(feed_gathered, feed_sizes)

    def whole_vector(start, size):
        return vectors[:, start : start + size].reshape(-1).astype(f32)

    full_query_bias = whole_vector(0, 4 * rows)
    full_key_bias = whole_vector(4 * rows, rows)
    full_value_bias = whole_vector(5 * rows, rows)
    bias_rows = jnp.concatenate(
        [
            pair_columns(full_query_bias, side, head_dim),
            jnp.concatenate([own_half(full_key_bias, side), own_half(full_value_bias, side)])[None],
        ],
        axis=0,
    )
    full_up_bias = whole_vector(9 * rows, 4 * rows).reshape(4, width)
    chain_vectors = jnp.concatenate(
        [
            whole_vector(6 * rows, rows)[None],
            whole_vector(7 * rows, rows)[None],
            whole_vector(8 * rows, rows)[None],
            full_up_bias,
            whole_vector(13 * rows, rows)[None],
            whole_vector(14 * rows, rows)[None],
            whole_vector(15 * rows, rows)[None],
        ],
        axis=0,
    )

    own_tokens = tokens[:, 0]
    marks = jnp.stack([kinds[:, 0], groups[:, 0]])
    xs = jnp.stack([own_tokens, swap(own_tokens)])
    both_marks = jnp.stack([marks, swap(marks)])
    kind_all, group_all = both_marks[:, 0], both_marks[:, 1]
    kind_col = kind_all[..., None]
    gk = group_all[..., None]
    gq = group_all[:, :, None, :]
    by_block = group_all.reshape(2, micro, per, BLOCK)
    low = jnp.swapaxes(by_block[..., 0], 0, 1).reshape(-1)
    high = jnp.swapaxes(by_block[..., BLOCK - 1], 0, 1).reshape(-1)

    qp, km, kmt, v, vt = project(xs, attn_w, bias_rows, kind_col)
    c, ct, lse = attend(low, high, qp, km, vt, gk, gq)
    c_other = swap(c[1])
    flat = micro * local
    mixed, dh1, left, right, dc_own, dc_other, sums = chain(
        side,
        own_tokens.reshape(flat, width),
        c[0].reshape(flat, half),
        c_other.reshape(flat, half),
        cotangent.reshape(flat, width),
        feed_w,
        chain_vectors,
    )

    dc = jnp.stack([dc_own, swap(dc_other)]).reshape(2, micro, local, half)
    feed_part = feed_grad(left, right)
    if devices != GROUPS:
        feed_part = ungroup(feed_part, feed_sizes, devices)
    feed_sum = lax.psum_scatter(feed_part, "shard", scatter_dimension=0, tiled=True)[0]
    d, db = attend_back(low, high, qp, km, kmt, v, dc, ct, lse, gk, gq, kind_col)

    query_own = unpair_columns(db[0, : 2 * width].reshape(2, width), head_dim)
    zero = jnp.zeros((half,), f32)

    def spread(own):
        return jnp.where(side == 0, jnp.concatenate([own, zero]), jnp.concatenate([zero, own]))

    query_spread = jnp.concatenate([spread(query_own[e, w]) for e in range(2) for w in range(2)])
    key_spread = spread(db[0, 2 * width : 2 * width + half])
    value_spread = spread(db[0, 2 * width + half :])
    grad_vectors = jnp.concatenate(
        [
            query_spread.reshape(devices, 4 * rows),
            key_spread.reshape(devices, rows),
            value_spread.reshape(devices, rows),
            sums[5].reshape(devices, rows),
            sums[3].reshape(devices, rows),
            sums[4].reshape(devices, rows),
            sums[8:12].reshape(devices, 4 * rows),
            sums[2].reshape(devices, rows),
            sums[0].reshape(devices, rows),
            sums[1].reshape(devices, rows),
        ],
        axis=1,
    ).astype(bf16)
    grad_vectors = jnp.pad(grad_vectors[:, None, :], ((0, 0), (0, 15), (0, width - piece)))
    if devices == GROUPS:
        attn_part = attn_grad(xs.reshape(2 * flat, width), d.reshape(2 * flat, 3 * width), grad_vectors)
    else:
        zeros = jnp.zeros((GROUPS, 16, width), bf16)
        attn_part = attn_grad(xs.reshape(2 * flat, width), d.reshape(2 * flat, 3 * width), zeros)
        attn_part = jnp.concatenate(
            [ungroup(attn_part[:, : 3 * (width // GROUPS)], attn_sizes, devices), grad_vectors], axis=1
        )
    attn_sum = lax.psum_scatter(attn_part, "shard", scatter_dimension=0, tiled=True)[0]

    dx_other = input_grad_part(d, attn_w, 1, bf16)
    dx_own = input_grad_part(d, attn_w, 0, f32)
    input_grad = dh1.reshape(micro, local, width) + dx_own + swap(dx_other).astype(f32)

    feed_total = feed_sum.astype(f32) + swap(feed_sum).astype(f32)
    grad_down = feed_total[: 4 * rows]
    grad_output = feed_total[4 * rows : 5 * rows]
    grad_up = jnp.concatenate(
        [feed_total[(5 + j) * rows : (6 + j) * rows] for j in range(4)], axis=1
    )
    attn_own = attn_sum.astype(f32)
    attn_other = swap(attn_sum).astype(f32)
    vec_total = attn_own[3 * rows, :piece] + attn_other[3 * rows, :piece]

    def by_side(own, other, axis):
        return jnp.where(
            side == 0,
            jnp.concatenate([own, other], axis=axis),
            jnp.concatenate([other, own], axis=axis),
        )

    def query_parts(block):
        pairs = jnp.stack([block[:rows], block[rows : 2 * rows]], axis=1)
        return unpair_columns(pairs, head_dim)

    grad_query = by_side(query_parts(attn_own), query_parts(attn_other), 3).reshape(rows, 4 * width)
    kv_own, kv_other = attn_own[2 * rows : 3 * rows], attn_other[2 * rows : 3 * rows]
    grad_key = by_side(kv_own[:, :half], kv_other[:, :half], 1)
    grad_value = by_side(kv_own[:, half:], kv_other[:, half:], 1)

    def piece_of(start, size):
        return vec_total[start : start + size]

    return (
        mixed.reshape(micro, 1, local, width),
        input_grad[:, None],
        grad_query,
        piece_of(0, 4 * rows),
        grad_key,
        piece_of(4 * rows, rows),
        grad_value,
        piece_of(5 * rows, rows),
        grad_output,
        piece_of(6 * rows, rows),
        piece_of(7 * rows, rows),
        piece_of(8 * rows, rows),
        grad_up,
        piece_of(9 * rows, 4 * rows),
        grad_down,
        piece_of(13 * rows, rows),
        piece_of(14 * rows, rows),
        piece_of(15 * rows, rows),
    )


def solution(mesh):
    weight = P("shard", None)
    vector = P("shard")
    tokens = P(None, "shard", "seq", None)
    marks = P(None, "shard", "seq")
    return jax.shard_map(
        on_device,
        mesh=mesh,
        in_specs=(tokens, marks, marks)
        + (weight, vector) * 4
        + (vector, vector)
        + (weight, vector) * 2
        + (vector, vector)
        + (tokens,),
        out_specs=(tokens, tokens)
        + (weight, vector) * 4
        + (vector, vector)
        + (weight, vector) * 2
        + (vector, vector),
        check_vma=False,
    )
```

```python
import jax
import jax.numpy as jnp
from jax import lax
from jax.experimental import pallas as pl
from jax.experimental.pallas import tpu as pltpu
from jax.sharding import PartitionSpec as P


HEADS = 12
GROUPS = 16
BLOCK = 256
masked_score = -1e30
layer_eps = 1e-12
bf16 = jnp.bfloat16
f32 = jnp.float32
VMEM_LIMIT = 60 * 1024 * 1024


def nn(a, b):
    return lax.dot_general(a, b, (((1,), (0,)), ((), ())), preferred_element_type=f32)


def nt(a, b):
    return lax.dot_general(a, b, (((1,), (1,)), ((), ())), preferred_element_type=f32)


def tn(a, b):
    return lax.dot_general(a, b, (((0,), (0,)), ((), ())), preferred_element_type=f32)


def swap(value):
    return lax.ppermute(value, "seq", [(0, 1), (1, 0)])


def cost(flops, moved, trans=0):
    return pl.CostEstimate(flops=flops, bytes_accessed=moved, transcendentals=trans)


def low_lanes(shape):
    return lax.broadcasted_iota(jnp.int32, shape, len(shape) - 1) % 128 < 64


def pack_kernel(side_ref, q_ref, k_ref, v_ref, vec_ref, out_ref):
    rows, width = k_ref.shape
    half = width // 2
    first = side_ref[0] == 0

    def own(ref, base):
        return jnp.where(
            first,
            ref[:, base : base + half].astype(f32),
            ref[:, base + half : base + width].astype(f32),
        )

    lo = low_lanes((rows, 128))
    for e in range(2):
        word = own(q_ref, 2 * e * width)
        entity = own(q_ref, (2 * e + 1) * width)
        for t in range(half // 128):
            a = word[:, 128 * t : 128 * t + 128]
            b = entity[:, 128 * t : 128 * t + 128]
            even = jnp.where(lo, a, pltpu.roll(b, 64, 1))
            odd = jnp.where(lo, pltpu.roll(a, 64, 1), b)
            out_ref[e * rows : e * rows + rows, 256 * t : 256 * t + 128] = even.astype(bf16)
            out_ref[e * rows : e * rows + rows, 256 * t + 128 : 256 * t + 256] = odd.astype(bf16)
    out_ref[2 * rows : 3 * rows, :half] = own(k_ref, 0).astype(bf16)
    out_ref[2 * rows : 3 * rows, half:] = own(v_ref, 0).astype(bf16)
    out_ref[3 * rows :, :] = jnp.broadcast_to(vec_ref[...], (16, width))


def pair_columns(columns, side, head_dim):
    lead = columns.shape[:-1]
    per = columns.shape[-1] // (8 * head_dim)
    view = columns.reshape(lead + (2, 2, 2, per, head_dim))
    view = jnp.where(side == 0, view[..., 0, :, :], view[..., 1, :, :])
    return jnp.swapaxes(view, -3, -2).reshape(lead + (2, -1))


def unpair_columns(pairs, head_dim):
    lead = pairs.shape[:-2]
    per = pairs.shape[-1] // (2 * head_dim)
    view = pairs.reshape(lead + (2, per, 2, head_dim))
    return jnp.swapaxes(view, -3, -2).reshape(lead + (2, 2, per * head_dim))


def own_half(columns, side):
    half = columns.shape[-1] // 2
    return jnp.where(side == 0, columns[..., :half], columns[..., half:])


def pack_attention(query_weight, key_weight, value_weight, vector, side, head_dim):
    rows, width = key_weight.shape
    if rows % 16 == 0:
        return pl.pallas_call(
            pack_kernel,
            out_shape=jax.ShapeDtypeStruct((3 * rows + 16, width), bf16),
            in_specs=[pl.BlockSpec(memory_space=pltpu.SMEM)]
            + [pl.BlockSpec(memory_space=pltpu.VMEM)] * 4,
            out_specs=pl.BlockSpec(memory_space=pltpu.VMEM),
            name="pack",
        )(side[None], query_weight, key_weight, value_weight, vector)
    pairs = pair_columns(query_weight, side, head_dim)
    key_value = jnp.concatenate([own_half(key_weight, side), own_half(value_weight, side)], axis=1)
    return jnp.concatenate(
        [pairs[:, 0], pairs[:, 1], key_value, jnp.broadcast_to(vector, (16, width))], axis=0
    )


def regroup(gathered, sizes):
    _, _, width = gathered.shape
    pieces = []
    start = 0
    for size in sizes:
        piece = gathered[:, start : start + size].reshape(GROUPS, -1, width)
        pieces.append(piece)
        start += size
    return jnp.concatenate(pieces, axis=1)


def ungroup(grouped, sizes, devices):
    _, _, width = grouped.shape
    pieces = []
    start = 0
    for size in sizes:
        wide = size * devices // GROUPS
        pieces.append(grouped[:, start : start + wide].reshape(devices, size, width))
        start += wide
    return jnp.concatenate(pieces, axis=1)


def project_kernel(x_ref, w_ref, bias_ref, kind_ref, qp_ref, km_ref, kmt_ref, v_ref, vt_ref):
    width = x_ref.shape[1]
    half = width // 2
    rows = width // GROUPS
    x = x_ref[...]
    kind = kind_ref[...]
    wa = w_ref[:, 0:rows, :].reshape(width, width)
    wb = w_ref[:, rows : 2 * rows, :].reshape(width, width)
    wkv = w_ref[:, 2 * rows : 3 * rows, :].reshape(width, width)
    qa = nn(x, wa) + bias_ref[0:1, :]
    qb = nn(x, wb) + bias_ref[1:2, :]
    qp_ref[...] = (jnp.where(kind == 1, qb, qa) * 0.125).astype(bf16)
    kv = nn(x, wkv) + bias_ref[2:3, :]
    lane_high = (lax.broadcasted_iota(jnp.int32, (BLOCK, 128), 1) >= 64).astype(jnp.int32)
    keep = lane_high == kind
    lo = lane_high == 0
    for t in range(half // 128):
        k = kv[:, 128 * t : 128 * t + 128]
        r = pltpu.roll(k, 64, 1)
        even = jnp.where(keep, jnp.where(lo, k, r), 0.0)
        odd = jnp.where(keep, jnp.where(lo, r, k), 0.0)
        km_ref[:, 256 * t : 256 * t + 128] = even.astype(bf16)
        km_ref[:, 256 * t + 128 : 256 * t + 256] = odd.astype(bf16)
        kmt_ref[256 * t : 256 * t + 128, :] = even.T.astype(bf16)
        kmt_ref[256 * t + 128 : 256 * t + 256, :] = odd.T.astype(bf16)
    v = kv[:, half:]
    v_ref[...] = v.astype(bf16)
    vt_ref[...] = v.T.astype(bf16)


def project(xs, weights, bias_rows, kind_col):
    halves, micro, local, width = xs.shape
    half = width // 2
    sub = local // BLOCK

    def rows_spec(cols):
        return pl.BlockSpec((None, None, BLOCK, cols), lambda a, m, i: (a, m, i, 0))

    def cols_spec(count):
        return pl.BlockSpec((None, None, count, BLOCK), lambda a, m, i: (a, m, 0, i))

    def shape(*dims):
        return jax.ShapeDtypeStruct((halves, micro) + dims, bf16)

    tokens = halves * micro * local
    return pl.pallas_call(
        project_kernel,
        grid=(halves, micro, sub),
        in_specs=[
            rows_spec(width),
            pl.BlockSpec(weights.shape, lambda a, m, i: (0, 0, 0)),
            pl.BlockSpec(bias_rows.shape, lambda a, m, i: (0, 0)),
            rows_spec(1),
        ],
        out_specs=[rows_spec(width), rows_spec(width), cols_spec(width), rows_spec(half), cols_spec(half)],
        out_shape=[
            shape(local, width),
            shape(local, width),
            shape(width, local),
            shape(local, half),
            shape(half, local),
        ],
        compiler_params=pltpu.CompilerParams(vmem_limit_bytes=VMEM_LIMIT),
        cost_estimate=cost(2 * tokens * width * 3 * width, tokens * width * 10),
        name="project",
    )(xs, weights, bias_rows, kind_col)


def place(block, per):
    return block // per, pl.multiple_of(lax.rem(block, per) * BLOCK, BLOCK)


def attend_kernel(
    low_ref, high_ref, qp_ref, km_ref, vt_ref, gk_ref, gq_ref, c_ref, ct_ref, lse_ref, m_sc, l_sc, acc_sc
):
    micro_at = pl.program_id(0)
    local = qp_ref.shape[1]
    per = local // BLOCK
    blocks = 2 * per
    heads = qp_ref.shape[2] // 128
    base = micro_at * blocks

    @pl.loop(0, blocks)
    def _(qb):
        qh, qo = place(qb, per)
        m_sc[...] = jnp.full_like(m_sc, masked_score)
        l_sc[...] = jnp.zeros_like(l_sc)
        acc_sc[...] = jnp.zeros_like(acc_sc)
        q_low, q_high = low_ref[base + qb], high_ref[base + qb]

        @pl.loop(0, blocks)
        def _(kb):
            @pl.when((q_low <= high_ref[base + kb]) & (low_ref[base + kb] <= q_high))
            def _():
                kh, ko = place(kb, per)
                same = gk_ref[kh, pl.ds(ko, BLOCK), :] == gq_ref[qh, :, pl.ds(qo, BLOCK)]
                bias = jnp.where(same, 0.0, masked_score)
                for h in range(heads):
                    at = slice(128 * h, 128 * h + 128)
                    vat = slice(64 * h, 64 * h + 64)
                    s = nt(km_ref[kh, pl.ds(ko, BLOCK), at], qp_ref[qh, pl.ds(qo, BLOCK), at]) + bias
                    m_old = m_sc[h : h + 1, :]
                    m_new = jnp.maximum(m_old, jnp.max(s, axis=0, keepdims=True))
                    alpha = jnp.exp(m_old - m_new)
                    p = jnp.exp(s - m_new)
                    m_sc[h : h + 1, :] = m_new
                    l_sc[h : h + 1, :] = alpha * l_sc[h : h + 1, :] + jnp.sum(p, axis=0, keepdims=True)
                    acc_sc[vat, :] = alpha * acc_sc[vat, :] + nn(
                        vt_ref[kh, vat, pl.ds(ko, BLOCK)], p.astype(bf16)
                    )

        cols = pl.ds(pl.multiple_of(qb * BLOCK, BLOCK), BLOCK)
        for h in range(heads):
            vat = slice(64 * h, 64 * h + 64)
            total = l_sc[h : h + 1, :]
            ct_ref[vat, cols] = acc_sc[vat, :] / total
            lse_ref[h : h + 1, cols] = m_sc[h : h + 1, :] + jnp.log(total)
        c_ref[qh, pl.ds(qo, BLOCK), :] = ct_ref[:, cols].T.astype(bf16)


def whole_micro(array):
    rest = array.shape[2:]
    return pl.BlockSpec((array.shape[0], None) + rest, lambda m, *_: (0, m) + (0,) * len(rest))


def attend(low, high, qp, km, vt, gk, gq):
    halves, micro, local, width = qp.shape
    half = width // 2
    heads = width // 128
    length = halves * local
    return pl.pallas_call(
        attend_kernel,
        grid_spec=pltpu.PrefetchScalarGridSpec(
            num_scalar_prefetch=2,
            grid=(micro,),
            in_specs=[whole_micro(a) for a in (qp, km, vt, gk, gq)],
            out_specs=[
                pl.BlockSpec((halves, None, local, half), lambda m, *_: (0, m, 0, 0)),
                pl.BlockSpec((None, half, length), lambda m, *_: (m, 0, 0)),
                pl.BlockSpec((None, 8, length), lambda m, *_: (m, 0, 0)),
            ],
            scratch_shapes=[
                pltpu.VMEM((8, BLOCK), f32),
                pltpu.VMEM((8, BLOCK), f32),
                pltpu.VMEM((half, BLOCK), f32),
            ],
        ),
        out_shape=[
            jax.ShapeDtypeStruct((halves, micro, local, half), bf16),
            jax.ShapeDtypeStruct((micro, half, length), f32),
            jax.ShapeDtypeStruct((micro, 8, length), f32),
        ],
        compiler_params=pltpu.CompilerParams(vmem_limit_bytes=VMEM_LIMIT),
        cost_estimate=cost(
            micro * heads * length * length * 512, micro * length * width * 8, micro * heads * length * length
        ),
        name="attend",
    )(low, high, qp, km, vt, gk, gq)


def attend_back_kernel(
    low_ref,
    high_ref,
    qp_ref,
    km_ref,
    kmt_ref,
    v_ref,
    dc_ref,
    ct_ref,
    lse_ref,
    gk_ref,
    gq_ref,
    kind_ref,
    d_ref,
    db_ref,
    dqt_sc,
    dk_sc,
    dv_sc,
    delta_sc,
):
    micro_at = pl.program_id(0)
    local, width = qp_ref.shape[1], qp_ref.shape[2]
    half = width // 2
    per = local // BLOCK
    blocks = 2 * per
    tiles = half // 128
    base = micro_at * blocks
    dk_sc[...] = jnp.zeros_like(dk_sc)
    dv_sc[...] = jnp.zeros_like(dv_sc)

    @pl.when(micro_at == 0)
    def _():
        db_ref[...] = jnp.zeros_like(db_ref)

    lo = low_lanes((BLOCK, 128))

    @pl.loop(0, blocks)
    def _(qb):
        qh, qo = place(qb, per)
        qrows = pl.ds(qo, BLOCK)
        cols = pl.ds(pl.multiple_of(qb * BLOCK, BLOCK), BLOCK)
        dct = dc_ref[qh, qrows, :].astype(f32).T
        inner = dct * ct_ref[:, cols]
        for h in range(2 * tiles):
            delta_sc[h : h + 1, :] = jnp.sum(inner[64 * h : 64 * h + 64, :], axis=0, keepdims=True)
        dqt_sc[...] = jnp.zeros_like(dqt_sc)
        q_low, q_high = low_ref[base + qb], high_ref[base + qb]

        @pl.loop(0, blocks)
        def _(kb):
            @pl.when((q_low <= high_ref[base + kb]) & (low_ref[base + kb] <= q_high))
            def _():
                kh, ko = place(kb, per)
                krows = pl.ds(ko, BLOCK)
                drows = pl.ds(pl.multiple_of(kb * BLOCK, BLOCK), BLOCK)
                same = gk_ref[kh, krows, :] == gq_ref[qh, :, qrows]
                bias = jnp.where(same, 0.0, masked_score)
                for t in range(tiles):
                    tat = slice(128 * t, 128 * t + 128)
                    v = v_ref[kh, krows, tat]
                    dc = dc_ref[qh, qrows, tat]
                    from_pair = []
                    for side in range(2):
                        h = 2 * t + side
                        at = slice(128 * h, 128 * h + 128)
                        q = qp_ref[qh, qrows, at]
                        s = nt(km_ref[kh, krows, at], q) + bias
                        p = jnp.exp(s - lse_ref[h : h + 1, cols])
                        zero = jnp.zeros_like(v)
                        vm = jnp.where(lo, v, zero) if side == 0 else jnp.where(lo, zero, v)
                        dp = nt(vm, dc)
                        ds = (p * (dp - delta_sc[h : h + 1, :])).astype(bf16)
                        dk_sc[drows, at] += nn(ds, q)
                        dqt_sc[at, :] += nn(kmt_ref[kh, at, krows], ds)
                        from_pair.append(nn(p.astype(bf16), dc))
                    dv_sc[drows, tat] += jnp.where(lo, from_pair[0], from_pair[1])

        dq = dqt_sc[...].T * 0.125
        entity = kind_ref[qh, qrows, :] == 1
        d_ref[qh, qrows, 0:width] = jnp.where(entity, 0.0, dq).astype(bf16)
        d_ref[qh, qrows, width : 2 * width] = jnp.where(entity, dq, 0.0).astype(bf16)

    @pl.loop(0, blocks)
    def _(kb):
        kh, ko = place(kb, per)
        krows = pl.ds(ko, BLOCK)
        drows = pl.ds(pl.multiple_of(kb * BLOCK, BLOCK), BLOCK)
        entity = kind_ref[kh, krows, :] == 1
        for t in range(tiles):
            even = dk_sc[drows, 256 * t : 256 * t + 128]
            odd = dk_sc[drows, 256 * t + 128 : 256 * t + 256]
            left = jnp.where(entity, pltpu.roll(even, 64, 1), even)
            right = jnp.where(entity, odd, pltpu.roll(odd, 64, 1))
            d_ref[kh, krows, 2 * width + 128 * t : 2 * width + 128 * t + 128] = jnp.where(
                lo, left, right
            ).astype(bf16)
        d_ref[kh, krows, 2 * width + half : 3 * width] = dv_sc[drows, :].astype(bf16)
        db_ref[0:1, :] += jnp.sum(d_ref[kh, krows, :].astype(f32), axis=0, keepdims=True)


def attend_back(low, high, qp, km, kmt, v, dc, ct, lse, gk, gq, kind_col):
    halves, micro, local, width = qp.shape
    half = width // 2
    heads = width // 128
    length = halves * local
    return pl.pallas_call(
        attend_back_kernel,
        grid_spec=pltpu.PrefetchScalarGridSpec(
            num_scalar_prefetch=2,
            grid=(micro,),
            in_specs=[whole_micro(a) for a in (qp, km, kmt, v, dc)]
            + [
                pl.BlockSpec((None, half, length), lambda m, *_: (m, 0, 0)),
                pl.BlockSpec((None, 8, length), lambda m, *_: (m, 0, 0)),
            ]
            + [whole_micro(a) for a in (gk, gq, kind_col)],
            out_specs=[
                pl.BlockSpec((halves, None, local, 3 * width), lambda m, *_: (0, m, 0, 0)),
                pl.BlockSpec((8, 3 * width), lambda m, *_: (0, 0)),
            ],
            scratch_shapes=[
                pltpu.VMEM((width, BLOCK), f32),
                pltpu.VMEM((length, width), f32),
                pltpu.VMEM((length, half), f32),
                pltpu.VMEM((8, BLOCK), f32),
            ],
        ),
        out_shape=[
            jax.ShapeDtypeStruct((halves, micro, local, 3 * width), bf16),
            jax.ShapeDtypeStruct((8, 3 * width), f32),
        ],
        compiler_params=pltpu.CompilerParams(vmem_limit_bytes=VMEM_LIMIT),
        cost_estimate=cost(
            micro * heads * length * length * 1280, micro * length * width * 16, micro * heads * length * length
        ),
        name="attend_back",
    )(low, high, qp, km, kmt, v, dc, ct, lse, gk, gq, kind_col)


def norm_forward(hidden):
    center = hidden - jnp.mean(hidden, axis=-1, keepdims=True)
    rescale = lax.rsqrt(jnp.mean(center * center, axis=-1, keepdims=True) + layer_eps)
    return center * rescale, rescale


def norm_backward(upstream, normed, rescale, gain):
    scaled = upstream * gain
    return rescale * (
        scaled
        - jnp.mean(scaled, axis=-1, keepdims=True)
        - normed * jnp.mean(scaled * normed, axis=-1, keepdims=True)
    )


def column_sum(values):
    return jnp.sum(values.astype(f32), axis=0, keepdims=True)


def chain_kernel(
    side_ref,
    x_ref,
    own_ref,
    other_ref,
    cot_ref,
    w_ref,
    vec_ref,
    mixed_ref,
    dh_ref,
    left_ref,
    right_ref,
    dco_ref,
    dcx_ref,
    sums_ref,
    slope_sc,
    z_sc,
):
    width = x_ref.shape[1]
    half = width // 2
    rows = width // GROUPS
    chunks = 4
    first = side_ref[0] == 0

    @pl.when(pl.program_id(0) == 0)
    def _():
        sums_ref[...] = jnp.zeros_like(sums_ref)

    def vector(at):
        return vec_ref[at : at + 1, :]

    def up_chunk(j):
        at = pl.multiple_of(5 * rows + j * rows, 16)
        return w_ref[:, pl.ds(at, rows), :].reshape(width, width)

    def down_chunk(j):
        return w_ref[pl.ds(j * (GROUPS // chunks), GROUPS // chunks), 0 : 4 * rows, :].reshape(width, width)

    def out_weight():
        return w_ref[:, 4 * rows : 5 * rows, :].reshape(width, width)

    own = own_ref[...].astype(f32)
    other = other_ref[...].astype(f32)
    context = jnp.concatenate(
        [jnp.where(first, own, other), jnp.where(first, other, own)], axis=1
    ).astype(bf16)
    left_ref[:, 0:width] = context
    hidden = x_ref[...].astype(f32) + (nn(context, out_weight()) + vector(0))
    n1, r1 = norm_forward(hidden)
    y1 = n1 * vector(1) + vector(2)
    left_ref[:, width : 2 * width] = y1.astype(bf16)
    z_sc[...] = y1 + vector(7)

    @pl.loop(0, chunks)
    def _(j):
        u = nn(left_ref[:, width : 2 * width], up_chunk(j)) + vec_ref[pl.ds(j + 3, 1), :]
        cumulative = 0.5 * (1.0 + lax.erf(u * 0.7071067811865476))
        at = pl.multiple_of(j * width, 128)
        slope_sc[:, pl.ds(at, width)] = (
            cumulative + u * jnp.exp(-0.5 * u * u) * 0.3989422804014327
        )
        g = (u * cumulative).astype(bf16)
        left_ref[:, pl.ds(pl.multiple_of(at + 2 * width, 128), width)] = g
        z_sc[...] += nn(g, down_chunk(j))

    n2, r2 = norm_forward(z_sc[...])
    mixed_ref[...] = (n2 * vector(8) + vector(9)).astype(bf16)
    upstream = cot_ref[...].astype(f32)
    sums_ref[0:1, :] += column_sum(upstream * n2)
    sums_ref[1:2, :] += column_sum(upstream)
    dh2 = norm_backward(upstream, n2, r2, vector(8))
    dz = dh2.astype(bf16)
    right_ref[:, 5 * width :] = dz
    sums_ref[2:3, :] += column_sum(dz)
    z_sc[...] = dh2

    @pl.loop(0, chunks)
    def _(j):
        at = pl.multiple_of(j * width, 128)
        du = (
            nt(right_ref[:, 5 * width :], down_chunk(j)) * slope_sc[:, pl.ds(at, width)]
        ).astype(bf16)
        right_ref[:, pl.ds(pl.multiple_of(at + width, 128), width)] = du
        sums_ref[pl.ds(j + 8, 1), :] += column_sum(du)
        z_sc[...] += nt(du, up_chunk(j))

    dy1 = z_sc[...]
    hidden = x_ref[...].astype(f32) + (nn(left_ref[:, 0:width], out_weight()) + vector(0))
    n1, r1 = norm_forward(hidden)
    sums_ref[3:4, :] += column_sum(dy1 * n1)
    sums_ref[4:5, :] += column_sum(dy1)
    dh1 = norm_backward(dy1, n1, r1, vector(1))
    dh_ref[...] = dh1
    da = dh1.astype(bf16)
    right_ref[:, 0:width] = da
    sums_ref[5:6, :] += column_sum(da)
    dc = nt(da, out_weight())
    dco_ref[...] = jnp.where(first, dc[:, :half], dc[:, half:]).astype(bf16)
    dcx_ref[...] = jnp.where(first, dc[:, half:], dc[:, :half]).astype(bf16)


def chain(side, x, c_own, c_other, cot, weights, vectors):
    tokens, width = x.shape
    half = width // 2

    def rows_spec(cols):
        return pl.BlockSpec((BLOCK, cols), lambda i, *_: (i, 0))

    def shape(cols, kind):
        return jax.ShapeDtypeStruct((tokens, cols), kind)

    return pl.pallas_call(
        chain_kernel,
        grid_spec=pltpu.PrefetchScalarGridSpec(
            num_scalar_prefetch=1,
            grid=(tokens // BLOCK,),
            in_specs=[
                rows_spec(width),
                rows_spec(half),
                rows_spec(half),
                rows_spec(width),
                pl.BlockSpec(weights.shape, lambda i, *_: (0, 0, 0), pipeline_mode=pl.Buffered(1)),
                pl.BlockSpec(vectors.shape, lambda i, *_: (0, 0)),
            ],
            out_specs=[
                rows_spec(width),
                rows_spec(width),
                rows_spec(6 * width),
                rows_spec(6 * width),
                rows_spec(half),
                rows_spec(half),
                pl.BlockSpec((16, width), lambda i, *_: (0, 0)),
            ],
            scratch_shapes=[pltpu.VMEM((BLOCK, 4 * width), f32), pltpu.VMEM((BLOCK, width), f32)],
        ),
        out_shape=[
            shape(width, bf16),
            shape(width, f32),
            shape(6 * width, bf16),
            shape(6 * width, bf16),
            shape(half, bf16),
            shape(half, bf16),
            jax.ShapeDtypeStruct((16, width), f32),
        ],
        compiler_params=pltpu.CompilerParams(vmem_limit_bytes=VMEM_LIMIT),
        cost_estimate=cost(2 * tokens * width * width * 19, tokens * width * 36 + weights.size * 2),
        name="chain",
    )(side[None], x, c_own, c_other, cot, weights, vectors)


def feed_grad_kernel(l_ref, r_ref, out_ref):
    width = l_ref.shape[1]
    rows = width // GROUPS
    at = pl.program_id(0)
    grad = tn(l_ref[...], r_ref[...]).astype(bf16)

    @pl.when(at == 0)
    def _():
        out_ref[:, 4 * rows : 5 * rows, :] = grad.reshape(GROUPS, rows, width)

    @pl.when((at >= 1) & (at < 5))
    def _():
        start = pl.multiple_of(5 * rows + (at - 1) * rows, 16)
        out_ref[:, pl.ds(start, rows), :] = grad.reshape(GROUPS, rows, width)

    @pl.when(at >= 5)
    def _():
        out_ref[pl.ds((at - 5) * 4, 4), 0 : 4 * rows, :] = grad.reshape(4, 4 * rows, width)


def feed_grad(left, right):
    tokens = left.shape[0]
    width = left.shape[1] // 6
    rows = width // GROUPS

    def left_at(i):
        return (0, jnp.where(i == 0, 0, jnp.where(i < 5, 1, i - 3)))

    def right_at(i):
        return (0, jnp.minimum(i, 5))

    return pl.pallas_call(
        feed_grad_kernel,
        grid=(9,),
        in_specs=[
            pl.BlockSpec((tokens, width), left_at),
            pl.BlockSpec((tokens, width), right_at),
        ],
        out_specs=pl.BlockSpec((GROUPS, 9 * rows, width), lambda i: (0, 0, 0)),
        out_shape=jax.ShapeDtypeStruct((GROUPS, 9 * rows, width), bf16),
        compiler_params=pltpu.CompilerParams(vmem_limit_bytes=VMEM_LIMIT),
        cost_estimate=cost(2 * tokens * width * width * 9, tokens * width * 24 + width * width * 18),
        name="feed_grad",
    )(left, right)


def attn_grad_kernel(x_ref, d_ref, vec_ref, out_ref):
    width = x_ref.shape[1]
    rows = width // GROUPS
    at = pl.program_id(0)
    grad = tn(x_ref[...], d_ref[...]).astype(bf16)
    start = pl.multiple_of(at * rows, 16)
    out_ref[:, pl.ds(start, rows), :] = grad.reshape(GROUPS, rows, width)
    out_ref[:, 3 * rows :, :] = vec_ref[...]


def attn_grad(x, d, vectors):
    tokens, width = x.shape
    rows = width // GROUPS
    return pl.pallas_call(
        attn_grad_kernel,
        grid=(3,),
        in_specs=[
            pl.BlockSpec((tokens, width), lambda i: (0, 0)),
            pl.BlockSpec((tokens, width), lambda i: (0, i)),
            pl.BlockSpec((GROUPS, 16, width), lambda i: (0, 0, 0)),
        ],
        out_specs=pl.BlockSpec((GROUPS, 3 * rows + 16, width), lambda i: (0, 0, 0)),
        out_shape=jax.ShapeDtypeStruct((GROUPS, 3 * rows + 16, width), bf16),
        compiler_params=pltpu.CompilerParams(vmem_limit_bytes=VMEM_LIMIT),
        cost_estimate=cost(2 * tokens * width * width * 3, tokens * width * 8 + width * width * 6),
        name="attn_grad",
    )(x, d, vectors)


def input_grad_kernel(d_ref, w_ref, out_ref):
    width = out_ref.shape[1]
    rows = width // GROUPS
    total = None
    for i in range(3):
        part = nt(
            d_ref[:, i * width : i * width + width],
            w_ref[:, i * rows : i * rows + rows, :].reshape(width, width),
        )
        total = part if total is None else total + part
    out_ref[...] = total.astype(out_ref.dtype)


def input_grad_part(d, weights, side_at, kind):
    _, micro, local, wide = d.shape
    width = wide // 3
    sub = local // BLOCK
    return pl.pallas_call(
        input_grad_kernel,
        grid=(micro, sub),
        in_specs=[
            pl.BlockSpec((None, None, BLOCK, wide), lambda m, i: (side_at, m, i, 0)),
            pl.BlockSpec(weights.shape, lambda m, i: (0, 0, 0)),
        ],
        out_specs=pl.BlockSpec((None, BLOCK, width), lambda m, i: (m, i, 0)),
        out_shape=jax.ShapeDtypeStruct((micro, local, width), kind),
        compiler_params=pltpu.CompilerParams(vmem_limit_bytes=VMEM_LIMIT),
        cost_estimate=cost(2 * micro * local * wide * width, micro * local * wide * 2 + weights.size * 2),
        name="input_grad",
    )(d, weights)


def on_device(
    tokens,
    kinds,
    groups,
    query_weight,
    query_bias,
    key_weight,
    key_bias,
    value_weight,
    value_bias,
    output_weight,
    output_bias,
    norm1_gain,
    norm1_shift,
    up_weight,
    up_bias,
    down_weight,
    down_bias,
    norm2_gain,
    norm2_shift,
    cotangent,
):
    micro, _, local, width = tokens.shape
    half = width // 2
    head_dim = width // HEADS
    devices = lax.axis_size("shard")
    rows = width // devices
    side = lax.axis_index("seq").astype(jnp.int32)
    per = local // BLOCK

    vector = jnp.concatenate(
        [
            query_bias,
            key_bias,
            value_bias,
            output_bias,
            norm1_gain,
            norm1_shift,
            up_bias,
            down_bias,
            norm2_gain,
            norm2_shift,
        ]
    )
    piece = vector.shape[0]
    vector_row = jnp.pad(vector, (0, width - piece))[None]
    attn_sizes = (rows, rows, rows)
    feed_sizes = (4 * rows,) + (rows,) * 5
    packed = pack_attention(query_weight, key_weight, value_weight, vector_row, side, head_dim)
    packed, down_weight, output_weight, up_weight = lax.optimization_barrier(
        (packed, down_weight, output_weight, up_weight)
    )
    attn_gathered = lax.all_gather(packed[None], "shard", axis=0, tiled=True)
    feed_local = jnp.concatenate(
        [down_weight, output_weight] + [up_weight[:, j * width : j * width + width] for j in range(4)],
        axis=0,
    )
    feed_gathered = lax.all_gather(feed_local[None], "shard", axis=0, tiled=True)
    vectors = attn_gathered[:, 3 * rows, :piece]
    if devices == GROUPS:
        attn_w, feed_w = attn_gathered, feed_gathered
    else:
        attn_w = regroup(attn_gathered, attn_sizes)
        feed_w = regroup(feed_gathered, feed_sizes)

    def whole_vector(start, size):
        return vectors[:, start : start + size].reshape(-1).astype(f32)

    full_query_bias = whole_vector(0, 4 * rows)
    full_key_bias = whole_vector(4 * rows, rows)
    full_value_bias = whole_vector(5 * rows, rows)
    bias_rows = jnp.concatenate(
        [
            pair_columns(full_query_bias, side, head_dim),
            jnp.concatenate([own_half(full_key_bias, side), own_half(full_value_bias, side)])[None],
        ],
        axis=0,
    )
    full_up_bias = whole_vector(9 * rows, 4 * rows).reshape(4, width)
    chain_vectors = jnp.concatenate(
        [
            whole_vector(6 * rows, rows)[None],
            whole_vector(7 * rows, rows)[None],
            whole_vector(8 * rows, rows)[None],
            full_up_bias,
            whole_vector(13 * rows, rows)[None],
            whole_vector(14 * rows, rows)[None],
            whole_vector(15 * rows, rows)[None],
        ],
        axis=0,
    )

    own_tokens = tokens[:, 0]
    marks = jnp.stack([kinds[:, 0], groups[:, 0]])
    xs = jnp.stack([own_tokens, swap(own_tokens)])
    both_marks = jnp.stack([marks, swap(marks)])
    kind_all, group_all = both_marks[:, 0], both_marks[:, 1]
    kind_col = kind_all[..., None]
    gk = group_all[..., None]
    gq = group_all[:, :, None, :]
    by_block = group_all.reshape(2, micro, per, BLOCK)
    low = jnp.swapaxes(by_block[..., 0], 0, 1).reshape(-1)
    high = jnp.swapaxes(by_block[..., BLOCK - 1], 0, 1).reshape(-1)

    qp, km, kmt, v, vt = project(xs, attn_w, bias_rows, kind_col)
    c, ct, lse = attend(low, high, qp, km, vt, gk, gq)
    c_other = swap(c[1])
    flat = micro * local
    mixed, dh1, left, right, dc_own, dc_other, sums = chain(
        side,
        own_tokens.reshape(flat, width),
        c[0].reshape(flat, half),
        c_other.reshape(flat, half),
        cotangent.reshape(flat, width),
        feed_w,
        chain_vectors,
    )

    dc_swapped = swap(dc_other)
    feed_part = feed_grad(left, right)
    dc_swapped, feed_part = lax.optimization_barrier((dc_swapped, feed_part))
    dc = jnp.stack([dc_own, dc_swapped]).reshape(2, micro, local, half)
    if devices != GROUPS:
        feed_part = ungroup(feed_part, feed_sizes, devices)
    feed_sum = lax.psum_scatter(feed_part, "shard", scatter_dimension=0, tiled=True)[0]
    d, db = attend_back(low, high, qp, km, kmt, v, dc, ct, lse, gk, gq, kind_col)

    query_own = unpair_columns(db[0, : 2 * width].reshape(2, width), head_dim)
    zero = jnp.zeros((half,), f32)

    def spread(own):
        return jnp.where(side == 0, jnp.concatenate([own, zero]), jnp.concatenate([zero, own]))

    query_spread = jnp.concatenate([spread(query_own[e, w]) for e in range(2) for w in range(2)])
    key_spread = spread(db[0, 2 * width : 2 * width + half])
    value_spread = spread(db[0, 2 * width + half :])
    grad_vectors = jnp.concatenate(
        [
            query_spread.reshape(devices, 4 * rows),
            key_spread.reshape(devices, rows),
            value_spread.reshape(devices, rows),
            sums[5].reshape(devices, rows),
            sums[3].reshape(devices, rows),
            sums[4].reshape(devices, rows),
            sums[8:12].reshape(devices, 4 * rows),
            sums[2].reshape(devices, rows),
            sums[0].reshape(devices, rows),
            sums[1].reshape(devices, rows),
        ],
        axis=1,
    ).astype(bf16)
    grad_vectors = jnp.pad(grad_vectors[:, None, :], ((0, 0), (0, 15), (0, width - piece)))
    if devices == GROUPS:
        attn_part = attn_grad(xs.reshape(2 * flat, width), d.reshape(2 * flat, 3 * width), grad_vectors)
    else:
        zeros = jnp.zeros((GROUPS, 16, width), bf16)
        attn_part = attn_grad(xs.reshape(2 * flat, width), d.reshape(2 * flat, 3 * width), zeros)
        attn_part = jnp.concatenate(
            [ungroup(attn_part[:, : 3 * (width // GROUPS)], attn_sizes, devices), grad_vectors], axis=1
        )
    attn_sum = lax.psum_scatter(attn_part, "shard", scatter_dimension=0, tiled=True)[0]

    dx_other = input_grad_part(d, attn_w, 1, bf16)
    dx_own = input_grad_part(d, attn_w, 0, f32)
    input_grad = dh1.reshape(micro, local, width) + dx_own + swap(dx_other).astype(f32)

    feed_total = feed_sum.astype(f32) + swap(feed_sum).astype(f32)
    grad_down = feed_total[: 4 * rows]
    grad_output = feed_total[4 * rows : 5 * rows]
    grad_up = jnp.concatenate(
        [feed_total[(5 + j) * rows : (6 + j) * rows] for j in range(4)], axis=1
    )
    attn_own = attn_sum.astype(f32)
    attn_other = swap(attn_sum).astype(f32)
    vec_total = attn_own[3 * rows, :piece] + attn_other[3 * rows, :piece]

    def by_side(own, other, axis):
        return jnp.where(
            side == 0,
            jnp.concatenate([own, other], axis=axis),
            jnp.concatenate([other, own], axis=axis),
        )

    def query_parts(block):
        pairs = jnp.stack([block[:rows], block[rows : 2 * rows]], axis=1)
        return unpair_columns(pairs, head_dim)

    grad_query = by_side(query_parts(attn_own), query_parts(attn_other), 3).reshape(rows, 4 * width)
    kv_own, kv_other = attn_own[2 * rows : 3 * rows], attn_other[2 * rows : 3 * rows]
    grad_key = by_side(kv_own[:, :half], kv_other[:, :half], 1)
    grad_value = by_side(kv_own[:, half:], kv_other[:, half:], 1)

    def piece_of(start, size):
        return vec_total[start : start + size]

    return (
        mixed.reshape(micro, 1, local, width),
        input_grad[:, None],
        grad_query,
        piece_of(0, 4 * rows),
        grad_key,
        piece_of(4 * rows, rows),
        grad_value,
        piece_of(5 * rows, rows),
        grad_output,
        piece_of(6 * rows, rows),
        piece_of(7 * rows, rows),
        piece_of(8 * rows, rows),
        grad_up,
        piece_of(9 * rows, 4 * rows),
        grad_down,
        piece_of(13 * rows, rows),
        piece_of(14 * rows, rows),
        piece_of(15 * rows, rows),
    )


def solution(mesh):
    weight = P("shard", None)
    vector = P("shard")
    tokens = P(None, "shard", "seq", None)
    marks = P(None, "shard", "seq")
    return jax.shard_map(
        on_device,
        mesh=mesh,
        in_specs=(tokens, marks, marks)
        + (weight, vector) * 4
        + (vector, vector)
        + (weight, vector) * 2
        + (vector, vector)
        + (tokens,),
        out_specs=(tokens, tokens)
        + (weight, vector) * 4
        + (vector, vector)
        + (weight, vector) * 2
        + (vector, vector),
        check_vma=False,
    )
```

```python
import jax
import jax.numpy as jnp
from jax import lax
from jax.experimental import pallas as pl
from jax.experimental.pallas import tpu as pltpu
from jax.sharding import PartitionSpec as P


HEADS = 12
GROUPS = 16
BLOCK = 256
masked_score = -1e30
layer_eps = 1e-12
bf16 = jnp.bfloat16
f32 = jnp.float32
VMEM_LIMIT = 60 * 1024 * 1024


def nn(a, b):
    return lax.dot_general(a, b, (((1,), (0,)), ((), ())), preferred_element_type=f32)


def nt(a, b):
    return lax.dot_general(a, b, (((1,), (1,)), ((), ())), preferred_element_type=f32)


def tn(a, b):
    return lax.dot_general(a, b, (((0,), (0,)), ((), ())), preferred_element_type=f32)


def swap(value):
    return lax.ppermute(value, "seq", [(0, 1), (1, 0)])


def cost(flops, moved, trans=0):
    return pl.CostEstimate(flops=flops, bytes_accessed=moved, transcendentals=trans)


def low_lanes(shape):
    return lax.broadcasted_iota(jnp.int32, shape, len(shape) - 1) % 128 < 64


def pack_into(first, q_ref, k_ref, v_ref, vec, out_ref):
    rows, width = k_ref.shape
    half = width // 2

    def own(ref, base):
        return jnp.where(
            first,
            ref[:, base : base + half].astype(f32),
            ref[:, base + half : base + width].astype(f32),
        )

    lo = low_lanes((rows, 128))
    for e in range(2):
        word = own(q_ref, 2 * e * width)
        entity = own(q_ref, (2 * e + 1) * width)
        for t in range(half // 128):
            a = word[:, 128 * t : 128 * t + 128]
            b = entity[:, 128 * t : 128 * t + 128]
            even = jnp.where(lo, a, pltpu.roll(b, 64, 1))
            odd = jnp.where(lo, pltpu.roll(a, 64, 1), b)
            out_ref[e * rows : e * rows + rows, 256 * t : 256 * t + 128] = even.astype(bf16)
            out_ref[e * rows : e * rows + rows, 256 * t + 128 : 256 * t + 256] = odd.astype(bf16)
    out_ref[2 * rows : 3 * rows, :half] = own(k_ref, 0).astype(bf16)
    out_ref[2 * rows : 3 * rows, half:] = own(v_ref, 0).astype(bf16)
    out_ref[3 * rows :, :] = jnp.broadcast_to(vec, (16, width)).astype(bf16)


def spots():
    x = lax.axis_index("seq")
    me = lax.axis_index("shard")
    core = lax.rem(me, 2)
    y = lax.rem(me // 2, 2)
    z = me // 4
    return x, me, z, y, core


def slot_of(z, y, core):
    return z * 4 + y * 2 + core


def greet(peers):
    barrier = pltpu.get_barrier_semaphore()
    for peer in peers:
        pl.semaphore_signal(barrier, inc=1, device_id=peer, device_id_type=pl.DeviceIdType.MESH)
    pl.semaphore_wait(barrier, len(peers))


def all_peers():
    x, me, z, y, core = spots()
    peers = [(x, slot_of(z, y, 1 - core)), (x, slot_of(z, 1 - y, core)), (1 - x, me)]
    for step in range(1, 4):
        peers.append((x, slot_of(lax.rem(z + step, 4), y, core)))
    return peers


def send(src, dst, send_sem, recv_sem, device):
    return pltpu.make_async_remote_copy(
        src_ref=src,
        dst_ref=dst,
        send_sem=send_sem,
        recv_sem=recv_sem,
        device_id=device,
        device_id_type=pl.DeviceIdType.MESH,
    )


def gather_kernel(*refs):
    q_ref, k_ref, v_ref = refs[:3]
    vec_refs = refs[3:13]
    tok_ref, kinds_ref, groups_ref = refs[13:16]
    w_ref, tok_out, kinds_out, groups_out = refs[16:20]
    mine, keep_sem, x_send, x_recv, z_send, z_recv, y_send, y_recv, c_send, c_recv = refs[20:]
    x, me, z, y, core = spots()
    across = (1 - x, me)
    beside = (x, slot_of(z, 1 - y, core))
    partner = (x, slot_of(z, y, 1 - core))
    greet(all_peers())
    over = [
        send(src, dst, x_send.at[i], x_recv.at[i], across)
        for i, (src, dst) in enumerate(
            ((kinds_ref, kinds_out), (groups_ref, groups_out), (tok_ref, tok_out))
        )
    ]
    for copy in over:
        copy.start()
    vec = jnp.concatenate([r[...].astype(f32) for r in vec_refs], axis=1)
    pack_into(x == 0, q_ref, k_ref, v_ref, vec, mine)
    started = []
    for step in range(1, 4):
        copy = send(
            mine,
            w_ref.at[me],
            z_send.at[step - 1],
            z_recv.at[z],
            (x, slot_of(lax.rem(z + step, 4), y, core)),
        )
        copy.start()
        started.append(copy)
    copy = send(mine, w_ref.at[me], y_send.at[z], y_recv.at[z], beside)
    copy.start()
    started.append(copy)
    copy = send(mine, w_ref.at[me], c_send.at[z * 2 + y], c_recv.at[z * 2 + y], partner)
    copy.start()
    started.append(copy)
    keep = pltpu.make_async_copy(mine, w_ref.at[me], keep_sem)
    keep.start()
    for step in range(1, 4):
        zz = lax.rem(z + step, 4)
        at = slot_of(zz, y, core)
        held = w_ref.at[at]
        send(held, held, z_send.at[0], z_recv.at[zz], partner).wait_recv()
        for copy in (
            send(held, held, y_send.at[zz], y_recv.at[zz], beside),
            send(held, held, c_send.at[zz * 2 + y], c_recv.at[zz * 2 + y], partner),
        ):
            copy.start()
            started.append(copy)
    for step in range(4):
        zz = lax.rem(z + step, 4)
        rail = zz * 2 + 1 - y
        held = w_ref.at[slot_of(zz, 1 - y, core)]
        send(held, held, y_send.at[0], y_recv.at[zz], partner).wait_recv()
        copy = send(held, held, c_send.at[rail], c_recv.at[rail], partner)
        copy.start()
        started.append(copy)
    for rail in range(8):
        held = w_ref.at[2 * rail + 1 - core]
        send(held, held, c_send.at[0], c_recv.at[rail], partner).wait_recv()
    keep.wait()
    for copy in started:
        copy.wait_send()
    for copy in over:
        copy.wait()


def gather_attention(query_weight, key_weight, value_weight, vectors, tokens, kinds, groups):
    rows, width = key_weight.shape
    vmem = pl.BlockSpec(memory_space=pltpu.VMEM)
    anywhere = pl.BlockSpec(memory_space=pl.ANY)
    sem = pltpu.SemaphoreType.DMA
    return pl.pallas_call(
        gather_kernel,
        in_specs=[vmem] * 13 + [anywhere] * 3,
        out_specs=[anywhere] * 4,
        out_shape=[
            jax.ShapeDtypeStruct((GROUPS, 3 * rows + 16, width), bf16),
            jax.ShapeDtypeStruct(tokens.shape, tokens.dtype),
            jax.ShapeDtypeStruct(kinds.shape, kinds.dtype),
            jax.ShapeDtypeStruct(groups.shape, groups.dtype),
        ],
        scratch_shapes=[
            pltpu.VMEM((3 * rows + 16, width), bf16),
            sem,
            sem((3,)),
            sem((3,)),
            sem((3,)),
            sem((4,)),
            sem((4,)),
            sem((4,)),
            sem((8,)),
            sem((8,)),
        ],
        compiler_params=pltpu.CompilerParams(
            collective_id=0, has_side_effects=True, vmem_limit_bytes=VMEM_LIMIT
        ),
        name="gather",
    )(query_weight, key_weight, value_weight, *[v[None] for v in vectors], tokens, kinds, groups)


def pair_columns(columns, side, head_dim):
    lead = columns.shape[:-1]
    per = columns.shape[-1] // (8 * head_dim)
    view = columns.reshape(lead + (2, 2, 2, per, head_dim))
    view = jnp.where(side == 0, view[..., 0, :, :], view[..., 1, :, :])
    return jnp.swapaxes(view, -3, -2).reshape(lead + (2, -1))


def unpair_columns(pairs, head_dim):
    lead = pairs.shape[:-2]
    per = pairs.shape[-1] // (2 * head_dim)
    view = pairs.reshape(lead + (2, per, 2, head_dim))
    return jnp.swapaxes(view, -3, -2).reshape(lead + (2, 2, per * head_dim))


def own_half(columns, side):
    half = columns.shape[-1] // 2
    return jnp.where(side == 0, columns[..., :half], columns[..., half:])


def pack_attention(query_weight, key_weight, value_weight, vector, side, head_dim):
    width = key_weight.shape[1]
    pairs = pair_columns(query_weight, side, head_dim)
    key_value = jnp.concatenate([own_half(key_weight, side), own_half(value_weight, side)], axis=1)
    return jnp.concatenate(
        [pairs[:, 0], pairs[:, 1], key_value, jnp.broadcast_to(vector, (16, width))], axis=0
    )


def pack_feed_kernel(down_ref, output_ref, up_ref, out_ref):
    rows, width = output_ref.shape
    out_ref[0 : 4 * rows, :] = down_ref[...]
    out_ref[4 * rows : 5 * rows, :] = output_ref[...]
    for j in range(4):
        out_ref[(5 + j) * rows : (6 + j) * rows, :] = up_ref[:, j * width : j * width + width]


def pack_feed(down_weight, output_weight, up_weight):
    rows, width = output_weight.shape
    if rows % 16:
        return jnp.concatenate(
            [down_weight, output_weight]
            + [up_weight[:, j * width : j * width + width] for j in range(4)],
            axis=0,
        )
    vmem = pl.BlockSpec(memory_space=pltpu.VMEM)
    return pl.pallas_call(
        pack_feed_kernel,
        in_specs=[vmem] * 3,
        out_specs=vmem,
        out_shape=jax.ShapeDtypeStruct((9 * rows, width), bf16),
        name="pack_feed",
    )(down_weight, output_weight, up_weight)


def regroup(gathered, sizes):
    _, _, width = gathered.shape
    pieces = []
    start = 0
    for size in sizes:
        piece = gathered[:, start : start + size].reshape(GROUPS, -1, width)
        pieces.append(piece)
        start += size
    return jnp.concatenate(pieces, axis=1)


def ungroup(grouped, sizes, devices):
    _, _, width = grouped.shape
    pieces = []
    start = 0
    for size in sizes:
        wide = size * devices // GROUPS
        pieces.append(grouped[:, start : start + wide].reshape(devices, size, width))
        start += wide
    return jnp.concatenate(pieces, axis=1)


def project_kernel(x_ref, w_ref, bias_ref, kind_ref, qp_ref, km_ref, kmt_ref, v_ref, vt_ref):
    width = x_ref.shape[1]
    half = width // 2
    rows = width // GROUPS
    x = x_ref[...]
    kind = kind_ref[...]
    wa = w_ref[:, 0:rows, :].reshape(width, width)
    wb = w_ref[:, rows : 2 * rows, :].reshape(width, width)
    wkv = w_ref[:, 2 * rows : 3 * rows, :].reshape(width, width)
    qa = nn(x, wa) + bias_ref[0:1, :]
    qb = nn(x, wb) + bias_ref[1:2, :]
    qp_ref[...] = (jnp.where(kind == 1, qb, qa) * 0.125).astype(bf16)
    kv = nn(x, wkv) + bias_ref[2:3, :]
    lane_high = (lax.broadcasted_iota(jnp.int32, (BLOCK, 128), 1) >= 64).astype(jnp.int32)
    keep = lane_high == kind
    lo = lane_high == 0
    for t in range(half // 128):
        k = kv[:, 128 * t : 128 * t + 128]
        r = pltpu.roll(k, 64, 1)
        even = jnp.where(keep, jnp.where(lo, k, r), 0.0)
        odd = jnp.where(keep, jnp.where(lo, r, k), 0.0)
        km_ref[:, 256 * t : 256 * t + 128] = even.astype(bf16)
        km_ref[:, 256 * t + 128 : 256 * t + 256] = odd.astype(bf16)
        kmt_ref[256 * t : 256 * t + 128, :] = even.T.astype(bf16)
        kmt_ref[256 * t + 128 : 256 * t + 256, :] = odd.T.astype(bf16)
    v = kv[:, half:]
    v_ref[...] = v.astype(bf16)
    vt_ref[...] = v.T.astype(bf16)


def project(xs, weights, bias_rows, kind_col):
    halves, micro, local, width = xs.shape
    half = width // 2
    sub = local // BLOCK

    def rows_spec(cols):
        return pl.BlockSpec((None, None, BLOCK, cols), lambda a, m, i: (a, m, i, 0))

    def cols_spec(count):
        return pl.BlockSpec((None, None, count, BLOCK), lambda a, m, i: (a, m, 0, i))

    def shape(*dims):
        return jax.ShapeDtypeStruct((halves, micro) + dims, bf16)

    tokens = halves * micro * local
    return pl.pallas_call(
        project_kernel,
        grid=(halves, micro, sub),
        in_specs=[
            rows_spec(width),
            pl.BlockSpec(weights.shape, lambda a, m, i: (0, 0, 0)),
            pl.BlockSpec(bias_rows.shape, lambda a, m, i: (0, 0)),
            rows_spec(1),
        ],
        out_specs=[rows_spec(width), rows_spec(width), cols_spec(width), rows_spec(half), cols_spec(half)],
        out_shape=[
            shape(local, width),
            shape(local, width),
            shape(width, local),
            shape(local, half),
            shape(half, local),
        ],
        compiler_params=pltpu.CompilerParams(vmem_limit_bytes=VMEM_LIMIT),
        cost_estimate=cost(2 * tokens * width * 3 * width, tokens * width * 10),
        name="project",
    )(xs, weights, bias_rows, kind_col)


def place(block, per):
    return block // per, pl.multiple_of(lax.rem(block, per) * BLOCK, BLOCK)


def attend_kernel(
    low_ref, high_ref, qp_ref, km_ref, vt_ref, gk_ref, gq_ref, c_ref, ct_ref, lse_ref, m_sc, l_sc, acc_sc
):
    micro_at = pl.program_id(0)
    local = qp_ref.shape[1]
    per = local // BLOCK
    blocks = 2 * per
    heads = qp_ref.shape[2] // 128
    base = micro_at * blocks

    @pl.loop(0, blocks)
    def _(qb):
        qh, qo = place(qb, per)
        m_sc[...] = jnp.full_like(m_sc, masked_score)
        l_sc[...] = jnp.zeros_like(l_sc)
        acc_sc[...] = jnp.zeros_like(acc_sc)
        q_low, q_high = low_ref[base + qb], high_ref[base + qb]

        @pl.loop(0, blocks)
        def _(kb):
            @pl.when((q_low <= high_ref[base + kb]) & (low_ref[base + kb] <= q_high))
            def _():
                kh, ko = place(kb, per)
                same = gk_ref[kh, pl.ds(ko, BLOCK), :] == gq_ref[qh, :, pl.ds(qo, BLOCK)]
                bias = jnp.where(same, 0.0, masked_score)
                for h in range(heads):
                    at = slice(128 * h, 128 * h + 128)
                    vat = slice(64 * h, 64 * h + 64)
                    s = nt(km_ref[kh, pl.ds(ko, BLOCK), at], qp_ref[qh, pl.ds(qo, BLOCK), at]) + bias
                    m_old = m_sc[h : h + 1, :]
                    m_new = jnp.maximum(m_old, jnp.max(s, axis=0, keepdims=True))
                    alpha = jnp.exp(m_old - m_new)
                    p = jnp.exp(s - m_new)
                    m_sc[h : h + 1, :] = m_new
                    l_sc[h : h + 1, :] = alpha * l_sc[h : h + 1, :] + jnp.sum(p, axis=0, keepdims=True)
                    acc_sc[vat, :] = alpha * acc_sc[vat, :] + nn(
                        vt_ref[kh, vat, pl.ds(ko, BLOCK)], p.astype(bf16)
                    )

        cols = pl.ds(pl.multiple_of(qb * BLOCK, BLOCK), BLOCK)
        for h in range(heads):
            vat = slice(64 * h, 64 * h + 64)
            total = l_sc[h : h + 1, :]
            ct_ref[vat, cols] = acc_sc[vat, :] / total
            lse_ref[h : h + 1, cols] = m_sc[h : h + 1, :] + jnp.log(total)
        c_ref[qh, pl.ds(qo, BLOCK), :] = ct_ref[:, cols].T.astype(bf16)


def whole_micro(array):
    rest = array.shape[2:]
    return pl.BlockSpec((array.shape[0], None) + rest, lambda m, *_: (0, m) + (0,) * len(rest))


def attend(low, high, qp, km, vt, gk, gq):
    halves, micro, local, width = qp.shape
    half = width // 2
    heads = width // 128
    length = halves * local
    return pl.pallas_call(
        attend_kernel,
        grid_spec=pltpu.PrefetchScalarGridSpec(
            num_scalar_prefetch=2,
            grid=(micro,),
            in_specs=[whole_micro(a) for a in (qp, km, vt, gk, gq)],
            out_specs=[
                pl.BlockSpec((halves, None, local, half), lambda m, *_: (0, m, 0, 0)),
                pl.BlockSpec((None, half, length), lambda m, *_: (m, 0, 0)),
                pl.BlockSpec((None, 8, length), lambda m, *_: (m, 0, 0)),
            ],
            scratch_shapes=[
                pltpu.VMEM((8, BLOCK), f32),
                pltpu.VMEM((8, BLOCK), f32),
                pltpu.VMEM((half, BLOCK), f32),
            ],
        ),
        out_shape=[
            jax.ShapeDtypeStruct((halves, micro, local, half), bf16),
            jax.ShapeDtypeStruct((micro, half, length), f32),
            jax.ShapeDtypeStruct((micro, 8, length), f32),
        ],
        compiler_params=pltpu.CompilerParams(vmem_limit_bytes=VMEM_LIMIT),
        cost_estimate=cost(
            micro * heads * length * length * 512, micro * length * width * 8, micro * heads * length * length
        ),
        name="attend",
    )(low, high, qp, km, vt, gk, gq)


def attend_back_kernel(
    low_ref,
    high_ref,
    qp_ref,
    km_ref,
    kmt_ref,
    v_ref,
    dc_ref,
    ct_ref,
    lse_ref,
    gk_ref,
    gq_ref,
    kind_ref,
    d_ref,
    db_ref,
    dqt_sc,
    dk_sc,
    dv_sc,
    delta_sc,
):
    micro_at = pl.program_id(0)
    local, width = qp_ref.shape[1], qp_ref.shape[2]
    half = width // 2
    per = local // BLOCK
    blocks = 2 * per
    tiles = half // 128
    base = micro_at * blocks
    dk_sc[...] = jnp.zeros_like(dk_sc)
    dv_sc[...] = jnp.zeros_like(dv_sc)

    @pl.when(micro_at == 0)
    def _():
        db_ref[...] = jnp.zeros_like(db_ref)

    lo = low_lanes((BLOCK, 128))

    @pl.loop(0, blocks)
    def _(qb):
        qh, qo = place(qb, per)
        qrows = pl.ds(qo, BLOCK)
        cols = pl.ds(pl.multiple_of(qb * BLOCK, BLOCK), BLOCK)
        dct = dc_ref[qh, qrows, :].astype(f32).T
        inner = dct * ct_ref[:, cols]
        for h in range(2 * tiles):
            delta_sc[h : h + 1, :] = jnp.sum(inner[64 * h : 64 * h + 64, :], axis=0, keepdims=True)
        dqt_sc[...] = jnp.zeros_like(dqt_sc)
        q_low, q_high = low_ref[base + qb], high_ref[base + qb]

        @pl.loop(0, blocks)
        def _(kb):
            @pl.when((q_low <= high_ref[base + kb]) & (low_ref[base + kb] <= q_high))
            def _():
                kh, ko = place(kb, per)
                krows = pl.ds(ko, BLOCK)
                drows = pl.ds(pl.multiple_of(kb * BLOCK, BLOCK), BLOCK)
                same = gk_ref[kh, krows, :] == gq_ref[qh, :, qrows]
                bias = jnp.where(same, 0.0, masked_score)
                for t in range(tiles):
                    tat = slice(128 * t, 128 * t + 128)
                    v = v_ref[kh, krows, tat]
                    dc = dc_ref[qh, qrows, tat]
                    from_pair = []
                    for side in range(2):
                        h = 2 * t + side
                        at = slice(128 * h, 128 * h + 128)
                        q = qp_ref[qh, qrows, at]
                        s = nt(km_ref[kh, krows, at], q) + bias
                        p = jnp.exp(s - lse_ref[h : h + 1, cols])
                        zero = jnp.zeros_like(v)
                        vm = jnp.where(lo, v, zero) if side == 0 else jnp.where(lo, zero, v)
                        dp = nt(vm, dc)
                        ds = (p * (dp - delta_sc[h : h + 1, :])).astype(bf16)
                        dk_sc[drows, at] += nn(ds, q)
                        dqt_sc[at, :] += nn(kmt_ref[kh, at, krows], ds)
                        from_pair.append(nn(p.astype(bf16), dc))
                    dv_sc[drows, tat] += jnp.where(lo, from_pair[0], from_pair[1])

        dq = dqt_sc[...].T * 0.125
        entity = kind_ref[qh, qrows, :] == 1
        d_ref[qh, qrows, 0:width] = jnp.where(entity, 0.0, dq).astype(bf16)
        d_ref[qh, qrows, width : 2 * width] = jnp.where(entity, dq, 0.0).astype(bf16)

    @pl.loop(0, blocks)
    def _(kb):
        kh, ko = place(kb, per)
        krows = pl.ds(ko, BLOCK)
        drows = pl.ds(pl.multiple_of(kb * BLOCK, BLOCK), BLOCK)
        entity = kind_ref[kh, krows, :] == 1
        for t in range(tiles):
            even = dk_sc[drows, 256 * t : 256 * t + 128]
            odd = dk_sc[drows, 256 * t + 128 : 256 * t + 256]
            left = jnp.where(entity, pltpu.roll(even, 64, 1), even)
            right = jnp.where(entity, odd, pltpu.roll(odd, 64, 1))
            d_ref[kh, krows, 2 * width + 128 * t : 2 * width + 128 * t + 128] = jnp.where(
                lo, left, right
            ).astype(bf16)
        d_ref[kh, krows, 2 * width + half : 3 * width] = dv_sc[drows, :].astype(bf16)
        db_ref[0:1, :] += jnp.sum(d_ref[kh, krows, :].astype(f32), axis=0, keepdims=True)


def attend_back(low, high, qp, km, kmt, v, dc, ct, lse, gk, gq, kind_col):
    halves, micro, local, width = qp.shape
    half = width // 2
    heads = width // 128
    length = halves * local
    return pl.pallas_call(
        attend_back_kernel,
        grid_spec=pltpu.PrefetchScalarGridSpec(
            num_scalar_prefetch=2,
            grid=(micro,),
            in_specs=[whole_micro(a) for a in (qp, km, kmt, v, dc)]
            + [
                pl.BlockSpec((None, half, length), lambda m, *_: (m, 0, 0)),
                pl.BlockSpec((None, 8, length), lambda m, *_: (m, 0, 0)),
            ]
            + [whole_micro(a) for a in (gk, gq, kind_col)],
            out_specs=[
                pl.BlockSpec((halves, None, local, 3 * width), lambda m, *_: (0, m, 0, 0)),
                pl.BlockSpec((8, 3 * width), lambda m, *_: (0, 0)),
            ],
            scratch_shapes=[
                pltpu.VMEM((width, BLOCK), f32),
                pltpu.VMEM((length, width), f32),
                pltpu.VMEM((length, half), f32),
                pltpu.VMEM((8, BLOCK), f32),
            ],
        ),
        out_shape=[
            jax.ShapeDtypeStruct((halves, micro, local, 3 * width), bf16),
            jax.ShapeDtypeStruct((8, 3 * width), f32),
        ],
        compiler_params=pltpu.CompilerParams(vmem_limit_bytes=VMEM_LIMIT),
        cost_estimate=cost(
            micro * heads * length * length * 1280, micro * length * width * 16, micro * heads * length * length
        ),
        name="attend_back",
    )(low, high, qp, km, kmt, v, dc, ct, lse, gk, gq, kind_col)


def norm_forward(hidden):
    center = hidden - jnp.mean(hidden, axis=-1, keepdims=True)
    rescale = lax.rsqrt(jnp.mean(center * center, axis=-1, keepdims=True) + layer_eps)
    return center * rescale, rescale


def norm_backward(upstream, normed, rescale, gain):
    scaled = upstream * gain
    return rescale * (
        scaled
        - jnp.mean(scaled, axis=-1, keepdims=True)
        - normed * jnp.mean(scaled * normed, axis=-1, keepdims=True)
    )


def column_sum(values):
    return jnp.sum(values.astype(f32), axis=0, keepdims=True)


def chain_kernel(
    side_ref,
    x_ref,
    own_ref,
    other_ref,
    cot_ref,
    w_ref,
    vec_ref,
    mixed_ref,
    dh_ref,
    left_ref,
    right_ref,
    dco_ref,
    dcx_ref,
    sums_ref,
    slope_sc,
    z_sc,
):
    width = x_ref.shape[1]
    half = width // 2
    rows = width // GROUPS
    chunks = 4
    first = side_ref[0] == 0

    @pl.when(pl.program_id(0) == 0)
    def _():
        sums_ref[...] = jnp.zeros_like(sums_ref)

    def vector(at):
        return vec_ref[at : at + 1, :]

    def up_chunk(j):
        at = pl.multiple_of(5 * rows + j * rows, 16)
        return w_ref[:, pl.ds(at, rows), :].reshape(width, width)

    def down_chunk(j):
        return w_ref[pl.ds(j * (GROUPS // chunks), GROUPS // chunks), 0 : 4 * rows, :].reshape(width, width)

    def out_weight():
        return w_ref[:, 4 * rows : 5 * rows, :].reshape(width, width)

    own = own_ref[...].astype(f32)
    other = other_ref[...].astype(f32)
    context = jnp.concatenate(
        [jnp.where(first, own, other), jnp.where(first, other, own)], axis=1
    ).astype(bf16)
    left_ref[:, 0:width] = context
    hidden = x_ref[...].astype(f32) + (nn(context, out_weight()) + vector(0))
    n1, r1 = norm_forward(hidden)
    y1 = n1 * vector(1) + vector(2)
    left_ref[:, width : 2 * width] = y1.astype(bf16)
    z_sc[...] = y1 + vector(7)

    @pl.loop(0, chunks)
    def _(j):
        u = nn(left_ref[:, width : 2 * width], up_chunk(j)) + vec_ref[pl.ds(j + 3, 1), :]
        cumulative = 0.5 * (1.0 + lax.erf(u * 0.7071067811865476))
        at = pl.multiple_of(j * width, 128)
        slope_sc[:, pl.ds(at, width)] = (
            cumulative + u * jnp.exp(-0.5 * u * u) * 0.3989422804014327
        )
        g = (u * cumulative).astype(bf16)
        left_ref[:, pl.ds(pl.multiple_of(at + 2 * width, 128), width)] = g
        z_sc[...] += nn(g, down_chunk(j))

    n2, r2 = norm_forward(z_sc[...])
    mixed_ref[...] = (n2 * vector(8) + vector(9)).astype(bf16)
    upstream = cot_ref[...].astype(f32)
    sums_ref[0:1, :] += column_sum(upstream * n2)
    sums_ref[1:2, :] += column_sum(upstream)
    dh2 = norm_backward(upstream, n2, r2, vector(8))
    dz = dh2.astype(bf16)
    right_ref[:, 5 * width :] = dz
    sums_ref[2:3, :] += column_sum(dz)
    z_sc[...] = dh2

    @pl.loop(0, chunks)
    def _(j):
        at = pl.multiple_of(j * width, 128)
        du = (
            nt(right_ref[:, 5 * width :], down_chunk(j)) * slope_sc[:, pl.ds(at, width)]
        ).astype(bf16)
        right_ref[:, pl.ds(pl.multiple_of(at + width, 128), width)] = du
        sums_ref[pl.ds(j + 8, 1), :] += column_sum(du)
        z_sc[...] += nt(du, up_chunk(j))

    dy1 = z_sc[...]
    hidden = x_ref[...].astype(f32) + (nn(left_ref[:, 0:width], out_weight()) + vector(0))
    n1, r1 = norm_forward(hidden)
    sums_ref[3:4, :] += column_sum(dy1 * n1)
    sums_ref[4:5, :] += column_sum(dy1)
    dh1 = norm_backward(dy1, n1, r1, vector(1))
    dh_ref[...] = dh1
    da = dh1.astype(bf16)
    right_ref[:, 0:width] = da
    sums_ref[5:6, :] += column_sum(da)
    dc = nt(da, out_weight())
    dco_ref[...] = jnp.where(first, dc[:, :half], dc[:, half:]).astype(bf16)
    dcx_ref[...] = jnp.where(first, dc[:, half:], dc[:, :half]).astype(bf16)


def chain(side, x, c_own, c_other, cot, weights, vectors):
    tokens, width = x.shape
    half = width // 2

    def rows_spec(cols):
        return pl.BlockSpec((BLOCK, cols), lambda i, *_: (i, 0))

    def shape(cols, kind):
        return jax.ShapeDtypeStruct((tokens, cols), kind)

    return pl.pallas_call(
        chain_kernel,
        grid_spec=pltpu.PrefetchScalarGridSpec(
            num_scalar_prefetch=1,
            grid=(tokens // BLOCK,),
            in_specs=[
                rows_spec(width),
                rows_spec(half),
                rows_spec(half),
                rows_spec(width),
                pl.BlockSpec(weights.shape, lambda i, *_: (0, 0, 0), pipeline_mode=pl.Buffered(1)),
                pl.BlockSpec(vectors.shape, lambda i, *_: (0, 0)),
            ],
            out_specs=[
                rows_spec(width),
                rows_spec(width),
                rows_spec(6 * width),
                rows_spec(6 * width),
                rows_spec(half),
                rows_spec(half),
                pl.BlockSpec((16, width), lambda i, *_: (0, 0)),
            ],
            scratch_shapes=[pltpu.VMEM((BLOCK, 4 * width), f32), pltpu.VMEM((BLOCK, width), f32)],
        ),
        out_shape=[
            shape(width, bf16),
            shape(width, f32),
            shape(6 * width, bf16),
            shape(6 * width, bf16),
            shape(half, bf16),
            shape(half, bf16),
            jax.ShapeDtypeStruct((16, width), f32),
        ],
        compiler_params=pltpu.CompilerParams(vmem_limit_bytes=VMEM_LIMIT),
        cost_estimate=cost(2 * tokens * width * width * 19, tokens * width * 36 + weights.size * 2),
        name="chain",
    )(side[None], x, c_own, c_other, cot, weights, vectors)


def feed_grad_kernel(l_ref, r_ref, out_ref):
    width = l_ref.shape[1]
    rows = width // GROUPS
    at = pl.program_id(0)
    grad = tn(l_ref[...], r_ref[...]).astype(bf16)

    @pl.when(at == 0)
    def _():
        out_ref[:, 4 * rows : 5 * rows, :] = grad.reshape(GROUPS, rows, width)

    @pl.when((at >= 1) & (at < 5))
    def _():
        start = pl.multiple_of(5 * rows + (at - 1) * rows, 16)
        out_ref[:, pl.ds(start, rows), :] = grad.reshape(GROUPS, rows, width)

    @pl.when(at >= 5)
    def _():
        out_ref[pl.ds((at - 5) * 4, 4), 0 : 4 * rows, :] = grad.reshape(4, 4 * rows, width)


def feed_grad(left, right):
    tokens = left.shape[0]
    width = left.shape[1] // 6
    rows = width // GROUPS

    def left_at(i):
        return (0, jnp.where(i == 0, 0, jnp.where(i < 5, 1, i - 3)))

    def right_at(i):
        return (0, jnp.minimum(i, 5))

    return pl.pallas_call(
        feed_grad_kernel,
        grid=(9,),
        in_specs=[
            pl.BlockSpec((tokens, width), left_at),
            pl.BlockSpec((tokens, width), right_at),
        ],
        out_specs=pl.BlockSpec((GROUPS, 9 * rows, width), lambda i: (0, 0, 0)),
        out_shape=jax.ShapeDtypeStruct((GROUPS, 9 * rows, width), bf16),
        compiler_params=pltpu.CompilerParams(vmem_limit_bytes=VMEM_LIMIT),
        cost_estimate=cost(2 * tokens * width * width * 9, tokens * width * 24 + width * width * 18),
        name="feed_grad",
    )(left, right)


def attn_grad_kernel(x_ref, d_ref, vec_ref, out_ref):
    width = x_ref.shape[1]
    rows = width // GROUPS
    at = pl.program_id(0)
    grad = tn(x_ref[...], d_ref[...]).astype(bf16)
    start = pl.multiple_of(at * rows, 16)
    out_ref[:, pl.ds(start, rows), :] = grad.reshape(GROUPS, rows, width)
    out_ref[:, 3 * rows :, :] = vec_ref[...]


def attn_grad(x, d, vectors):
    tokens, width = x.shape
    rows = width // GROUPS
    return pl.pallas_call(
        attn_grad_kernel,
        grid=(3,),
        in_specs=[
            pl.BlockSpec((tokens, width), lambda i: (0, 0)),
            pl.BlockSpec((tokens, width), lambda i: (0, i)),
            pl.BlockSpec((GROUPS, 16, width), lambda i: (0, 0, 0)),
        ],
        out_specs=pl.BlockSpec((GROUPS, 3 * rows + 16, width), lambda i: (0, 0, 0)),
        out_shape=jax.ShapeDtypeStruct((GROUPS, 3 * rows + 16, width), bf16),
        compiler_params=pltpu.CompilerParams(vmem_limit_bytes=VMEM_LIMIT),
        cost_estimate=cost(2 * tokens * width * width * 3, tokens * width * 8 + width * width * 6),
        name="attn_grad",
    )(x, d, vectors)


def scatter_kernel(
    x_ref,
    d_ref,
    vec_ref,
    gq_ref,
    gk_ref,
    gv_ref,
    gvec_ref,
    part,
    from_core,
    from_y,
    from_z,
    from_x,
    out_y,
    out_z,
    held,
    total,
    c_send,
    c_recv,
    y_send,
    y_recv,
    z_send,
    z_recv,
    x_send,
    x_recv,
):
    width = x_ref.shape[1]
    half = width // 2
    rows = width // GROUPS
    step_at = pl.program_id(0)
    x, me, z, y, core = spots()
    across = (1 - x, me)
    beside = (x, slot_of(z, 1 - y, core))
    partner = (x, slot_of(z, y, 1 - core))
    spans = ((0, rows), (rows, rows), (2 * rows, rows + 16))

    def core_copy(chunk, rail):
        start, size = spans[chunk]
        return send(
            part.at[2 * rail + 1 - core, pl.ds(start, size), :],
            from_core.at[rail, pl.ds(start, size), :],
            c_send.at[chunk * 8 + rail],
            c_recv.at[chunk * 8 + rail],
            partner,
        )

    @pl.when(step_at == 0)
    def _():
        greet(all_peers())

    grad = tn(x_ref[...], d_ref[...]).astype(bf16)
    for chunk in range(3):

        @pl.when(step_at == chunk)
        def _(chunk=chunk):
            start = spans[chunk][0]
            part[:, start : start + rows, :] = grad.reshape(GROUPS, rows, width)
            if chunk == 2:
                part[:, 3 * rows :, :] = vec_ref[...]
            for rail in range(8):
                core_copy(chunk, rail).start()

    @pl.when(step_at == 2)
    def _():
        def z_order(step):
            return lax.rem(z + 1 + step, 4)

        def y_copy(zz):
            return send(out_y.at[zz], from_y.at[zz], y_send.at[zz], y_recv.at[zz], beside)

        def z_copy(zz):
            return send(
                out_z.at[zz], from_z.at[z], z_send.at[zz], z_recv.at[z], (x, slot_of(zz, y, core))
            )

        def core_wait(rail):
            for chunk in range(3):
                start, size = spans[chunk]
                send(
                    part.at[0, pl.ds(start, size), :],
                    from_core.at[rail, pl.ds(start, size), :],
                    c_send.at[0],
                    c_recv.at[chunk * 8 + rail],
                    partner,
                ).wait_recv()

        for step in range(4):
            zz = z_order(step)
            rail = zz * 2 + 1 - y
            core_wait(rail)
            out_y[zz] = (part[2 * rail + core].astype(f32) + from_core[rail].astype(f32)).astype(bf16)
            y_copy(zz).start()
        for step in range(4):
            zz = z_order(step)
            rail = zz * 2 + y
            core_wait(rail)
            held[zz] = part[2 * rail + core].astype(f32) + from_core[rail].astype(f32)
        for step in range(3):
            zz = z_order(step)
            y_copy(zz).wait_recv()
            out_z[zz] = (held[zz] + from_y[zz].astype(f32)).astype(bf16)
            z_copy(zz).start()
        y_copy(z).wait_recv()
        result = held[z] + from_y[z].astype(f32)
        for step in range(3):
            zz = z_order(step)
            send(out_z.at[zz], from_z.at[zz], z_send.at[zz], z_recv.at[zz], partner).wait_recv()
            result = result + from_z[zz].astype(f32)
        total[...] = result.astype(bf16)
        last = send(total, from_x, x_send, x_recv, across)
        last.start()
        for chunk in range(3):
            for rail in range(8):
                core_copy(chunk, rail).wait_send()
        for step in range(4):
            y_copy(z_order(step)).wait_send()
        for step in range(3):
            z_copy(z_order(step)).wait_send()
        last.wait()
        first = x == 0
        lo = low_lanes((rows, 128))

        def ordered(start, size, at):
            own = total[start : start + size, at].astype(f32)
            other = from_x[start : start + size, at].astype(f32)
            return jnp.where(first, own, other), jnp.where(first, other, own)

        for e in range(2):
            for t in range(half // 128):
                evens = ordered(e * rows, rows, slice(256 * t, 256 * t + 128))
                odds = ordered(e * rows, rows, slice(256 * t + 128, 256 * t + 256))
                for s in range(2):
                    word = jnp.where(lo, evens[s], pltpu.roll(odds[s], 64, 1))
                    entity = jnp.where(lo, pltpu.roll(evens[s], 64, 1), odds[s])
                    base = 2 * e * width + s * half + 128 * t
                    gq_ref[:, base : base + 128] = word
                    gq_ref[:, base + width : base + width + 128] = entity
        for ref, base in ((gk_ref, 0), (gv_ref, half)):
            a, b = ordered(2 * rows, rows, slice(base, base + half))
            ref[:, :half] = a
            ref[:, half:] = b
        gvec_ref[...] = total[3 * rows :, :].astype(f32) + from_x[3 * rows :, :].astype(f32)


def scatter_attention(x, d, vectors):
    tokens, width = x.shape
    rows = width // GROUPS
    tall = 3 * rows + 16
    sem = pltpu.SemaphoreType.DMA

    def whole(*dims):
        return pl.BlockSpec(dims, lambda i: (0,) * len(dims))

    outs = ((rows, 4 * width), (rows, width), (rows, width), (16, width))
    return pl.pallas_call(
        scatter_kernel,
        grid=(3,),
        in_specs=[
            whole(tokens, width),
            pl.BlockSpec((tokens, width), lambda i: (0, i)),
            whole(GROUPS, 16, width),
        ],
        out_specs=[whole(*dims) for dims in outs],
        out_shape=[jax.ShapeDtypeStruct(dims, f32) for dims in outs],
        scratch_shapes=[
            pltpu.VMEM((GROUPS, tall, width), bf16),
            pltpu.VMEM((8, tall, width), bf16),
            pltpu.VMEM((4, tall, width), bf16),
            pltpu.VMEM((4, tall, width), bf16),
            pltpu.VMEM((tall, width), bf16),
            pltpu.VMEM((4, tall, width), bf16),
            pltpu.VMEM((4, tall, width), bf16),
            pltpu.VMEM((4, tall, width), f32),
            pltpu.VMEM((tall, width), bf16),
            sem((24,)),
            sem((24,)),
            sem((4,)),
            sem((4,)),
            sem((4,)),
            sem((4,)),
            sem,
            sem,
        ],
        compiler_params=pltpu.CompilerParams(
            collective_id=1, has_side_effects=True, vmem_limit_bytes=VMEM_LIMIT
        ),
        cost_estimate=cost(2 * tokens * width * width * 3, tokens * width * 8 + width * width * 6),
        name="scatter",
    )(x, d, vectors)


def input_grad_kernel(d_ref, w_ref, out_ref):
    width = out_ref.shape[1]
    rows = width // GROUPS
    total = None
    for i in range(3):
        part = nt(
            d_ref[:, i * width : i * width + width],
            w_ref[:, i * rows : i * rows + rows, :].reshape(width, width),
        )
        total = part if total is None else total + part
    out_ref[...] = total.astype(out_ref.dtype)


def input_grad_part(d, weights, side_at, kind):
    _, micro, local, wide = d.shape
    width = wide // 3
    sub = local // BLOCK
    return pl.pallas_call(
        input_grad_kernel,
        grid=(micro, sub),
        in_specs=[
            pl.BlockSpec((None, None, BLOCK, wide), lambda m, i: (side_at, m, i, 0)),
            pl.BlockSpec(weights.shape, lambda m, i: (0, 0, 0)),
        ],
        out_specs=pl.BlockSpec((None, BLOCK, width), lambda m, i: (m, i, 0)),
        out_shape=jax.ShapeDtypeStruct((micro, local, width), kind),
        compiler_params=pltpu.CompilerParams(vmem_limit_bytes=VMEM_LIMIT),
        cost_estimate=cost(2 * micro * local * wide * width, micro * local * wide * 2 + weights.size * 2),
        name="input_grad",
    )(d, weights)


def assemble(attn_own, attn_other, side, head_dim, rows, piece):
    attn_own, attn_other = attn_own.astype(f32), attn_other.astype(f32)
    width = attn_own.shape[1]
    half = width // 2
    vec_total = attn_own[3 * rows, :piece] + attn_other[3 * rows, :piece]

    def by_side(own, other, axis):
        return jnp.where(
            side == 0,
            jnp.concatenate([own, other], axis=axis),
            jnp.concatenate([other, own], axis=axis),
        )

    def query_parts(block):
        pairs = jnp.stack([block[:rows], block[rows : 2 * rows]], axis=1)
        return unpair_columns(pairs, head_dim)

    grad_query = by_side(query_parts(attn_own), query_parts(attn_other), 3).reshape(rows, 4 * width)
    kv_own, kv_other = attn_own[2 * rows : 3 * rows], attn_other[2 * rows : 3 * rows]
    grad_key = by_side(kv_own[:, :half], kv_other[:, :half], 1)
    grad_value = by_side(kv_own[:, half:], kv_other[:, half:], 1)
    return grad_query, grad_key, grad_value, vec_total


def on_device(
    tokens,
    kinds,
    groups,
    query_weight,
    query_bias,
    key_weight,
    key_bias,
    value_weight,
    value_bias,
    output_weight,
    output_bias,
    norm1_gain,
    norm1_shift,
    up_weight,
    up_bias,
    down_weight,
    down_bias,
    norm2_gain,
    norm2_shift,
    cotangent,
):
    micro, _, local, width = tokens.shape
    half = width // 2
    head_dim = width // HEADS
    devices = lax.axis_size("shard")
    rows = width // devices
    side = lax.axis_index("seq").astype(jnp.int32)
    per = local // BLOCK

    vectors = (
        query_bias,
        key_bias,
        value_bias,
        output_bias,
        norm1_gain,
        norm1_shift,
        up_bias,
        down_bias,
        norm2_gain,
        norm2_shift,
    )
    piece = 16 * rows
    direct = devices == GROUPS
    attn_sizes = (rows, rows, rows)
    feed_sizes = (4 * rows,) + (rows,) * 5
    if not direct:
        vector_row = jnp.pad(jnp.concatenate(vectors), (0, width - piece))[None]
        packed = pack_attention(query_weight, key_weight, value_weight, vector_row, side, head_dim)
        attn_gathered = lax.all_gather(packed[None], "shard", axis=0, tiled=True)
        other_tokens, other_kinds, other_groups = swap(tokens), swap(kinds), swap(groups)
    feed_local = pack_feed(down_weight, output_weight, up_weight)
    feed_gathered = lax.all_gather(feed_local[None], "shard", axis=0, tiled=True)
    if direct:
        attn_gathered, other_tokens, other_kinds, other_groups = gather_attention(
            query_weight, key_weight, value_weight, vectors, tokens, kinds, groups
        )
    vectors = attn_gathered[:, 3 * rows, :piece]
    if direct:
        attn_w, feed_w = attn_gathered, feed_gathered
    else:
        attn_w = regroup(attn_gathered, attn_sizes)
        feed_w = regroup(feed_gathered, feed_sizes)

    def whole_vector(start, size):
        return vectors[:, start : start + size].reshape(-1).astype(f32)

    full_query_bias = whole_vector(0, 4 * rows)
    full_key_bias = whole_vector(4 * rows, rows)
    full_value_bias = whole_vector(5 * rows, rows)
    bias_rows = jnp.concatenate(
        [
            pair_columns(full_query_bias, side, head_dim),
            jnp.concatenate([own_half(full_key_bias, side), own_half(full_value_bias, side)])[None],
        ],
        axis=0,
    )
    full_up_bias = whole_vector(9 * rows, 4 * rows).reshape(4, width)
    chain_vectors = jnp.concatenate(
        [
            whole_vector(6 * rows, rows)[None],
            whole_vector(7 * rows, rows)[None],
            whole_vector(8 * rows, rows)[None],
            full_up_bias,
            whole_vector(13 * rows, rows)[None],
            whole_vector(14 * rows, rows)[None],
            whole_vector(15 * rows, rows)[None],
        ],
        axis=0,
    )

    own_tokens = tokens[:, 0]
    xs = jnp.stack([own_tokens, other_tokens[:, 0]])
    kind_all = jnp.stack([kinds[:, 0], other_kinds[:, 0]])
    group_all = jnp.stack([groups[:, 0], other_groups[:, 0]])
    kind_col = kind_all[..., None]
    gk = group_all[..., None]
    gq = group_all[:, :, None, :]
    by_block = group_all.reshape(2, micro, per, BLOCK)
    low = jnp.swapaxes(by_block[..., 0], 0, 1).reshape(-1)
    high = jnp.swapaxes(by_block[..., BLOCK - 1], 0, 1).reshape(-1)

    qp, km, kmt, v, vt = project(xs, attn_w, bias_rows, kind_col)
    c, ct, lse = attend(low, high, qp, km, vt, gk, gq)
    c_other = swap(c[1])
    flat = micro * local
    mixed, dh1, left, right, dc_own, dc_other, sums = chain(
        side,
        own_tokens.reshape(flat, width),
        c[0].reshape(flat, half),
        c_other.reshape(flat, half),
        cotangent.reshape(flat, width),
        feed_w,
        chain_vectors,
    )

    dc_swapped = swap(dc_other)
    feed_part = feed_grad(left, right)
    dc_swapped, feed_part = lax.optimization_barrier((dc_swapped, feed_part))
    dc = jnp.stack([dc_own, dc_swapped]).reshape(2, micro, local, half)
    if devices != GROUPS:
        feed_part = ungroup(feed_part, feed_sizes, devices)
    feed_sum = lax.psum_scatter(feed_part, "shard", scatter_dimension=0, tiled=True)[0]
    d, db = attend_back(low, high, qp, km, kmt, v, dc, ct, lse, gk, gq, kind_col)

    query_own = unpair_columns(db[0, : 2 * width].reshape(2, width), head_dim)
    zero = jnp.zeros((half,), f32)

    def spread(own):
        return jnp.where(side == 0, jnp.concatenate([own, zero]), jnp.concatenate([zero, own]))

    query_spread = jnp.concatenate([spread(query_own[e, w]) for e in range(2) for w in range(2)])
    key_spread = spread(db[0, 2 * width : 2 * width + half])
    value_spread = spread(db[0, 2 * width + half :])
    grad_vectors = jnp.concatenate(
        [
            query_spread.reshape(devices, 4 * rows),
            key_spread.reshape(devices, rows),
            value_spread.reshape(devices, rows),
            sums[5].reshape(devices, rows),
            sums[3].reshape(devices, rows),
            sums[4].reshape(devices, rows),
            sums[8:12].reshape(devices, 4 * rows),
            sums[2].reshape(devices, rows),
            sums[0].reshape(devices, rows),
            sums[1].reshape(devices, rows),
        ],
        axis=1,
    ).astype(bf16)
    grad_vectors = jnp.pad(grad_vectors[:, None, :], ((0, 0), (0, 15), (0, width - piece)))
    dx_other = input_grad_part(d, attn_w, 1, bf16)
    flat_x = xs.reshape(2 * flat, width)
    flat_d = d.reshape(2 * flat, 3 * width)
    if direct:
        grad_query, grad_key, grad_value, vec_rows = scatter_attention(flat_x, flat_d, grad_vectors)
        vec_total = vec_rows[0, :piece]
    else:
        zeros = jnp.zeros((GROUPS, 16, width), bf16)
        attn_part = attn_grad(flat_x, flat_d, zeros)
        attn_part = jnp.concatenate(
            [ungroup(attn_part[:, : 3 * (width // GROUPS)], attn_sizes, devices), grad_vectors], axis=1
        )
        attn_sum = lax.psum_scatter(attn_part, "shard", scatter_dimension=0, tiled=True)[0]
        attn_other = swap(attn_sum)
        grad_query, grad_key, grad_value, vec_total = assemble(
            attn_sum, attn_other, side, head_dim, rows, piece
        )
    dx_own = input_grad_part(d, attn_w, 0, f32)
    input_grad = dh1.reshape(micro, local, width) + dx_own + swap(dx_other).astype(f32)

    feed_total = feed_sum.astype(f32) + swap(feed_sum).astype(f32)
    grad_down = feed_total[: 4 * rows]
    grad_output = feed_total[4 * rows : 5 * rows]
    grad_up = jnp.concatenate(
        [feed_total[(5 + j) * rows : (6 + j) * rows] for j in range(4)], axis=1
    )

    def piece_of(start, size):
        return vec_total[start : start + size]

    return (
        mixed.reshape(micro, 1, local, width),
        input_grad[:, None],
        grad_query,
        piece_of(0, 4 * rows),
        grad_key,
        piece_of(4 * rows, rows),
        grad_value,
        piece_of(5 * rows, rows),
        grad_output,
        piece_of(6 * rows, rows),
        piece_of(7 * rows, rows),
        piece_of(8 * rows, rows),
        grad_up,
        piece_of(9 * rows, 4 * rows),
        grad_down,
        piece_of(13 * rows, rows),
        piece_of(14 * rows, rows),
        piece_of(15 * rows, rows),
    )


def solution(mesh):
    weight = P("shard", None)
    vector = P("shard")
    tokens = P(None, "shard", "seq", None)
    marks = P(None, "shard", "seq")
    return jax.shard_map(
        on_device,
        mesh=mesh,
        in_specs=(tokens, marks, marks)
        + (weight, vector) * 4
        + (vector, vector)
        + (weight, vector) * 2
        + (vector, vector)
        + (tokens,),
        out_specs=(tokens, tokens)
        + (weight, vector) * 4
        + (vector, vector)
        + (weight, vector) * 2
        + (vector, vector),
        check_vma=False,
    )
```

```python
import jax
import jax.numpy as jnp
from jax import lax
from jax.experimental import pallas as pl
from jax.experimental.pallas import tpu as pltpu
from jax.sharding import PartitionSpec as P


HEADS = 12
GROUPS = 16
BLOCK = 256
masked_score = -1e30
layer_eps = 1e-12
bf16 = jnp.bfloat16
f32 = jnp.float32
VMEM_LIMIT = 60 * 1024 * 1024


def nn(a, b):
    return lax.dot_general(a, b, (((1,), (0,)), ((), ())), preferred_element_type=f32)


def nt(a, b):
    return lax.dot_general(a, b, (((1,), (1,)), ((), ())), preferred_element_type=f32)


def tn(a, b):
    return lax.dot_general(a, b, (((0,), (0,)), ((), ())), preferred_element_type=f32)


def swap(value):
    return lax.ppermute(value, "seq", [(0, 1), (1, 0)])


def cost(flops, moved, trans=0):
    return pl.CostEstimate(flops=flops, bytes_accessed=moved, transcendentals=trans)


def low_lanes(shape):
    return lax.broadcasted_iota(jnp.int32, shape, len(shape) - 1) % 128 < 64


def pack_into(first, q_ref, k_ref, v_ref, vec, out_ref):
    rows, width = k_ref.shape
    half = width // 2

    def own(ref, base):
        return jnp.where(
            first,
            ref[:, base : base + half].astype(f32),
            ref[:, base + half : base + width].astype(f32),
        )

    lo = low_lanes((rows, 128))
    for e in range(2):
        word = own(q_ref, 2 * e * width)
        entity = own(q_ref, (2 * e + 1) * width)
        for t in range(half // 128):
            a = word[:, 128 * t : 128 * t + 128]
            b = entity[:, 128 * t : 128 * t + 128]
            even = jnp.where(lo, a, pltpu.roll(b, 64, 1))
            odd = jnp.where(lo, pltpu.roll(a, 64, 1), b)
            out_ref[e * rows : e * rows + rows, 256 * t : 256 * t + 128] = even.astype(bf16)
            out_ref[e * rows : e * rows + rows, 256 * t + 128 : 256 * t + 256] = odd.astype(bf16)
    out_ref[2 * rows : 3 * rows, :half] = own(k_ref, 0).astype(bf16)
    out_ref[2 * rows : 3 * rows, half:] = own(v_ref, 0).astype(bf16)
    out_ref[3 * rows :, :] = jnp.broadcast_to(vec, (16, width)).astype(bf16)


def spots():
    x = lax.axis_index("seq")
    me = lax.axis_index("shard")
    core = lax.rem(me, 2)
    y = lax.rem(me // 2, 2)
    z = me // 4
    return x, me, z, y, core


def slot_of(z, y, core):
    return z * 4 + y * 2 + core


def greet(peers):
    barrier = pltpu.get_barrier_semaphore()
    for peer in peers:
        pl.semaphore_signal(barrier, inc=1, device_id=peer, device_id_type=pl.DeviceIdType.MESH)
    pl.semaphore_wait(barrier, len(peers))


def all_peers():
    x, me, z, y, core = spots()
    peers = [(x, slot_of(z, y, 1 - core)), (x, slot_of(z, 1 - y, core)), (1 - x, me)]
    for step in range(1, 4):
        peers.append((x, slot_of(lax.rem(z + step, 4), y, core)))
    return peers


def send(src, dst, send_sem, recv_sem, device):
    return pltpu.make_async_remote_copy(
        src_ref=src,
        dst_ref=dst,
        send_sem=send_sem,
        recv_sem=recv_sem,
        device_id=device,
        device_id_type=pl.DeviceIdType.MESH,
    )


def gather_kernel(*refs):
    q_ref, k_ref, v_ref = refs[:3]
    vec_refs = refs[3:13]
    tok_ref, kinds_ref, groups_ref = refs[13:16]
    w_ref, tok_out, kinds_out, groups_out = refs[16:20]
    mine, keep_sem, x_send, x_recv, z_send, z_recv, y_send, y_recv, c_send, c_recv = refs[20:]
    x, me, z, y, core = spots()
    across = (1 - x, me)
    beside = (x, slot_of(z, 1 - y, core))
    partner = (x, slot_of(z, y, 1 - core))
    greet(all_peers())
    over = [
        send(src, dst, x_send.at[i], x_recv.at[i], across)
        for i, (src, dst) in enumerate(
            ((kinds_ref, kinds_out), (groups_ref, groups_out), (tok_ref, tok_out))
        )
    ]
    for copy in over:
        copy.start()
    vec = jnp.concatenate([r[...].astype(f32) for r in vec_refs], axis=1)
    pack_into(x == 0, q_ref, k_ref, v_ref, vec, mine)
    started = []
    for step in range(1, 4):
        copy = send(
            mine,
            w_ref.at[me],
            z_send.at[step - 1],
            z_recv.at[z],
            (x, slot_of(lax.rem(z + step, 4), y, core)),
        )
        copy.start()
        started.append(copy)
    copy = send(mine, w_ref.at[me], y_send.at[z], y_recv.at[z], beside)
    copy.start()
    started.append(copy)
    copy = send(mine, w_ref.at[me], c_send.at[z * 2 + y], c_recv.at[z * 2 + y], partner)
    copy.start()
    started.append(copy)
    keep = pltpu.make_async_copy(mine, w_ref.at[me], keep_sem)
    keep.start()
    for step in range(1, 4):
        zz = lax.rem(z + step, 4)
        at = slot_of(zz, y, core)
        held = w_ref.at[at]
        send(held, held, z_send.at[0], z_recv.at[zz], partner).wait_recv()
        for copy in (
            send(held, held, y_send.at[zz], y_recv.at[zz], beside),
            send(held, held, c_send.at[zz * 2 + y], c_recv.at[zz * 2 + y], partner),
        ):
            copy.start()
            started.append(copy)
    for step in range(4):
        zz = lax.rem(z + step, 4)
        rail = zz * 2 + 1 - y
        held = w_ref.at[slot_of(zz, 1 - y, core)]
        send(held, held, y_send.at[0], y_recv.at[zz], partner).wait_recv()
        copy = send(held, held, c_send.at[rail], c_recv.at[rail], partner)
        copy.start()
        started.append(copy)
    for rail in range(8):
        held = w_ref.at[2 * rail + 1 - core]
        send(held, held, c_send.at[0], c_recv.at[rail], partner).wait_recv()
    keep.wait()
    for copy in started:
        copy.wait_send()
    for copy in over:
        copy.wait()


def gather_attention(query_weight, key_weight, value_weight, vectors, tokens, kinds, groups):
    rows, width = key_weight.shape
    vmem = pl.BlockSpec(memory_space=pltpu.VMEM)
    anywhere = pl.BlockSpec(memory_space=pl.ANY)
    sem = pltpu.SemaphoreType.DMA
    return pl.pallas_call(
        gather_kernel,
        in_specs=[vmem] * 13 + [anywhere] * 3,
        out_specs=[anywhere] * 4,
        out_shape=[
            jax.ShapeDtypeStruct((GROUPS, 3 * rows + 16, width), bf16),
            jax.ShapeDtypeStruct(tokens.shape, tokens.dtype),
            jax.ShapeDtypeStruct(kinds.shape, kinds.dtype),
            jax.ShapeDtypeStruct(groups.shape, groups.dtype),
        ],
        scratch_shapes=[
            pltpu.VMEM((3 * rows + 16, width), bf16),
            sem,
            sem((3,)),
            sem((3,)),
            sem((3,)),
            sem((4,)),
            sem((4,)),
            sem((4,)),
            sem((8,)),
            sem((8,)),
        ],
        compiler_params=pltpu.CompilerParams(
            collective_id=0, has_side_effects=True, vmem_limit_bytes=VMEM_LIMIT
        ),
        name="gather",
    )(query_weight, key_weight, value_weight, *[v[None] for v in vectors], tokens, kinds, groups)


def pair_columns(columns, side, head_dim):
    lead = columns.shape[:-1]
    per = columns.shape[-1] // (8 * head_dim)
    view = columns.reshape(lead + (2, 2, 2, per, head_dim))
    view = jnp.where(side == 0, view[..., 0, :, :], view[..., 1, :, :])
    return jnp.swapaxes(view, -3, -2).reshape(lead + (2, -1))


def unpair_columns(pairs, head_dim):
    lead = pairs.shape[:-2]
    per = pairs.shape[-1] // (2 * head_dim)
    view = pairs.reshape(lead + (2, per, 2, head_dim))
    return jnp.swapaxes(view, -3, -2).reshape(lead + (2, 2, per * head_dim))


def own_half(columns, side):
    half = columns.shape[-1] // 2
    return jnp.where(side == 0, columns[..., :half], columns[..., half:])


def pack_attention(query_weight, key_weight, value_weight, vector, side, head_dim):
    width = key_weight.shape[1]
    pairs = pair_columns(query_weight, side, head_dim)
    key_value = jnp.concatenate([own_half(key_weight, side), own_half(value_weight, side)], axis=1)
    return jnp.concatenate(
        [pairs[:, 0], pairs[:, 1], key_value, jnp.broadcast_to(vector, (16, width))], axis=0
    )


def pack_feed_kernel(down_ref, output_ref, up_ref, out_ref):
    rows, width = output_ref.shape
    out_ref[0 : 4 * rows, :] = down_ref[...]
    out_ref[4 * rows : 5 * rows, :] = output_ref[...]
    for j in range(4):
        out_ref[(5 + j) * rows : (6 + j) * rows, :] = up_ref[:, j * width : j * width + width]


def pack_feed(down_weight, output_weight, up_weight):
    rows, width = output_weight.shape
    if rows % 16:
        return jnp.concatenate(
            [down_weight, output_weight]
            + [up_weight[:, j * width : j * width + width] for j in range(4)],
            axis=0,
        )
    vmem = pl.BlockSpec(memory_space=pltpu.VMEM)
    return pl.pallas_call(
        pack_feed_kernel,
        in_specs=[vmem] * 3,
        out_specs=vmem,
        out_shape=jax.ShapeDtypeStruct((9 * rows, width), bf16),
        name="pack_feed",
    )(down_weight, output_weight, up_weight)


def regroup(gathered, sizes):
    _, _, width = gathered.shape
    pieces = []
    start = 0
    for size in sizes:
        piece = gathered[:, start : start + size].reshape(GROUPS, -1, width)
        pieces.append(piece)
        start += size
    return jnp.concatenate(pieces, axis=1)


def ungroup(grouped, sizes, devices):
    _, _, width = grouped.shape
    pieces = []
    start = 0
    for size in sizes:
        wide = size * devices // GROUPS
        pieces.append(grouped[:, start : start + wide].reshape(devices, size, width))
        start += wide
    return jnp.concatenate(pieces, axis=1)


def project_kernel(
    own_ref,
    other_ref,
    own_kind_ref,
    other_kind_ref,
    own_group_ref,
    other_group_ref,
    w_ref,
    bias_ref,
    qp_ref,
    km_ref,
    kmt_ref,
    v_ref,
    vt_ref,
    xs_ref,
    kind_ref,
    gk_ref,
    gq_ref,
):
    width = own_ref.shape[1]
    half = width // 2
    rows = width // GROUPS
    mine = pl.program_id(0) == 0

    def column(row):
        return jnp.broadcast_to(row.astype(f32), (128, BLOCK)).T.astype(jnp.int32)

    x = jnp.where(mine, own_ref[...].astype(f32), other_ref[...].astype(f32)).astype(bf16)
    group = jnp.where(mine, own_group_ref[...], other_group_ref[...])
    kinds = column(jnp.where(mine, own_kind_ref[...], other_kind_ref[...]))
    kind = kinds[:, 0:1]
    xs_ref[...] = x
    kind_ref[...] = kind
    gk_ref[...] = column(group)[:, 0:1]
    gq_ref[...] = group
    wa = w_ref[:, 0:rows, :].reshape(width, width)
    wb = w_ref[:, rows : 2 * rows, :].reshape(width, width)
    wkv = w_ref[:, 2 * rows : 3 * rows, :].reshape(width, width)
    qa = nn(x, wa) + bias_ref[0:1, :]
    qb = nn(x, wb) + bias_ref[1:2, :]
    qp_ref[...] = (jnp.where(kind == 1, qb, qa) * 0.125).astype(bf16)
    kv = nn(x, wkv) + bias_ref[2:3, :]
    lane_high = (lax.broadcasted_iota(jnp.int32, (BLOCK, 128), 1) >= 64).astype(jnp.int32)
    keep = lane_high == kinds
    lo = lane_high == 0
    for t in range(half // 128):
        k = kv[:, 128 * t : 128 * t + 128]
        r = pltpu.roll(k, 64, 1)
        even = jnp.where(keep, jnp.where(lo, k, r), 0.0)
        odd = jnp.where(keep, jnp.where(lo, r, k), 0.0)
        km_ref[:, 256 * t : 256 * t + 128] = even.astype(bf16)
        km_ref[:, 256 * t + 128 : 256 * t + 256] = odd.astype(bf16)
        kmt_ref[256 * t : 256 * t + 128, :] = even.T.astype(bf16)
        kmt_ref[256 * t + 128 : 256 * t + 256, :] = odd.T.astype(bf16)
    v = kv[:, half:]
    v_ref[...] = v.astype(bf16)
    vt_ref[...] = v.T.astype(bf16)


def project(tokens, other_tokens, kinds, other_kinds, groups, other_groups, weights, bias_rows):
    micro, _, local, width = tokens.shape
    halves = 2
    half = width // 2
    sub = local // BLOCK

    def rows_spec(cols):
        return pl.BlockSpec((None, None, BLOCK, cols), lambda a, m, i: (a, m, i, 0))

    def cols_spec(count):
        return pl.BlockSpec((None, None, count, BLOCK), lambda a, m, i: (a, m, 0, i))

    def shape(*dims, kind=bf16):
        return jax.ShapeDtypeStruct((halves, micro) + dims, kind)

    def pick(own, a, index, stop):
        return jnp.where(a == 0, index, stop) if own else jnp.where(a == 0, 0, index)

    def token_spec(own):
        return pl.BlockSpec(
            (None, None, BLOCK, width),
            lambda a, m, i: (pick(own, a, m, micro - 1), 0, pick(own, a, i, sub - 1), 0),
        )

    def mark_spec(own):
        return pl.BlockSpec(
            (None, 1, BLOCK),
            lambda a, m, i: (pick(own, a, m, micro - 1), 0, pick(own, a, i, sub - 1)),
        )

    count = halves * micro * local
    return pl.pallas_call(
        project_kernel,
        grid=(halves, micro, sub),
        in_specs=[
            token_spec(True),
            token_spec(False),
            mark_spec(True),
            mark_spec(False),
            mark_spec(True),
            mark_spec(False),
            pl.BlockSpec(weights.shape, lambda a, m, i: (0, 0, 0)),
            pl.BlockSpec(bias_rows.shape, lambda a, m, i: (0, 0)),
        ],
        out_specs=[
            rows_spec(width),
            rows_spec(width),
            cols_spec(width),
            rows_spec(half),
            cols_spec(half),
            rows_spec(width),
            rows_spec(1),
            rows_spec(1),
            cols_spec(1),
        ],
        out_shape=[
            shape(local, width),
            shape(local, width),
            shape(width, local),
            shape(local, half),
            shape(half, local),
            shape(local, width),
            shape(local, 1, kind=jnp.int32),
            shape(local, 1, kind=jnp.int32),
            shape(1, local, kind=jnp.int32),
        ],
        compiler_params=pltpu.CompilerParams(vmem_limit_bytes=VMEM_LIMIT),
        cost_estimate=cost(2 * count * width * 3 * width, count * width * 10),
        name="project",
    )(tokens, other_tokens, kinds, other_kinds, groups, other_groups, weights, bias_rows)


def place(block, per):
    return block // per, pl.multiple_of(lax.rem(block, per) * BLOCK, BLOCK)


def ends_of(own_ref, other_ref, micro_at, block, per):
    at = lax.rem(block, per) * BLOCK
    mine = block < per
    first = jnp.where(mine, own_ref[micro_at, at], other_ref[micro_at, at])
    last_at = at + BLOCK - 1
    return first, jnp.where(mine, own_ref[micro_at, last_at], other_ref[micro_at, last_at])


def attend_kernel(
    own_ref, other_ref, qp_ref, km_ref, vt_ref, gk_ref, gq_ref, c_ref, ct_ref, lse_ref, m_sc, l_sc, acc_sc
):
    micro_at = pl.program_id(0)
    local = qp_ref.shape[1]
    per = local // BLOCK
    blocks = 2 * per
    heads = qp_ref.shape[2] // 128

    @pl.loop(0, blocks)
    def _(qb):
        qh, qo = place(qb, per)
        m_sc[...] = jnp.full_like(m_sc, masked_score)
        l_sc[...] = jnp.zeros_like(l_sc)
        acc_sc[...] = jnp.zeros_like(acc_sc)
        q_low, q_high = ends_of(own_ref, other_ref, micro_at, qb, per)

        @pl.loop(0, blocks)
        def _(kb):
            k_low, k_high = ends_of(own_ref, other_ref, micro_at, kb, per)

            @pl.when((q_low <= k_high) & (k_low <= q_high))
            def _():
                kh, ko = place(kb, per)
                same = gk_ref[kh, pl.ds(ko, BLOCK), :] == gq_ref[qh, :, pl.ds(qo, BLOCK)]
                bias = jnp.where(same, 0.0, masked_score)
                for h in range(heads):
                    at = slice(128 * h, 128 * h + 128)
                    vat = slice(64 * h, 64 * h + 64)
                    s = nt(km_ref[kh, pl.ds(ko, BLOCK), at], qp_ref[qh, pl.ds(qo, BLOCK), at]) + bias
                    m_old = m_sc[h : h + 1, :]
                    m_new = jnp.maximum(m_old, jnp.max(s, axis=0, keepdims=True))
                    alpha = jnp.exp(m_old - m_new)
                    p = jnp.exp(s - m_new)
                    m_sc[h : h + 1, :] = m_new
                    l_sc[h : h + 1, :] = alpha * l_sc[h : h + 1, :] + jnp.sum(p, axis=0, keepdims=True)
                    acc_sc[vat, :] = alpha * acc_sc[vat, :] + nn(
                        vt_ref[kh, vat, pl.ds(ko, BLOCK)], p.astype(bf16)
                    )

        cols = pl.ds(pl.multiple_of(qb * BLOCK, BLOCK), BLOCK)
        for h in range(heads):
            vat = slice(64 * h, 64 * h + 64)
            total = l_sc[h : h + 1, :]
            ct_ref[vat, cols] = acc_sc[vat, :] / total
            lse_ref[h : h + 1, cols] = m_sc[h : h + 1, :] + jnp.log(total)
        c_ref[qh, pl.ds(qo, BLOCK), :] = ct_ref[:, cols].T.astype(bf16)


def whole_micro(array):
    rest = array.shape[2:]
    return pl.BlockSpec((array.shape[0], None) + rest, lambda m, *_: (0, m) + (0,) * len(rest))


def attend(own_groups, other_groups, qp, km, vt, gk, gq):
    halves, micro, local, width = qp.shape
    half = width // 2
    heads = width // 128
    length = halves * local
    return pl.pallas_call(
        attend_kernel,
        grid_spec=pltpu.PrefetchScalarGridSpec(
            num_scalar_prefetch=2,
            grid=(micro,),
            in_specs=[whole_micro(a) for a in (qp, km, vt, gk, gq)],
            out_specs=[
                pl.BlockSpec((halves, None, local, half), lambda m, *_: (0, m, 0, 0)),
                pl.BlockSpec((None, half, length), lambda m, *_: (m, 0, 0)),
                pl.BlockSpec((None, 8, length), lambda m, *_: (m, 0, 0)),
            ],
            scratch_shapes=[
                pltpu.VMEM((8, BLOCK), f32),
                pltpu.VMEM((8, BLOCK), f32),
                pltpu.VMEM((half, BLOCK), f32),
            ],
        ),
        out_shape=[
            jax.ShapeDtypeStruct((halves, micro, local, half), bf16),
            jax.ShapeDtypeStruct((micro, half, length), f32),
            jax.ShapeDtypeStruct((micro, 8, length), f32),
        ],
        compiler_params=pltpu.CompilerParams(vmem_limit_bytes=VMEM_LIMIT),
        cost_estimate=cost(
            micro * heads * length * length * 512, micro * length * width * 8, micro * heads * length * length
        ),
        name="attend",
    )(own_groups, other_groups, qp, km, vt, gk, gq)


def attend_back_kernel(
    own_ref,
    other_ref,
    qp_ref,
    km_ref,
    kmt_ref,
    v_ref,
    dc_ref,
    ct_ref,
    lse_ref,
    gk_ref,
    gq_ref,
    kind_ref,
    d_ref,
    db_ref,
    dqt_sc,
    dk_sc,
    dv_sc,
    delta_sc,
):
    micro_at = pl.program_id(0)
    local, width = qp_ref.shape[1], qp_ref.shape[2]
    half = width // 2
    per = local // BLOCK
    blocks = 2 * per
    tiles = half // 128
    dk_sc[...] = jnp.zeros_like(dk_sc)
    dv_sc[...] = jnp.zeros_like(dv_sc)

    @pl.when(micro_at == 0)
    def _():
        db_ref[...] = jnp.zeros_like(db_ref)

    lo = low_lanes((BLOCK, 128))

    @pl.loop(0, blocks)
    def _(qb):
        qh, qo = place(qb, per)
        qrows = pl.ds(qo, BLOCK)
        cols = pl.ds(pl.multiple_of(qb * BLOCK, BLOCK), BLOCK)
        dct = dc_ref[qh, qrows, :].astype(f32).T
        inner = dct * ct_ref[:, cols]
        for h in range(2 * tiles):
            delta_sc[h : h + 1, :] = jnp.sum(inner[64 * h : 64 * h + 64, :], axis=0, keepdims=True)
        dqt_sc[...] = jnp.zeros_like(dqt_sc)
        q_low, q_high = ends_of(own_ref, other_ref, micro_at, qb, per)

        @pl.loop(0, blocks)
        def _(kb):
            k_low, k_high = ends_of(own_ref, other_ref, micro_at, kb, per)

            @pl.when((q_low <= k_high) & (k_low <= q_high))
            def _():
                kh, ko = place(kb, per)
                krows = pl.ds(ko, BLOCK)
                drows = pl.ds(pl.multiple_of(kb * BLOCK, BLOCK), BLOCK)
                same = gk_ref[kh, krows, :] == gq_ref[qh, :, qrows]
                bias = jnp.where(same, 0.0, masked_score)
                for t in range(tiles):
                    tat = slice(128 * t, 128 * t + 128)
                    v = v_ref[kh, krows, tat]
                    dc = dc_ref[qh, qrows, tat]
                    from_pair = []
                    for side in range(2):
                        h = 2 * t + side
                        at = slice(128 * h, 128 * h + 128)
                        q = qp_ref[qh, qrows, at]
                        s = nt(km_ref[kh, krows, at], q) + bias
                        p = jnp.exp(s - lse_ref[h : h + 1, cols])
                        zero = jnp.zeros_like(v)
                        vm = jnp.where(lo, v, zero) if side == 0 else jnp.where(lo, zero, v)
                        dp = nt(vm, dc)
                        ds = (p * (dp - delta_sc[h : h + 1, :])).astype(bf16)
                        dk_sc[drows, at] += nn(ds, q)
                        dqt_sc[at, :] += nn(kmt_ref[kh, at, krows], ds)
                        from_pair.append(nn(p.astype(bf16), dc))
                    dv_sc[drows, tat] += jnp.where(lo, from_pair[0], from_pair[1])

        dq = dqt_sc[...].T * 0.125
        entity = kind_ref[qh, qrows, :] == 1
        d_ref[qh, qrows, 0:width] = jnp.where(entity, 0.0, dq).astype(bf16)
        d_ref[qh, qrows, width : 2 * width] = jnp.where(entity, dq, 0.0).astype(bf16)

    @pl.loop(0, blocks)
    def _(kb):
        kh, ko = place(kb, per)
        krows = pl.ds(ko, BLOCK)
        drows = pl.ds(pl.multiple_of(kb * BLOCK, BLOCK), BLOCK)
        entity = kind_ref[kh, krows, :] == 1
        for t in range(tiles):
            even = dk_sc[drows, 256 * t : 256 * t + 128]
            odd = dk_sc[drows, 256 * t + 128 : 256 * t + 256]
            left = jnp.where(entity, pltpu.roll(even, 64, 1), even)
            right = jnp.where(entity, odd, pltpu.roll(odd, 64, 1))
            d_ref[kh, krows, 2 * width + 128 * t : 2 * width + 128 * t + 128] = jnp.where(
                lo, left, right
            ).astype(bf16)
        d_ref[kh, krows, 2 * width + half : 3 * width] = dv_sc[drows, :].astype(bf16)
        db_ref[0:1, :] += jnp.sum(d_ref[kh, krows, :].astype(f32), axis=0, keepdims=True)


def attend_back(own_groups, other_groups, qp, km, kmt, v, dc, ct, lse, gk, gq, kind_col):
    halves, micro, local, width = qp.shape
    half = width // 2
    heads = width // 128
    length = halves * local
    return pl.pallas_call(
        attend_back_kernel,
        grid_spec=pltpu.PrefetchScalarGridSpec(
            num_scalar_prefetch=2,
            grid=(micro,),
            in_specs=[whole_micro(a) for a in (qp, km, kmt, v, dc)]
            + [
                pl.BlockSpec((None, half, length), lambda m, *_: (m, 0, 0)),
                pl.BlockSpec((None, 8, length), lambda m, *_: (m, 0, 0)),
            ]
            + [whole_micro(a) for a in (gk, gq, kind_col)],
            out_specs=[
                pl.BlockSpec((halves, None, local, 3 * width), lambda m, *_: (0, m, 0, 0)),
                pl.BlockSpec((8, 3 * width), lambda m, *_: (0, 0)),
            ],
            scratch_shapes=[
                pltpu.VMEM((width, BLOCK), f32),
                pltpu.VMEM((length, width), f32),
                pltpu.VMEM((length, half), f32),
                pltpu.VMEM((8, BLOCK), f32),
            ],
        ),
        out_shape=[
            jax.ShapeDtypeStruct((halves, micro, local, 3 * width), bf16),
            jax.ShapeDtypeStruct((8, 3 * width), f32),
        ],
        compiler_params=pltpu.CompilerParams(vmem_limit_bytes=VMEM_LIMIT),
        cost_estimate=cost(
            micro * heads * length * length * 1280, micro * length * width * 16, micro * heads * length * length
        ),
        name="attend_back",
    )(own_groups, other_groups, qp, km, kmt, v, dc, ct, lse, gk, gq, kind_col)


def norm_forward(hidden):
    center = hidden - jnp.mean(hidden, axis=-1, keepdims=True)
    rescale = lax.rsqrt(jnp.mean(center * center, axis=-1, keepdims=True) + layer_eps)
    return center * rescale, rescale


def norm_backward(upstream, normed, rescale, gain):
    scaled = upstream * gain
    return rescale * (
        scaled
        - jnp.mean(scaled, axis=-1, keepdims=True)
        - normed * jnp.mean(scaled * normed, axis=-1, keepdims=True)
    )


def column_sum(values):
    return jnp.sum(values.astype(f32), axis=0, keepdims=True)


def chain_kernel(
    side_ref,
    x_ref,
    own_ref,
    other_ref,
    cot_ref,
    w_ref,
    vec_ref,
    mixed_ref,
    dh_ref,
    left_ref,
    right_ref,
    dco_ref,
    dcx_ref,
    sums_ref,
    slope_sc,
    z_sc,
):
    width = x_ref.shape[1]
    half = width // 2
    rows = width // GROUPS
    chunks = 4
    first = side_ref[0] == 0

    @pl.when(pl.program_id(0) == 0)
    def _():
        sums_ref[...] = jnp.zeros_like(sums_ref)

    def vector(at):
        return vec_ref[at : at + 1, :]

    def up_chunk(j):
        at = pl.multiple_of(5 * rows + j * rows, 16)
        return w_ref[:, pl.ds(at, rows), :].reshape(width, width)

    def down_chunk(j):
        return w_ref[pl.ds(j * (GROUPS // chunks), GROUPS // chunks), 0 : 4 * rows, :].reshape(width, width)

    def out_weight():
        return w_ref[:, 4 * rows : 5 * rows, :].reshape(width, width)

    own = own_ref[...].astype(f32)
    other = other_ref[...].astype(f32)
    context = jnp.concatenate(
        [jnp.where(first, own, other), jnp.where(first, other, own)], axis=1
    ).astype(bf16)
    left_ref[:, 0:width] = context
    hidden = x_ref[...].astype(f32) + (nn(context, out_weight()) + vector(0))
    n1, r1 = norm_forward(hidden)
    y1 = n1 * vector(1) + vector(2)
    left_ref[:, width : 2 * width] = y1.astype(bf16)
    z_sc[...] = y1 + vector(7)

    @pl.loop(0, chunks)
    def _(j):
        u = nn(left_ref[:, width : 2 * width], up_chunk(j)) + vec_ref[pl.ds(j + 3, 1), :]
        cumulative = 0.5 * (1.0 + lax.erf(u * 0.7071067811865476))
        at = pl.multiple_of(j * width, 128)
        slope_sc[:, pl.ds(at, width)] = (
            cumulative + u * jnp.exp(-0.5 * u * u) * 0.3989422804014327
        )
        g = (u * cumulative).astype(bf16)
        left_ref[:, pl.ds(pl.multiple_of(at + 2 * width, 128), width)] = g
        z_sc[...] += nn(g, down_chunk(j))

    n2, r2 = norm_forward(z_sc[...])
    mixed_ref[...] = (n2 * vector(8) + vector(9)).astype(bf16)
    upstream = cot_ref[...].astype(f32)
    sums_ref[0:1, :] += column_sum(upstream * n2)
    sums_ref[1:2, :] += column_sum(upstream)
    dh2 = norm_backward(upstream, n2, r2, vector(8))
    dz = dh2.astype(bf16)
    right_ref[:, 5 * width :] = dz
    sums_ref[2:3, :] += column_sum(dz)
    z_sc[...] = dh2

    @pl.loop(0, chunks)
    def _(j):
        at = pl.multiple_of(j * width, 128)
        du = (
            nt(right_ref[:, 5 * width :], down_chunk(j)) * slope_sc[:, pl.ds(at, width)]
        ).astype(bf16)
        right_ref[:, pl.ds(pl.multiple_of(at + width, 128), width)] = du
        sums_ref[pl.ds(j + 8, 1), :] += column_sum(du)
        z_sc[...] += nt(du, up_chunk(j))

    dy1 = z_sc[...]
    hidden = x_ref[...].astype(f32) + (nn(left_ref[:, 0:width], out_weight()) + vector(0))
    n1, r1 = norm_forward(hidden)
    sums_ref[3:4, :] += column_sum(dy1 * n1)
    sums_ref[4:5, :] += column_sum(dy1)
    dh1 = norm_backward(dy1, n1, r1, vector(1))
    dh_ref[...] = dh1
    da = dh1.astype(bf16)
    right_ref[:, 0:width] = da
    sums_ref[5:6, :] += column_sum(da)
    dc = nt(da, out_weight())
    dco_ref[...] = jnp.where(first, dc[:, :half], dc[:, half:]).astype(bf16)
    dcx_ref[...] = jnp.where(first, dc[:, half:], dc[:, :half]).astype(bf16)


def chain(side, x, c_own, c_other, cot, weights, vectors):
    tokens, width = x.shape
    half = width // 2

    def rows_spec(cols):
        return pl.BlockSpec((BLOCK, cols), lambda i, *_: (i, 0))

    def shape(cols, kind):
        return jax.ShapeDtypeStruct((tokens, cols), kind)

    return pl.pallas_call(
        chain_kernel,
        grid_spec=pltpu.PrefetchScalarGridSpec(
            num_scalar_prefetch=1,
            grid=(tokens // BLOCK,),
            in_specs=[
                rows_spec(width),
                rows_spec(half),
                rows_spec(half),
                rows_spec(width),
                pl.BlockSpec(weights.shape, lambda i, *_: (0, 0, 0), pipeline_mode=pl.Buffered(1)),
                pl.BlockSpec(vectors.shape, lambda i, *_: (0, 0)),
            ],
            out_specs=[
                rows_spec(width),
                rows_spec(width),
                rows_spec(6 * width),
                rows_spec(6 * width),
                rows_spec(half),
                rows_spec(half),
                pl.BlockSpec((16, width), lambda i, *_: (0, 0)),
            ],
            scratch_shapes=[pltpu.VMEM((BLOCK, 4 * width), f32), pltpu.VMEM((BLOCK, width), f32)],
        ),
        out_shape=[
            shape(width, bf16),
            shape(width, f32),
            shape(6 * width, bf16),
            shape(6 * width, bf16),
            shape(half, bf16),
            shape(half, bf16),
            jax.ShapeDtypeStruct((16, width), f32),
        ],
        compiler_params=pltpu.CompilerParams(vmem_limit_bytes=VMEM_LIMIT),
        cost_estimate=cost(2 * tokens * width * width * 19, tokens * width * 36 + weights.size * 2),
        name="chain",
    )(side[None], x, c_own, c_other, cot, weights, vectors)


def feed_grad_kernel(l_ref, r_ref, out_ref):
    width = l_ref.shape[1]
    rows = width // GROUPS
    at = pl.program_id(0)
    grad = tn(l_ref[...], r_ref[...]).astype(bf16)

    @pl.when(at == 0)
    def _():
        out_ref[:, 4 * rows : 5 * rows, :] = grad.reshape(GROUPS, rows, width)

    @pl.when((at >= 1) & (at < 5))
    def _():
        start = pl.multiple_of(5 * rows + (at - 1) * rows, 16)
        out_ref[:, pl.ds(start, rows), :] = grad.reshape(GROUPS, rows, width)

    @pl.when(at >= 5)
    def _():
        out_ref[pl.ds((at - 5) * 4, 4), 0 : 4 * rows, :] = grad.reshape(4, 4 * rows, width)


def chip_grad_kernel(l_ref, r_ref, out_ref, part, from_core, c_send, c_recv):
    width = l_ref.shape[1]
    rows = width // GROUPS
    at = pl.program_id(0)
    x, _, z, y, core = spots()
    partner = (x, slot_of(z, y, 1 - core))
    spans = [(slice(0, 8), 4 * rows + i * rows, rows) for i in range(5)]
    spans += [(slice(2 * j, 2 * j + 2), 0, 4 * rows) for j in range(4)]

    def copy_of(i):
        rails, start, size = spans[i]
        return send(
            part.at[rails, 1 - core, slice(start, start + size), :],
            from_core.at[rails, slice(start, start + size), :],
            c_send.at[i],
            c_recv.at[i],
            partner,
        )

    def add(i):
        rails, start, size = spans[i]
        copy_of(i).wait_recv()
        for rail in range(rails.start, rails.stop):
            mine = part[rail, core, start : start + size, :].astype(f32)
            theirs = from_core[rail, start : start + size, :].astype(f32)
            out_ref[rail, start : start + size, :] = (mine + theirs).astype(bf16)

    @pl.when(at == 0)
    def _():
        greet([partner])

    grad = tn(l_ref[...], r_ref[...]).astype(bf16)
    for i in range(9):

        @pl.when(at == i)
        def _(i=i):
            rails, start, size = spans[i]
            count = rails.stop - rails.start
            part[rails, :, start : start + size, :] = grad.reshape(count, 2, size, width)
            copy_of(i).start()
            if i >= 2:
                add(i - 2)
            if i == 8:
                add(7)
                add(8)
                for k in range(9):
                    copy_of(k).wait_send()


def feed_grad(left, right, direct):
    tokens = left.shape[0]
    width = left.shape[1] // 6
    rows = width // GROUPS

    def left_at(i):
        return (0, jnp.where(i == 0, 0, jnp.where(i < 5, 1, i - 3)))

    def right_at(i):
        return (0, jnp.minimum(i, 5))

    slots = 8 if direct else GROUPS
    scratch = [
        pltpu.VMEM((8, 2, 9 * rows, width), bf16),
        pltpu.VMEM((8, 9 * rows, width), bf16),
        pltpu.SemaphoreType.DMA((9,)),
        pltpu.SemaphoreType.DMA((9,)),
    ]
    extra = dict(collective_id=2, has_side_effects=True) if direct else {}
    return pl.pallas_call(
        chip_grad_kernel if direct else feed_grad_kernel,
        grid=(9,),
        in_specs=[
            pl.BlockSpec((tokens, width), left_at),
            pl.BlockSpec((tokens, width), right_at),
        ],
        out_specs=pl.BlockSpec((slots, 9 * rows, width), lambda i: (0, 0, 0)),
        out_shape=jax.ShapeDtypeStruct((slots, 9 * rows, width), bf16),
        scratch_shapes=scratch if direct else (),
        compiler_params=pltpu.CompilerParams(vmem_limit_bytes=VMEM_LIMIT, **extra),
        cost_estimate=cost(2 * tokens * width * width * 9, tokens * width * 24 + width * width * 18),
        name="feed_grad",
    )(left, right)


def attn_grad_kernel(x_ref, d_ref, vec_ref, out_ref):
    width = x_ref.shape[1]
    rows = width // GROUPS
    at = pl.program_id(0)
    grad = tn(x_ref[...], d_ref[...]).astype(bf16)
    start = pl.multiple_of(at * rows, 16)
    out_ref[:, pl.ds(start, rows), :] = grad.reshape(GROUPS, rows, width)
    out_ref[:, 3 * rows :, :] = vec_ref[...]


def attn_grad(x, d, vectors):
    tokens, width = x.shape
    rows = width // GROUPS
    return pl.pallas_call(
        attn_grad_kernel,
        grid=(3,),
        in_specs=[
            pl.BlockSpec((tokens, width), lambda i: (0, 0)),
            pl.BlockSpec((tokens, width), lambda i: (0, i)),
            pl.BlockSpec((GROUPS, 16, width), lambda i: (0, 0, 0)),
        ],
        out_specs=pl.BlockSpec((GROUPS, 3 * rows + 16, width), lambda i: (0, 0, 0)),
        out_shape=jax.ShapeDtypeStruct((GROUPS, 3 * rows + 16, width), bf16),
        compiler_params=pltpu.CompilerParams(vmem_limit_bytes=VMEM_LIMIT),
        cost_estimate=cost(2 * tokens * width * width * 3, tokens * width * 8 + width * width * 6),
        name="attn_grad",
    )(x, d, vectors)


def scatter_kernel(
    x_ref,
    d_ref,
    vec_ref,
    w_ref,
    dh_ref,
    dx_ref,
    gq_ref,
    gk_ref,
    gv_ref,
    gvec_ref,
    part,
    from_core,
    from_y,
    from_z,
    from_x,
    out_y,
    out_z,
    held,
    total,
    dx_out,
    from_dx,
    d_send,
    d_recv,
    c_send,
    c_recv,
    y_send,
    y_recv,
    z_send,
    z_recv,
    x_send,
    x_recv,
):
    width = x_ref.shape[1]
    half = width // 2
    rows = width // GROUPS
    step_at = pl.program_id(0)
    x, me, z, y, core = spots()
    across = (1 - x, me)
    beside = (x, slot_of(z, 1 - y, core))
    partner = (x, slot_of(z, y, 1 - core))
    spans = ((0, rows), (rows, rows), (2 * rows, rows + 16))

    def core_copy(chunk, rail):
        start, size = spans[chunk]
        return send(
            part.at[2 * rail + 1 - core, pl.ds(start, size), :],
            from_core.at[rail, pl.ds(start, size), :],
            c_send.at[chunk * 8 + rail],
            c_recv.at[chunk * 8 + rail],
            partner,
        )

    @pl.when(step_at == 0)
    def _():
        greet(all_peers())

    columns = pl.ds(pl.multiple_of(step_at * width, 128), width)
    grad = tn(x_ref[...], d_ref[:, columns]).astype(bf16)
    for chunk in range(3):

        @pl.when(step_at == chunk)
        def _(chunk=chunk):
            start = spans[chunk][0]
            part[:, start : start + rows, :] = grad.reshape(GROUPS, rows, width)
            if chunk == 2:
                part[:, 3 * rows :, :] = vec_ref[...]
            for rail in range(8):
                core_copy(chunk, rail).start()

    flat = dh_ref.shape[0]

    def input_part(start):
        found = None
        for i in range(3):
            piece = nt(
                d_ref[pl.ds(pl.multiple_of(start, BLOCK), BLOCK), i * width : i * width + width],
                w_ref[:, i * rows : i * rows + rows, :].reshape(width, width),
            )
            found = piece if found is None else found + piece
        return found

    @pl.when(step_at == 2)
    def _():
        def z_order(step):
            return lax.rem(z + 1 + step, 4)

        def y_copy(zz):
            return send(out_y.at[zz], from_y.at[zz], y_send.at[zz], y_recv.at[zz], beside)

        def z_copy(zz):
            return send(
                out_z.at[zz], from_z.at[z], z_send.at[zz], z_recv.at[z], (x, slot_of(zz, y, core))
            )

        def core_wait(rail):
            for chunk in range(3):
                start, size = spans[chunk]
                send(
                    part.at[0, pl.ds(start, size), :],
                    from_core.at[rail, pl.ds(start, size), :],
                    c_send.at[0],
                    c_recv.at[chunk * 8 + rail],
                    partner,
                ).wait_recv()

        for step in range(4):
            zz = z_order(step)
            rail = zz * 2 + 1 - y
            core_wait(rail)
            out_y[zz] = (part[2 * rail + core].astype(f32) + from_core[rail].astype(f32)).astype(bf16)
            y_copy(zz).start()

        @pl.loop(0, flat // BLOCK)
        def _(i):
            at = pl.ds(pl.multiple_of(i * BLOCK, BLOCK), BLOCK)
            dx_out[at, :] = input_part(flat + i * BLOCK).astype(bf16)

        exchange = send(dx_out, from_dx, d_send, d_recv, across)
        exchange.start()
        for step in range(4):
            zz = z_order(step)
            rail = zz * 2 + y
            core_wait(rail)
            held[zz] = part[2 * rail + core].astype(f32) + from_core[rail].astype(f32)
        for step in range(3):
            zz = z_order(step)
            y_copy(zz).wait_recv()
            out_z[zz] = (held[zz] + from_y[zz].astype(f32)).astype(bf16)
            z_copy(zz).start()

        @pl.loop(0, flat // BLOCK)
        def _(i):
            at = pl.ds(pl.multiple_of(i * BLOCK, BLOCK), BLOCK)
            dx_ref[at, :] = dh_ref[at, :] + input_part(i * BLOCK)

        y_copy(z).wait_recv()
        result = held[z] + from_y[z].astype(f32)
        for step in range(3):
            zz = z_order(step)
            send(out_z.at[zz], from_z.at[zz], z_send.at[zz], z_recv.at[zz], partner).wait_recv()
            result = result + from_z[zz].astype(f32)
        total[...] = result.astype(bf16)
        last = send(total, from_x, x_send, x_recv, across)
        last.start()
        exchange.wait()

        @pl.loop(0, flat // BLOCK)
        def _(i):
            at = pl.ds(pl.multiple_of(i * BLOCK, BLOCK), BLOCK)
            dx_ref[at, :] += from_dx[at, :].astype(f32)

        for chunk in range(3):
            for rail in range(8):
                core_copy(chunk, rail).wait_send()
        for step in range(4):
            y_copy(z_order(step)).wait_send()
        for step in range(3):
            z_copy(z_order(step)).wait_send()
        last.wait()
        first = x == 0
        lo = low_lanes((rows, 128))

        def ordered(start, size, at):
            own = total[start : start + size, at].astype(f32)
            other = from_x[start : start + size, at].astype(f32)
            return jnp.where(first, own, other), jnp.where(first, other, own)

        for e in range(2):
            for t in range(half // 128):
                evens = ordered(e * rows, rows, slice(256 * t, 256 * t + 128))
                odds = ordered(e * rows, rows, slice(256 * t + 128, 256 * t + 256))
                for s in range(2):
                    word = jnp.where(lo, evens[s], pltpu.roll(odds[s], 64, 1))
                    entity = jnp.where(lo, pltpu.roll(evens[s], 64, 1), odds[s])
                    base = 2 * e * width + s * half + 128 * t
                    gq_ref[:, base : base + 128] = word
                    gq_ref[:, base + width : base + width + 128] = entity
        for ref, base in ((gk_ref, 0), (gv_ref, half)):
            a, b = ordered(2 * rows, rows, slice(base, base + half))
            ref[:, :half] = a
            ref[:, half:] = b
        gvec_ref[...] = total[3 * rows :, :].astype(f32) + from_x[3 * rows :, :].astype(f32)


def scatter_attention(x, d, vectors, weights, dh):
    tokens, width = x.shape
    rows = width // GROUPS
    tall = 3 * rows + 16
    sem = pltpu.SemaphoreType.DMA

    def whole(*dims):
        return pl.BlockSpec(dims, lambda i: (0,) * len(dims), pipeline_mode=pl.Buffered(1))

    outs = (dh.shape, (rows, 4 * width), (rows, width), (rows, width), (16, width))
    return pl.pallas_call(
        scatter_kernel,
        grid=(3,),
        in_specs=[
            whole(tokens, width),
            whole(*d.shape),
            whole(GROUPS, 16, width),
            whole(*weights.shape),
            whole(*dh.shape),
        ],
        out_specs=[whole(*dims) for dims in outs],
        out_shape=[jax.ShapeDtypeStruct(dims, f32) for dims in outs],
        scratch_shapes=[
            pltpu.VMEM((GROUPS, tall, width), bf16),
            pltpu.VMEM((8, tall, width), bf16),
            pltpu.VMEM((4, tall, width), bf16),
            pltpu.VMEM((4, tall, width), bf16),
            pltpu.VMEM((tall, width), bf16),
            pltpu.VMEM((4, tall, width), bf16),
            pltpu.VMEM((4, tall, width), bf16),
            pltpu.VMEM((4, tall, width), f32),
            pltpu.VMEM((tall, width), bf16),
            pltpu.VMEM(dh.shape, bf16),
            pltpu.VMEM(dh.shape, bf16),
            sem,
            sem,
            sem((24,)),
            sem((24,)),
            sem((4,)),
            sem((4,)),
            sem((4,)),
            sem((4,)),
            sem,
            sem,
        ],
        compiler_params=pltpu.CompilerParams(
            collective_id=1, has_side_effects=True, vmem_limit_bytes=VMEM_LIMIT
        ),
        cost_estimate=cost(2 * tokens * width * width * 3, tokens * width * 8 + width * width * 6),
        name="scatter",
    )(x, d, vectors, weights, dh)


def input_grad_kernel(d_ref, w_ref, out_ref):
    width = out_ref.shape[1]
    rows = width // GROUPS
    total = None
    for i in range(3):
        part = nt(
            d_ref[:, i * width : i * width + width],
            w_ref[:, i * rows : i * rows + rows, :].reshape(width, width),
        )
        total = part if total is None else total + part
    out_ref[...] = total.astype(out_ref.dtype)


def input_grad_part(d, weights, side_at, kind):
    _, micro, local, wide = d.shape
    width = wide // 3
    sub = local // BLOCK
    return pl.pallas_call(
        input_grad_kernel,
        grid=(micro, sub),
        in_specs=[
            pl.BlockSpec((None, None, BLOCK, wide), lambda m, i: (side_at, m, i, 0)),
            pl.BlockSpec(weights.shape, lambda m, i: (0, 0, 0)),
        ],
        out_specs=pl.BlockSpec((None, BLOCK, width), lambda m, i: (m, i, 0)),
        out_shape=jax.ShapeDtypeStruct((micro, local, width), kind),
        compiler_params=pltpu.CompilerParams(vmem_limit_bytes=VMEM_LIMIT),
        cost_estimate=cost(2 * micro * local * wide * width, micro * local * wide * 2 + weights.size * 2),
        name="input_grad",
    )(d, weights)


def assemble(attn_own, attn_other, side, head_dim, rows, piece):
    attn_own, attn_other = attn_own.astype(f32), attn_other.astype(f32)
    width = attn_own.shape[1]
    half = width // 2
    vec_total = attn_own[3 * rows, :piece] + attn_other[3 * rows, :piece]

    def by_side(own, other, axis):
        return jnp.where(
            side == 0,
            jnp.concatenate([own, other], axis=axis),
            jnp.concatenate([other, own], axis=axis),
        )

    def query_parts(block):
        pairs = jnp.stack([block[:rows], block[rows : 2 * rows]], axis=1)
        return unpair_columns(pairs, head_dim)

    grad_query = by_side(query_parts(attn_own), query_parts(attn_other), 3).reshape(rows, 4 * width)
    kv_own, kv_other = attn_own[2 * rows : 3 * rows], attn_other[2 * rows : 3 * rows]
    grad_key = by_side(kv_own[:, :half], kv_other[:, :half], 1)
    grad_value = by_side(kv_own[:, half:], kv_other[:, half:], 1)
    return grad_query, grad_key, grad_value, vec_total


def on_device(
    tokens,
    kinds,
    groups,
    query_weight,
    query_bias,
    key_weight,
    key_bias,
    value_weight,
    value_bias,
    output_weight,
    output_bias,
    norm1_gain,
    norm1_shift,
    up_weight,
    up_bias,
    down_weight,
    down_bias,
    norm2_gain,
    norm2_shift,
    cotangent,
):
    micro, _, local, width = tokens.shape
    half = width // 2
    head_dim = width // HEADS
    devices = lax.axis_size("shard")
    rows = width // devices
    side = lax.axis_index("seq").astype(jnp.int32)

    vectors = (
        query_bias,
        key_bias,
        value_bias,
        output_bias,
        norm1_gain,
        norm1_shift,
        up_bias,
        down_bias,
        norm2_gain,
        norm2_shift,
    )
    piece = 16 * rows
    direct = devices == GROUPS
    attn_sizes = (rows, rows, rows)
    feed_sizes = (4 * rows,) + (rows,) * 5
    if not direct:
        vector_row = jnp.pad(jnp.concatenate(vectors), (0, width - piece))[None]
        packed = pack_attention(query_weight, key_weight, value_weight, vector_row, side, head_dim)
        attn_gathered = lax.all_gather(packed[None], "shard", axis=0, tiled=True)
        other_tokens, other_kinds, other_groups = swap(tokens), swap(kinds), swap(groups)
    feed_local = pack_feed(down_weight, output_weight, up_weight)
    feed_gathered = lax.all_gather(feed_local[None], "shard", axis=0, tiled=True)
    if direct:
        attn_gathered, other_tokens, other_kinds, other_groups = gather_attention(
            query_weight, key_weight, value_weight, vectors, tokens, kinds, groups
        )
    vectors = attn_gathered[:, 3 * rows, :piece]
    if direct:
        attn_w, feed_w = attn_gathered, feed_gathered
    else:
        attn_w = regroup(attn_gathered, attn_sizes)
        feed_w = regroup(feed_gathered, feed_sizes)

    def whole_vector(start, size):
        return vectors[:, start : start + size].reshape(-1).astype(f32)

    full_query_bias = whole_vector(0, 4 * rows)
    full_key_bias = whole_vector(4 * rows, rows)
    full_value_bias = whole_vector(5 * rows, rows)
    bias_rows = jnp.concatenate(
        [
            pair_columns(full_query_bias, side, head_dim),
            jnp.concatenate([own_half(full_key_bias, side), own_half(full_value_bias, side)])[None],
        ],
        axis=0,
    )
    full_up_bias = whole_vector(9 * rows, 4 * rows).reshape(4, width)
    chain_vectors = jnp.concatenate(
        [
            whole_vector(6 * rows, rows)[None],
            whole_vector(7 * rows, rows)[None],
            whole_vector(8 * rows, rows)[None],
            full_up_bias,
            whole_vector(13 * rows, rows)[None],
            whole_vector(14 * rows, rows)[None],
            whole_vector(15 * rows, rows)[None],
        ],
        axis=0,
    )

    own_tokens = tokens[:, 0]
    own_groups, far_groups = groups.reshape(micro, local), other_groups.reshape(micro, local)
    qp, km, kmt, v, vt, xs, kind_col, gk, gq = project(
        tokens, other_tokens, kinds, other_kinds, groups, other_groups, attn_w, bias_rows
    )
    c, ct, lse = attend(own_groups, far_groups, qp, km, vt, gk, gq)
    c_other = swap(c[1])
    flat = micro * local
    mixed, dh1, left, right, dc_own, dc_other, sums = chain(
        side,
        own_tokens.reshape(flat, width),
        c[0].reshape(flat, half),
        c_other.reshape(flat, half),
        cotangent.reshape(flat, width),
        feed_w,
        chain_vectors,
    )

    dc_swapped = swap(dc_other)
    feed_part = feed_grad(left, right, direct)
    dc_swapped, feed_part = lax.optimization_barrier((dc_swapped, feed_part))
    dc = jnp.stack([dc_own, dc_swapped]).reshape(2, micro, local, half)
    rails = None
    if direct:
        rails = [[2 * rail + core for rail in range(8)] for core in range(2)]
    else:
        feed_part = ungroup(feed_part, feed_sizes, devices)
    feed_sum = lax.psum_scatter(
        feed_part, "shard", scatter_dimension=0, axis_index_groups=rails, tiled=True
    )[0]
    d, db = attend_back(own_groups, far_groups, qp, km, kmt, v, dc, ct, lse, gk, gq, kind_col)

    query_own = unpair_columns(db[0, : 2 * width].reshape(2, width), head_dim)
    zero = jnp.zeros((half,), f32)

    def spread(own):
        return jnp.where(side == 0, jnp.concatenate([own, zero]), jnp.concatenate([zero, own]))

    query_spread = jnp.concatenate([spread(query_own[e, w]) for e in range(2) for w in range(2)])
    key_spread = spread(db[0, 2 * width : 2 * width + half])
    value_spread = spread(db[0, 2 * width + half :])
    grad_vectors = jnp.concatenate(
        [
            query_spread.reshape(devices, 4 * rows),
            key_spread.reshape(devices, rows),
            value_spread.reshape(devices, rows),
            sums[5].reshape(devices, rows),
            sums[3].reshape(devices, rows),
            sums[4].reshape(devices, rows),
            sums[8:12].reshape(devices, 4 * rows),
            sums[2].reshape(devices, rows),
            sums[0].reshape(devices, rows),
            sums[1].reshape(devices, rows),
        ],
        axis=1,
    ).astype(bf16)
    grad_vectors = jnp.pad(grad_vectors[:, None, :], ((0, 0), (0, 15), (0, width - piece)))
    flat_x = xs.reshape(2 * flat, width)
    flat_d = d.reshape(2 * flat, 3 * width)
    if direct:
        input_grad, grad_query, grad_key, grad_value, vec_rows = scatter_attention(
            flat_x, flat_d, grad_vectors, attn_w, dh1
        )
        input_grad = input_grad.reshape(micro, local, width)
        vec_total = vec_rows[0, :piece]
    else:
        zeros = jnp.zeros((GROUPS, 16, width), bf16)
        attn_part = attn_grad(flat_x, flat_d, zeros)
        attn_part = jnp.concatenate(
            [ungroup(attn_part[:, : 3 * (width // GROUPS)], attn_sizes, devices), grad_vectors], axis=1
        )
        attn_sum = lax.psum_scatter(attn_part, "shard", scatter_dimension=0, tiled=True)[0]
        attn_other = swap(attn_sum)
        grad_query, grad_key, grad_value, vec_total = assemble(
            attn_sum, attn_other, side, head_dim, rows, piece
        )
        dx_other = input_grad_part(d, attn_w, 1, bf16)
        dx_own = input_grad_part(d, attn_w, 0, f32)
        input_grad = dh1.reshape(micro, local, width) + dx_own + swap(dx_other).astype(f32)

    feed_total = feed_sum.astype(f32) + swap(feed_sum).astype(f32)
    grad_down = feed_total[: 4 * rows]
    grad_output = feed_total[4 * rows : 5 * rows]
    grad_up = jnp.concatenate(
        [feed_total[(5 + j) * rows : (6 + j) * rows] for j in range(4)], axis=1
    )

    def piece_of(start, size):
        return vec_total[start : start + size]

    return (
        mixed.reshape(micro, 1, local, width),
        input_grad[:, None],
        grad_query,
        piece_of(0, 4 * rows),
        grad_key,
        piece_of(4 * rows, rows),
        grad_value,
        piece_of(5 * rows, rows),
        grad_output,
        piece_of(6 * rows, rows),
        piece_of(7 * rows, rows),
        piece_of(8 * rows, rows),
        grad_up,
        piece_of(9 * rows, 4 * rows),
        grad_down,
        piece_of(13 * rows, rows),
        piece_of(14 * rows, rows),
        piece_of(15 * rows, rows),
    )


def solution(mesh):
    weight = P("shard", None)
    vector = P("shard")
    tokens = P(None, "shard", "seq", None)
    marks = P(None, "shard", "seq")
    return jax.shard_map(
        on_device,
        mesh=mesh,
        in_specs=(tokens, marks, marks)
        + (weight, vector) * 4
        + (vector, vector)
        + (weight, vector) * 2
        + (vector, vector)
        + (tokens,),
        out_specs=(tokens, tokens)
        + (weight, vector) * 4
        + (vector, vector)
        + (weight, vector) * 2
        + (vector, vector),
        check_vma=False,
    )
```

```python
import functools

import jax
import jax.numpy as jnp
from jax import lax
from jax.experimental import pallas as pl
from jax.experimental.pallas import tpu as pltpu
from jax.sharding import PartitionSpec as P


HEADS = 12
GROUPS = 16
BLOCK = 256
masked_score = -1e30
layer_eps = 1e-12
bf16 = jnp.bfloat16
f32 = jnp.float32
VMEM_LIMIT = 60 * 1024 * 1024


def nn(a, b):
    return lax.dot_general(a, b, (((1,), (0,)), ((), ())), preferred_element_type=f32)


def nt(a, b):
    return lax.dot_general(a, b, (((1,), (1,)), ((), ())), preferred_element_type=f32)


def tn(a, b):
    return lax.dot_general(a, b, (((0,), (0,)), ((), ())), preferred_element_type=f32)


def swap(value):
    return lax.ppermute(value, "seq", [(0, 1), (1, 0)])


def cost(flops, moved, trans=0):
    return pl.CostEstimate(flops=flops, bytes_accessed=moved, transcendentals=trans)


def low_lanes(shape):
    return lax.broadcasted_iota(jnp.int32, shape, len(shape) - 1) % 128 < 64


def pack_into(first, q_ref, k_ref, v_ref, vec, out_ref):
    rows, width = k_ref.shape
    half = width // 2

    def own(ref, base):
        return jnp.where(
            first,
            ref[:, base : base + half].astype(f32),
            ref[:, base + half : base + width].astype(f32),
        )

    lo = low_lanes((rows, 128))
    for e in range(2):
        word = own(q_ref, 2 * e * width)
        entity = own(q_ref, (2 * e + 1) * width)
        for t in range(half // 128):
            a = word[:, 128 * t : 128 * t + 128]
            b = entity[:, 128 * t : 128 * t + 128]
            even = jnp.where(lo, a, pltpu.roll(b, 64, 1))
            odd = jnp.where(lo, pltpu.roll(a, 64, 1), b)
            out_ref[e * rows : e * rows + rows, 256 * t : 256 * t + 128] = even.astype(bf16)
            out_ref[e * rows : e * rows + rows, 256 * t + 128 : 256 * t + 256] = odd.astype(bf16)
    out_ref[2 * rows : 3 * rows, :half] = own(k_ref, 0).astype(bf16)
    out_ref[2 * rows : 3 * rows, half:] = own(v_ref, 0).astype(bf16)
    out_ref[3 * rows :, :] = jnp.broadcast_to(vec, (16, width)).astype(bf16)


def spots():
    x = lax.axis_index("seq")
    me = lax.axis_index("shard")
    core = lax.rem(me, 2)
    y = lax.rem(me // 2, 2)
    z = me // 4
    return x, me, z, y, core


def slot_of(z, y, core):
    return z * 4 + y * 2 + core


def greet(peers):
    barrier = pltpu.get_barrier_semaphore()
    for peer in peers:
        pl.semaphore_signal(barrier, inc=1, device_id=peer, device_id_type=pl.DeviceIdType.MESH)
    pl.semaphore_wait(barrier, len(peers))


def all_peers():
    x, me, z, y, core = spots()
    peers = [(x, slot_of(z, y, 1 - core)), (x, slot_of(z, 1 - y, core)), (1 - x, me)]
    for step in range(1, 4):
        peers.append((x, slot_of(lax.rem(z + step, 4), y, core)))
    return peers


def send(src, dst, send_sem, recv_sem, device):
    return pltpu.make_async_remote_copy(
        src_ref=src,
        dst_ref=dst,
        send_sem=send_sem,
        recv_sem=recv_sem,
        device_id=device,
        device_id_type=pl.DeviceIdType.MESH,
    )


def gather_kernel(*refs):
    q_ref, k_ref, v_ref = refs[:3]
    vec_refs = refs[3:13]
    tok_ref, kinds_ref, groups_ref = refs[13:16]
    w_ref, tok_out, kinds_out, groups_out = refs[16:20]
    mine, keep_sem, x_send, x_recv, z_send, z_recv, y_send, y_recv, c_send, c_recv = refs[20:]
    x, me, z, y, core = spots()
    across = (1 - x, me)
    beside = (x, slot_of(z, 1 - y, core))
    partner = (x, slot_of(z, y, 1 - core))
    greet(all_peers())
    over = [
        send(src, dst, x_send.at[i], x_recv.at[i], across)
        for i, (src, dst) in enumerate(
            ((kinds_ref, kinds_out), (groups_ref, groups_out), (tok_ref, tok_out))
        )
    ]
    for copy in over:
        copy.start()
    vec = jnp.concatenate([r[...].astype(f32) for r in vec_refs], axis=1)
    pack_into(x == 0, q_ref, k_ref, v_ref, vec, mine)
    started = []
    for step in range(1, 4):
        copy = send(
            mine,
            w_ref.at[me],
            z_send.at[step - 1],
            z_recv.at[z],
            (x, slot_of(lax.rem(z + step, 4), y, core)),
        )
        copy.start()
        started.append(copy)
    copy = send(mine, w_ref.at[me], y_send.at[z], y_recv.at[z], beside)
    copy.start()
    started.append(copy)
    copy = send(mine, w_ref.at[me], c_send.at[z * 2 + y], c_recv.at[z * 2 + y], partner)
    copy.start()
    started.append(copy)
    keep = pltpu.make_async_copy(mine, w_ref.at[me], keep_sem)
    keep.start()
    for step in range(1, 4):
        zz = lax.rem(z + step, 4)
        at = slot_of(zz, y, core)
        held = w_ref.at[at]
        send(held, held, z_send.at[0], z_recv.at[zz], partner).wait_recv()
        for copy in (
            send(held, held, y_send.at[zz], y_recv.at[zz], beside),
            send(held, held, c_send.at[zz * 2 + y], c_recv.at[zz * 2 + y], partner),
        ):
            copy.start()
            started.append(copy)
    for step in range(4):
        zz = lax.rem(z + step, 4)
        rail = zz * 2 + 1 - y
        held = w_ref.at[slot_of(zz, 1 - y, core)]
        send(held, held, y_send.at[0], y_recv.at[zz], partner).wait_recv()
        copy = send(held, held, c_send.at[rail], c_recv.at[rail], partner)
        copy.start()
        started.append(copy)
    for rail in range(8):
        held = w_ref.at[2 * rail + 1 - core]
        send(held, held, c_send.at[0], c_recv.at[rail], partner).wait_recv()
    keep.wait()
    for copy in started:
        copy.wait_send()
    for copy in over:
        copy.wait()


def gather_attention(query_weight, key_weight, value_weight, vectors, tokens, kinds, groups):
    rows, width = key_weight.shape
    vmem = pl.BlockSpec(memory_space=pltpu.VMEM)
    anywhere = pl.BlockSpec(memory_space=pl.ANY)
    sem = pltpu.SemaphoreType.DMA
    return pl.pallas_call(
        gather_kernel,
        in_specs=[vmem] * 13 + [anywhere] * 3,
        out_specs=[anywhere] * 4,
        out_shape=[
            jax.ShapeDtypeStruct((GROUPS, 3 * rows + 16, width), bf16),
            jax.ShapeDtypeStruct(tokens.shape, tokens.dtype),
            jax.ShapeDtypeStruct(kinds.shape, kinds.dtype),
            jax.ShapeDtypeStruct(groups.shape, groups.dtype),
        ],
        scratch_shapes=[
            pltpu.VMEM((3 * rows + 16, width), bf16),
            sem,
            sem((3,)),
            sem((3,)),
            sem((3,)),
            sem((4,)),
            sem((4,)),
            sem((4,)),
            sem((8,)),
            sem((8,)),
        ],
        compiler_params=pltpu.CompilerParams(
            collective_id=0, has_side_effects=True, vmem_limit_bytes=VMEM_LIMIT
        ),
        name="gather",
    )(query_weight, key_weight, value_weight, *[v[None] for v in vectors], tokens, kinds, groups)


def pair_columns(columns, side, head_dim):
    lead = columns.shape[:-1]
    per = columns.shape[-1] // (8 * head_dim)
    view = columns.reshape(lead + (2, 2, 2, per, head_dim))
    view = jnp.where(side == 0, view[..., 0, :, :], view[..., 1, :, :])
    return jnp.swapaxes(view, -3, -2).reshape(lead + (2, -1))


def unpair_columns(pairs, head_dim):
    lead = pairs.shape[:-2]
    per = pairs.shape[-1] // (2 * head_dim)
    view = pairs.reshape(lead + (2, per, 2, head_dim))
    return jnp.swapaxes(view, -3, -2).reshape(lead + (2, 2, per * head_dim))


def own_half(columns, side):
    half = columns.shape[-1] // 2
    return jnp.where(side == 0, columns[..., :half], columns[..., half:])


def pack_attention(query_weight, key_weight, value_weight, vector, side, head_dim):
    width = key_weight.shape[1]
    pairs = pair_columns(query_weight, side, head_dim)
    key_value = jnp.concatenate([own_half(key_weight, side), own_half(value_weight, side)], axis=1)
    return jnp.concatenate(
        [pairs[:, 0], pairs[:, 1], key_value, jnp.broadcast_to(vector, (16, width))], axis=0
    )


def pack_feed_kernel(down_ref, output_ref, up_ref, out_ref):
    rows, width = output_ref.shape
    out_ref[0 : 4 * rows, :] = down_ref[...]
    out_ref[4 * rows : 5 * rows, :] = output_ref[...]
    for j in range(4):
        out_ref[(5 + j) * rows : (6 + j) * rows, :] = up_ref[:, j * width : j * width + width]


def pack_feed(down_weight, output_weight, up_weight):
    rows, width = output_weight.shape
    if rows % 16:
        return jnp.concatenate(
            [down_weight, output_weight]
            + [up_weight[:, j * width : j * width + width] for j in range(4)],
            axis=0,
        )
    vmem = pl.BlockSpec(memory_space=pltpu.VMEM)
    return pl.pallas_call(
        pack_feed_kernel,
        in_specs=[vmem] * 3,
        out_specs=vmem,
        out_shape=jax.ShapeDtypeStruct((9 * rows, width), bf16),
        name="pack_feed",
    )(down_weight, output_weight, up_weight)


def regroup(gathered, sizes):
    _, _, width = gathered.shape
    pieces = []
    start = 0
    for size in sizes:
        piece = gathered[:, start : start + size].reshape(GROUPS, -1, width)
        pieces.append(piece)
        start += size
    return jnp.concatenate(pieces, axis=1)


def ungroup(grouped, sizes, devices):
    _, _, width = grouped.shape
    pieces = []
    start = 0
    for size in sizes:
        wide = size * devices // GROUPS
        pieces.append(grouped[:, start : start + wide].reshape(devices, size, width))
        start += wide
    return jnp.concatenate(pieces, axis=1)


def project_kernel(
    own_ref,
    other_ref,
    own_kind_ref,
    other_kind_ref,
    own_group_ref,
    other_group_ref,
    w_ref,
    bias_ref,
    qp_ref,
    km_ref,
    kmt_ref,
    v_ref,
    vt_ref,
    xs_ref,
    kind_ref,
    gk_ref,
    gq_ref,
):
    width = own_ref.shape[1]
    half = width // 2
    rows = width // GROUPS
    mine = pl.program_id(0) == 0

    def column(row):
        return jnp.broadcast_to(row.astype(f32), (128, BLOCK)).T.astype(jnp.int32)

    x = jnp.where(mine, own_ref[...].astype(f32), other_ref[...].astype(f32)).astype(bf16)
    group = jnp.where(mine, own_group_ref[...], other_group_ref[...])
    kinds = column(jnp.where(mine, own_kind_ref[...], other_kind_ref[...]))
    kind = kinds[:, 0:1]
    xs_ref[...] = x
    kind_ref[...] = kind
    gk_ref[...] = column(group)[:, 0:1]
    gq_ref[...] = group
    wa = w_ref[:, 0:rows, :].reshape(width, width)
    wb = w_ref[:, rows : 2 * rows, :].reshape(width, width)
    wkv = w_ref[:, 2 * rows : 3 * rows, :].reshape(width, width)
    qa = nn(x, wa) + bias_ref[0:1, :]
    qb = nn(x, wb) + bias_ref[1:2, :]
    qp_ref[...] = (jnp.where(kind == 1, qb, qa) * 0.125).astype(bf16)
    kv = nn(x, wkv) + bias_ref[2:3, :]
    lane_high = (lax.broadcasted_iota(jnp.int32, (BLOCK, 128), 1) >= 64).astype(jnp.int32)
    keep = lane_high == kinds
    lo = lane_high == 0
    for t in range(half // 128):
        k = kv[:, 128 * t : 128 * t + 128]
        r = pltpu.roll(k, 64, 1)
        even = jnp.where(keep, jnp.where(lo, k, r), 0.0)
        odd = jnp.where(keep, jnp.where(lo, r, k), 0.0)
        km_ref[:, 256 * t : 256 * t + 128] = even.astype(bf16)
        km_ref[:, 256 * t + 128 : 256 * t + 256] = odd.astype(bf16)
        kmt_ref[256 * t : 256 * t + 128, :] = even.T.astype(bf16)
        kmt_ref[256 * t + 128 : 256 * t + 256, :] = odd.T.astype(bf16)
    v = kv[:, half:]
    v_ref[...] = v.astype(bf16)
    vt_ref[...] = v.T.astype(bf16)


def project(tokens, other_tokens, kinds, other_kinds, groups, other_groups, weights, bias_rows):
    micro, _, local, width = tokens.shape
    halves = 2
    half = width // 2
    sub = local // BLOCK

    def rows_spec(cols):
        return pl.BlockSpec((None, None, BLOCK, cols), lambda a, m, i: (a, m, i, 0))

    def cols_spec(count):
        return pl.BlockSpec((None, None, count, BLOCK), lambda a, m, i: (a, m, 0, i))

    def shape(*dims, kind=bf16):
        return jax.ShapeDtypeStruct((halves, micro) + dims, kind)

    def pick(own, a, index, stop):
        return jnp.where(a == 0, index, stop) if own else jnp.where(a == 0, 0, index)

    def token_spec(own):
        return pl.BlockSpec(
            (None, None, BLOCK, width),
            lambda a, m, i: (pick(own, a, m, micro - 1), 0, pick(own, a, i, sub - 1), 0),
        )

    def mark_spec(own):
        return pl.BlockSpec(
            (None, 1, BLOCK),
            lambda a, m, i: (pick(own, a, m, micro - 1), 0, pick(own, a, i, sub - 1)),
        )

    count = halves * micro * local
    return pl.pallas_call(
        project_kernel,
        grid=(halves, micro, sub),
        in_specs=[
            token_spec(True),
            token_spec(False),
            mark_spec(True),
            mark_spec(False),
            mark_spec(True),
            mark_spec(False),
            pl.BlockSpec(weights.shape, lambda a, m, i: (0, 0, 0)),
            pl.BlockSpec(bias_rows.shape, lambda a, m, i: (0, 0)),
        ],
        out_specs=[
            rows_spec(width),
            rows_spec(width),
            cols_spec(width),
            rows_spec(half),
            cols_spec(half),
            rows_spec(width),
            rows_spec(1),
            rows_spec(1),
            cols_spec(1),
        ],
        out_shape=[
            shape(local, width),
            shape(local, width),
            shape(width, local),
            shape(local, half),
            shape(half, local),
            shape(local, width),
            shape(local, 1, kind=jnp.int32),
            shape(local, 1, kind=jnp.int32),
            shape(1, local, kind=jnp.int32),
        ],
        compiler_params=pltpu.CompilerParams(vmem_limit_bytes=VMEM_LIMIT),
        cost_estimate=cost(2 * count * width * 3 * width, count * width * 10),
        name="project",
    )(tokens, other_tokens, kinds, other_kinds, groups, other_groups, weights, bias_rows)


def place(block, per):
    return block // per, pl.multiple_of(lax.rem(block, per) * BLOCK, BLOCK)


def ends_of(own_ref, other_ref, micro_at, block, per):
    at = lax.rem(block, per) * BLOCK
    mine = block < per
    first = jnp.where(mine, own_ref[micro_at, at], other_ref[micro_at, at])
    last_at = at + BLOCK - 1
    return first, jnp.where(mine, own_ref[micro_at, last_at], other_ref[micro_at, last_at])


def attend_kernel(
    own_ref, other_ref, qp_ref, km_ref, vt_ref, gk_ref, gq_ref, c_ref, ct_ref, lse_ref, m_sc, l_sc, acc_sc
):
    micro_at = pl.program_id(0)
    local = qp_ref.shape[1]
    per = local // BLOCK
    blocks = 2 * per
    heads = qp_ref.shape[2] // 128

    @pl.loop(0, blocks)
    def _(qb):
        qh, qo = place(qb, per)
        m_sc[...] = jnp.full_like(m_sc, masked_score)
        l_sc[...] = jnp.zeros_like(l_sc)
        acc_sc[...] = jnp.zeros_like(acc_sc)
        q_low, q_high = ends_of(own_ref, other_ref, micro_at, qb, per)

        @pl.loop(0, blocks)
        def _(kb):
            k_low, k_high = ends_of(own_ref, other_ref, micro_at, kb, per)

            @pl.when((q_low <= k_high) & (k_low <= q_high))
            def _():
                kh, ko = place(kb, per)
                same = gk_ref[kh, pl.ds(ko, BLOCK), :] == gq_ref[qh, :, pl.ds(qo, BLOCK)]
                bias = jnp.where(same, 0.0, masked_score)
                for h in range(heads):
                    at = slice(128 * h, 128 * h + 128)
                    vat = slice(64 * h, 64 * h + 64)
                    s = nt(km_ref[kh, pl.ds(ko, BLOCK), at], qp_ref[qh, pl.ds(qo, BLOCK), at]) + bias
                    m_old = m_sc[h : h + 1, :]
                    m_new = jnp.maximum(m_old, jnp.max(s, axis=0, keepdims=True))
                    alpha = jnp.exp(m_old - m_new)
                    p = jnp.exp(s - m_new)
                    m_sc[h : h + 1, :] = m_new
                    l_sc[h : h + 1, :] = alpha * l_sc[h : h + 1, :] + jnp.sum(p, axis=0, keepdims=True)
                    acc_sc[vat, :] = alpha * acc_sc[vat, :] + nn(
                        vt_ref[kh, vat, pl.ds(ko, BLOCK)], p.astype(bf16)
                    )

        cols = pl.ds(pl.multiple_of(qb * BLOCK, BLOCK), BLOCK)
        for h in range(heads):
            vat = slice(64 * h, 64 * h + 64)
            total = l_sc[h : h + 1, :]
            ct_ref[vat, cols] = acc_sc[vat, :] / total
            lse_ref[h : h + 1, cols] = m_sc[h : h + 1, :] + jnp.log(total)
        c_ref[qh, pl.ds(qo, BLOCK), :] = ct_ref[:, cols].T.astype(bf16)


def whole_micro(array):
    rest = array.shape[2:]
    return pl.BlockSpec((array.shape[0], None) + rest, lambda m, *_: (0, m) + (0,) * len(rest))


def attend(own_groups, other_groups, qp, km, vt, gk, gq):
    halves, micro, local, width = qp.shape
    half = width // 2
    heads = width // 128
    length = halves * local
    return pl.pallas_call(
        attend_kernel,
        grid_spec=pltpu.PrefetchScalarGridSpec(
            num_scalar_prefetch=2,
            grid=(micro,),
            in_specs=[whole_micro(a) for a in (qp, km, vt, gk, gq)],
            out_specs=[
                pl.BlockSpec((halves, None, local, half), lambda m, *_: (0, m, 0, 0)),
                pl.BlockSpec((None, half, length), lambda m, *_: (m, 0, 0)),
                pl.BlockSpec((None, 8, length), lambda m, *_: (m, 0, 0)),
            ],
            scratch_shapes=[
                pltpu.VMEM((8, BLOCK), f32),
                pltpu.VMEM((8, BLOCK), f32),
                pltpu.VMEM((half, BLOCK), f32),
            ],
        ),
        out_shape=[
            jax.ShapeDtypeStruct((halves, micro, local, half), bf16),
            jax.ShapeDtypeStruct((micro, half, length), f32),
            jax.ShapeDtypeStruct((micro, 8, length), f32),
        ],
        compiler_params=pltpu.CompilerParams(vmem_limit_bytes=VMEM_LIMIT),
        cost_estimate=cost(
            micro * heads * length * length * 512, micro * length * width * 8, micro * heads * length * length
        ),
        name="attend",
    )(own_groups, other_groups, qp, km, vt, gk, gq)


def attend_back_kernel(
    micro_at,
    own_ref,
    other_ref,
    qp_ref,
    km_ref,
    kmt_ref,
    v_ref,
    dc_ref,
    ct_ref,
    lse_ref,
    gk_ref,
    gq_ref,
    kind_ref,
    *rest,
):
    d_ref, db_ref, dqt_sc, dk_sc, dv_sc, delta_sc = rest[-6:]
    local, width = qp_ref.shape[1], qp_ref.shape[2]
    half = width // 2
    per = local // BLOCK
    blocks = 2 * per
    tiles = half // 128
    dk_sc[...] = jnp.zeros_like(dk_sc)
    dv_sc[...] = jnp.zeros_like(dv_sc)

    db_ref[...] = jnp.zeros_like(db_ref)

    lo = low_lanes((BLOCK, 128))

    @pl.loop(0, blocks)
    def _(qb):
        qh, qo = place(qb, per)
        qrows = pl.ds(qo, BLOCK)
        cols = pl.ds(pl.multiple_of(qb * BLOCK, BLOCK), BLOCK)
        dct = dc_ref[qh, qrows, :].astype(f32).T
        inner = dct * ct_ref[:, cols]
        for h in range(2 * tiles):
            delta_sc[h : h + 1, :] = jnp.sum(inner[64 * h : 64 * h + 64, :], axis=0, keepdims=True)
        dqt_sc[...] = jnp.zeros_like(dqt_sc)
        q_low, q_high = ends_of(own_ref, other_ref, micro_at, qb, per)

        @pl.loop(0, blocks)
        def _(kb):
            k_low, k_high = ends_of(own_ref, other_ref, micro_at, kb, per)

            @pl.when((q_low <= k_high) & (k_low <= q_high))
            def _():
                kh, ko = place(kb, per)
                krows = pl.ds(ko, BLOCK)
                drows = pl.ds(pl.multiple_of(kb * BLOCK, BLOCK), BLOCK)
                same = gk_ref[kh, krows, :] == gq_ref[qh, :, qrows]
                bias = jnp.where(same, 0.0, masked_score)
                for t in range(tiles):
                    tat = slice(128 * t, 128 * t + 128)
                    v = v_ref[kh, krows, tat]
                    dc = dc_ref[qh, qrows, tat]
                    from_pair = []
                    for side in range(2):
                        h = 2 * t + side
                        at = slice(128 * h, 128 * h + 128)
                        q = qp_ref[qh, qrows, at]
                        s = nt(km_ref[kh, krows, at], q) + bias
                        p = jnp.exp(s - lse_ref[h : h + 1, cols])
                        zero = jnp.zeros_like(v)
                        vm = jnp.where(lo, v, zero) if side == 0 else jnp.where(lo, zero, v)
                        dp = nt(vm, dc)
                        ds = (p * (dp - delta_sc[h : h + 1, :])).astype(bf16)
                        dk_sc[drows, at] += nn(ds, q)
                        dqt_sc[at, :] += nn(kmt_ref[kh, at, krows], ds)
                        from_pair.append(nn(p.astype(bf16), dc))
                    dv_sc[drows, tat] += jnp.where(lo, from_pair[0], from_pair[1])

        dq = dqt_sc[...].T * 0.125
        entity = kind_ref[qh, qrows, :] == 1
        d_ref[qh, qrows, 0:width] = jnp.where(entity, 0.0, dq).astype(bf16)
        d_ref[qh, qrows, width : 2 * width] = jnp.where(entity, dq, 0.0).astype(bf16)

    @pl.loop(0, blocks)
    def _(kb):
        kh, ko = place(kb, per)
        krows = pl.ds(ko, BLOCK)
        drows = pl.ds(pl.multiple_of(kb * BLOCK, BLOCK), BLOCK)
        entity = kind_ref[kh, krows, :] == 1
        for t in range(tiles):
            even = dk_sc[drows, 256 * t : 256 * t + 128]
            odd = dk_sc[drows, 256 * t + 128 : 256 * t + 256]
            left = jnp.where(entity, pltpu.roll(even, 64, 1), even)
            right = jnp.where(entity, odd, pltpu.roll(odd, 64, 1))
            d_ref[kh, krows, 2 * width + 128 * t : 2 * width + 128 * t + 128] = jnp.where(
                lo, left, right
            ).astype(bf16)
        d_ref[kh, krows, 2 * width + half : 3 * width] = dv_sc[drows, :].astype(bf16)
        db_ref[0:1, :] += jnp.sum(d_ref[kh, krows, :].astype(f32), axis=0, keepdims=True)


def attend_back(own_groups, other_groups, qp, km, kmt, v, dc, ct, lse, gk, gq, kind_col, micro_at, d_before):
    halves, micro, local, width = qp.shape
    half = width // 2
    heads = width // 128
    length = halves * local

    def one(array):
        rest = array.shape[2:]
        return pl.BlockSpec(
            (array.shape[0], None) + rest, lambda m, *_: (0, micro_at) + (0,) * len(rest)
        )

    before = () if d_before is None else (d_before,)
    return pl.pallas_call(
        functools.partial(attend_back_kernel, micro_at),
        grid_spec=pltpu.PrefetchScalarGridSpec(
            num_scalar_prefetch=2,
            grid=(1,),
            in_specs=[one(a) for a in (qp, km, kmt, v, dc)]
            + [
                pl.BlockSpec((None, half, length), lambda m, *_: (micro_at, 0, 0)),
                pl.BlockSpec((None, 8, length), lambda m, *_: (micro_at, 0, 0)),
            ]
            + [one(a) for a in (gk, gq, kind_col)]
            + [pl.BlockSpec(memory_space=pl.ANY)] * len(before),
            out_specs=[
                pl.BlockSpec((halves, None, local, 3 * width), lambda m, *_: (0, micro_at, 0, 0)),
                pl.BlockSpec((8, 3 * width), lambda m, *_: (0, 0)),
            ],
            scratch_shapes=[
                pltpu.VMEM((width, BLOCK), f32),
                pltpu.VMEM((length, width), f32),
                pltpu.VMEM((length, half), f32),
                pltpu.VMEM((8, BLOCK), f32),
            ],
        ),
        out_shape=[
            jax.ShapeDtypeStruct((halves, micro, local, 3 * width), bf16),
            jax.ShapeDtypeStruct((8, 3 * width), f32),
        ],
        compiler_params=pltpu.CompilerParams(vmem_limit_bytes=VMEM_LIMIT),
        cost_estimate=cost(
            heads * length * length * 1280, length * width * 16, heads * length * length
        ),
        input_output_aliases={12: 0} if before else {},
        name="attend_back",
    )(own_groups, other_groups, qp, km, kmt, v, dc, ct, lse, gk, gq, kind_col, *before)


def norm_forward(hidden):
    center = hidden - jnp.mean(hidden, axis=-1, keepdims=True)
    rescale = lax.rsqrt(jnp.mean(center * center, axis=-1, keepdims=True) + layer_eps)
    return center * rescale, rescale


def norm_backward(upstream, normed, rescale, gain):
    scaled = upstream * gain
    return rescale * (
        scaled
        - jnp.mean(scaled, axis=-1, keepdims=True)
        - normed * jnp.mean(scaled * normed, axis=-1, keepdims=True)
    )


def column_sum(values):
    return jnp.sum(values.astype(f32), axis=0, keepdims=True)


def chain_kernel(
    side_ref,
    x_ref,
    own_ref,
    far_ref,
    cot_ref,
    w_ref,
    vec_ref,
    mixed_ref,
    dh_ref,
    left_ref,
    right_ref,
    dco_ref,
    dcx_ref,
    sums_ref,
    slope_sc,
    z_sc,
    landed,
    c_send,
    c_recv,
):
    width = x_ref.shape[1]
    half = width // 2
    rows = width // GROUPS
    chunks = 4
    first = side_ref[0] == 0

    step_at = pl.program_id(0)
    blocks = landed.shape[0]
    per = far_ref.shape[2] // BLOCK
    across = (1 - lax.axis_index("seq"), lax.axis_index("shard"))

    def far_copy(i):
        return send(
            far_ref.at[1, i // per, pl.ds((i % per) * BLOCK, BLOCK), :],
            landed.at[i],
            c_send.at[i],
            c_recv.at[i],
            across,
        )

    @pl.when(step_at == 0)
    def _():
        sums_ref[...] = jnp.zeros_like(sums_ref)
        greet([across])
        for i in range(blocks):
            far_copy(i).start()

    for i in range(blocks):

        @pl.when(step_at == i)
        def _(i=i):
            far_copy(i).wait_recv()
            if i == blocks - 1:
                for k in range(blocks):
                    far_copy(k).wait_send()

    def vector(at):
        return vec_ref[at : at + 1, :]

    def up_chunk(j):
        at = pl.multiple_of(5 * rows + j * rows, 16)
        return w_ref[:, pl.ds(at, rows), :].reshape(width, width)

    def down_chunk(j):
        return w_ref[pl.ds(j * (GROUPS // chunks), GROUPS // chunks), 0 : 4 * rows, :].reshape(width, width)

    def out_weight():
        return w_ref[:, 4 * rows : 5 * rows, :].reshape(width, width)

    own = own_ref[...].astype(f32)
    other = landed[step_at].astype(f32)
    context = jnp.concatenate(
        [jnp.where(first, own, other), jnp.where(first, other, own)], axis=1
    ).astype(bf16)
    left_ref[:, 0:width] = context
    hidden = x_ref[...].astype(f32) + (nn(context, out_weight()) + vector(0))
    n1, r1 = norm_forward(hidden)
    y1 = n1 * vector(1) + vector(2)
    left_ref[:, width : 2 * width] = y1.astype(bf16)
    z_sc[...] = y1 + vector(7)

    @pl.loop(0, chunks)
    def _(j):
        u = nn(left_ref[:, width : 2 * width], up_chunk(j)) + vec_ref[pl.ds(j + 3, 1), :]
        cumulative = 0.5 * (1.0 + lax.erf(u * 0.7071067811865476))
        at = pl.multiple_of(j * width, 128)
        slope_sc[:, pl.ds(at, width)] = (
            cumulative + u * jnp.exp(-0.5 * u * u) * 0.3989422804014327
        )
        g = (u * cumulative).astype(bf16)
        left_ref[:, pl.ds(pl.multiple_of(at + 2 * width, 128), width)] = g
        z_sc[...] += nn(g, down_chunk(j))

    n2, r2 = norm_forward(z_sc[...])
    mixed_ref[...] = (n2 * vector(8) + vector(9)).astype(bf16)
    upstream = cot_ref[...].astype(f32)
    sums_ref[0:1, :] += column_sum(upstream * n2)
    sums_ref[1:2, :] += column_sum(upstream)
    dh2 = norm_backward(upstream, n2, r2, vector(8))
    dz = dh2.astype(bf16)
    right_ref[:, 5 * width :] = dz
    sums_ref[2:3, :] += column_sum(dz)
    z_sc[...] = dh2

    @pl.loop(0, chunks)
    def _(j):
        at = pl.multiple_of(j * width, 128)
        du = (
            nt(right_ref[:, 5 * width :], down_chunk(j)) * slope_sc[:, pl.ds(at, width)]
        ).astype(bf16)
        right_ref[:, pl.ds(pl.multiple_of(at + width, 128), width)] = du
        sums_ref[pl.ds(j + 8, 1), :] += column_sum(du)
        z_sc[...] += nt(du, up_chunk(j))

    dy1 = z_sc[...]
    hidden = x_ref[...].astype(f32) + (nn(left_ref[:, 0:width], out_weight()) + vector(0))
    n1, r1 = norm_forward(hidden)
    sums_ref[3:4, :] += column_sum(dy1 * n1)
    sums_ref[4:5, :] += column_sum(dy1)
    dh1 = norm_backward(dy1, n1, r1, vector(1))
    dh_ref[...] = dh1
    da = dh1.astype(bf16)
    right_ref[:, 0:width] = da
    sums_ref[5:6, :] += column_sum(da)
    dc = nt(da, out_weight())
    dco_ref[...] = jnp.where(first, dc[:, :half], dc[:, half:]).astype(bf16)
    dcx_ref[...] = jnp.where(first, dc[:, half:], dc[:, :half]).astype(bf16)


def chain(side, x, c, cot, weights, vectors):
    tokens, width = x.shape
    half = width // 2
    per = c.shape[2] // BLOCK
    blocks = tokens // BLOCK

    def rows_spec(cols):
        return pl.BlockSpec((BLOCK, cols), lambda i, *_: (i, 0))

    def shape(cols, kind):
        return jax.ShapeDtypeStruct((tokens, cols), kind)

    return pl.pallas_call(
        chain_kernel,
        grid_spec=pltpu.PrefetchScalarGridSpec(
            num_scalar_prefetch=1,
            grid=(tokens // BLOCK,),
            in_specs=[
                rows_spec(width),
                pl.BlockSpec((None, None, BLOCK, half), lambda i, *_: (0, i // per, i % per, 0)),
                pl.BlockSpec(memory_space=pl.ANY),
                rows_spec(width),
                pl.BlockSpec(weights.shape, lambda i, *_: (0, 0, 0), pipeline_mode=pl.Buffered(1)),
                pl.BlockSpec(vectors.shape, lambda i, *_: (0, 0)),
            ],
            out_specs=[
                rows_spec(width),
                rows_spec(width),
                rows_spec(6 * width),
                rows_spec(6 * width),
                rows_spec(half),
                rows_spec(half),
                pl.BlockSpec((16, width), lambda i, *_: (0, 0)),
            ],
            scratch_shapes=[
                pltpu.VMEM((BLOCK, 4 * width), f32),
                pltpu.VMEM((BLOCK, width), f32),
                pltpu.VMEM((blocks, BLOCK, half), bf16),
                pltpu.SemaphoreType.DMA((blocks,)),
                pltpu.SemaphoreType.DMA((blocks,)),
            ],
        ),
        out_shape=[
            shape(width, bf16),
            shape(width, f32),
            shape(6 * width, bf16),
            shape(6 * width, bf16),
            shape(half, bf16),
            shape(half, bf16),
            jax.ShapeDtypeStruct((16, width), f32),
        ],
        compiler_params=pltpu.CompilerParams(
            collective_id=3, has_side_effects=True, vmem_limit_bytes=VMEM_LIMIT
        ),
        cost_estimate=cost(2 * tokens * width * width * 19, tokens * width * 36 + weights.size * 2),
        name="chain",
    )(side[None], x, c, c, cot, weights, vectors)


def feed_grad_kernel(l_ref, r_ref, out_ref):
    width = l_ref.shape[1]
    rows = width // GROUPS
    at = pl.program_id(0)
    grad = tn(l_ref[...], r_ref[...]).astype(bf16)

    @pl.when(at == 0)
    def _():
        out_ref[:, 4 * rows : 5 * rows, :] = grad.reshape(GROUPS, rows, width)

    @pl.when((at >= 1) & (at < 5))
    def _():
        start = pl.multiple_of(5 * rows + (at - 1) * rows, 16)
        out_ref[:, pl.ds(start, rows), :] = grad.reshape(GROUPS, rows, width)

    @pl.when(at >= 5)
    def _():
        out_ref[pl.ds((at - 5) * 4, 4), 0 : 4 * rows, :] = grad.reshape(4, 4 * rows, width)


def chip_grad_kernel(l_ref, r_ref, keep_ref, give_ref, part, from_core, c_send, c_recv):
    width = l_ref.shape[1]
    rows = width // GROUPS
    at = pl.program_id(0)
    x, _, z, y, core = spots()
    partner = (x, slot_of(z, y, 1 - core))
    spans = [(slice(0, 8), 4 * rows + i * rows, rows) for i in range(5)]
    spans += [(slice(2 * j, 2 * j + 2), 0, 4 * rows) for j in range(4)]

    def copy_of(i):
        rails, start, size = spans[i]
        return send(
            part.at[rails, 1 - core, slice(start, start + size), :],
            from_core.at[rails, slice(start, start + size), :],
            c_send.at[i],
            c_recv.at[i],
            partner,
        )

    def add(i):
        rails, start, size = spans[i]
        copy_of(i).wait_recv()
        for rail in range(rails.start, rails.stop):
            mine = part[rail, core, start : start + size, :].astype(f32)
            theirs = from_core[rail, start : start + size, :].astype(f32)
            whole = mine + theirs
            left, right = whole[:, : width // 2], whole[:, width // 2 :]
            keep_ref[rail, start : start + size, :] = jnp.where(x == 0, left, right).astype(bf16)
            give_ref[rail, start : start + size, :] = jnp.where(x == 0, right, left).astype(bf16)

    @pl.when(at == 0)
    def _():
        greet([partner])

    grad = tn(l_ref[...], r_ref[...]).astype(bf16)
    for i in range(9):

        @pl.when(at == i)
        def _(i=i):
            rails, start, size = spans[i]
            count = rails.stop - rails.start
            part[rails, :, start : start + size, :] = grad.reshape(count, 2, size, width)
            copy_of(i).start()
            if i >= 2:
                add(i - 2)
            if i == 8:
                add(7)
                add(8)
                for k in range(9):
                    copy_of(k).wait_send()


def feed_grad(left, right, direct):
    tokens = left.shape[0]
    width = left.shape[1] // 6
    rows = width // GROUPS

    def left_at(i):
        return (0, jnp.where(i == 0, 0, jnp.where(i < 5, 1, i - 3)))

    def right_at(i):
        return (0, jnp.minimum(i, 5))

    out = (8, 9 * rows, width // 2) if direct else (GROUPS, 9 * rows, width)
    count = 2 if direct else 1
    scratch = [
        pltpu.VMEM((8, 2, 9 * rows, width), bf16),
        pltpu.VMEM((8, 9 * rows, width), bf16),
        pltpu.SemaphoreType.DMA((9,)),
        pltpu.SemaphoreType.DMA((9,)),
    ]
    extra = dict(collective_id=2, has_side_effects=True) if direct else {}
    return pl.pallas_call(
        chip_grad_kernel if direct else feed_grad_kernel,
        grid=(9,),
        in_specs=[
            pl.BlockSpec((tokens, width), left_at),
            pl.BlockSpec((tokens, width), right_at),
        ],
        out_specs=[pl.BlockSpec(out, lambda i: (0, 0, 0))] * count,
        out_shape=[jax.ShapeDtypeStruct(out, bf16)] * count,
        scratch_shapes=scratch if direct else (),
        compiler_params=pltpu.CompilerParams(vmem_limit_bytes=VMEM_LIMIT, **extra),
        cost_estimate=cost(2 * tokens * width * width * 9, tokens * width * 24 + width * width * 18),
        name="feed_grad",
    )(left, right)


def attn_grad_kernel(x_ref, d_ref, vec_ref, out_ref):
    width = x_ref.shape[1]
    rows = width // GROUPS
    at = pl.program_id(0)
    grad = tn(x_ref[...], d_ref[...]).astype(bf16)
    start = pl.multiple_of(at * rows, 16)
    out_ref[:, pl.ds(start, rows), :] = grad.reshape(GROUPS, rows, width)
    out_ref[:, 3 * rows :, :] = vec_ref[...]


def attn_grad(x, d, vectors):
    tokens, width = x.shape
    rows = width // GROUPS
    return pl.pallas_call(
        attn_grad_kernel,
        grid=(3,),
        in_specs=[
            pl.BlockSpec((tokens, width), lambda i: (0, 0)),
            pl.BlockSpec((tokens, width), lambda i: (0, i)),
            pl.BlockSpec((GROUPS, 16, width), lambda i: (0, 0, 0)),
        ],
        out_specs=pl.BlockSpec((GROUPS, 3 * rows + 16, width), lambda i: (0, 0, 0)),
        out_shape=jax.ShapeDtypeStruct((GROUPS, 3 * rows + 16, width), bf16),
        compiler_params=pltpu.CompilerParams(vmem_limit_bytes=VMEM_LIMIT),
        cost_estimate=cost(2 * tokens * width * width * 3, tokens * width * 8 + width * width * 6),
        name="attn_grad",
    )(x, d, vectors)


def scatter_kernel(
    x_ref,
    d_ref,
    vec_ref,
    w_ref,
    dh_ref,
    dx_ref,
    gq_ref,
    gk_ref,
    gv_ref,
    gvec_ref,
    part,
    from_core,
    from_y,
    from_z,
    from_x,
    out_y,
    out_z,
    held,
    total,
    dx_out,
    from_dx,
    d_send,
    d_recv,
    c_send,
    c_recv,
    y_send,
    y_recv,
    z_send,
    z_recv,
    x_send,
    x_recv,
):
    width = x_ref.shape[1]
    half = width // 2
    rows = width // GROUPS
    step_at = pl.program_id(0)
    x, me, z, y, core = spots()
    across = (1 - x, me)
    beside = (x, slot_of(z, 1 - y, core))
    partner = (x, slot_of(z, y, 1 - core))
    spans = ((0, rows), (rows, rows), (2 * rows, rows + 16))

    def core_copy(chunk, rail):
        start, size = spans[chunk]
        return send(
            part.at[2 * rail + 1 - core, pl.ds(start, size), :],
            from_core.at[rail, pl.ds(start, size), :],
            c_send.at[chunk * 8 + rail],
            c_recv.at[chunk * 8 + rail],
            partner,
        )

    @pl.when(step_at == 0)
    def _():
        greet(all_peers())

    columns = pl.ds(pl.multiple_of(step_at * width, 128), width)
    grad = tn(x_ref[...], d_ref[:, columns]).astype(bf16)
    for chunk in range(3):

        @pl.when(step_at == chunk)
        def _(chunk=chunk):
            start = spans[chunk][0]
            part[:, start : start + rows, :] = grad.reshape(GROUPS, rows, width)
            if chunk == 2:
                part[:, 3 * rows :, :] = vec_ref[...]
            for rail in range(8):
                core_copy(chunk, rail).start()

    flat = dh_ref.shape[0]

    def input_part(start):
        found = None
        for i in range(3):
            piece = nt(
                d_ref[pl.ds(pl.multiple_of(start, BLOCK), BLOCK), i * width : i * width + width],
                w_ref[:, i * rows : i * rows + rows, :].reshape(width, width),
            )
            found = piece if found is None else found + piece
        return found

    @pl.when(step_at == 2)
    def _():
        def z_order(step):
            return lax.rem(z + 1 + step, 4)

        def y_copy(zz):
            return send(out_y.at[zz], from_y.at[zz], y_send.at[zz], y_recv.at[zz], beside)

        def z_copy(zz):
            return send(
                out_z.at[zz], from_z.at[z], z_send.at[zz], z_recv.at[z], (x, slot_of(zz, y, core))
            )

        def core_wait(rail):
            for chunk in range(3):
                start, size = spans[chunk]
                send(
                    part.at[0, pl.ds(start, size), :],
                    from_core.at[rail, pl.ds(start, size), :],
                    c_send.at[0],
                    c_recv.at[chunk * 8 + rail],
                    partner,
                ).wait_recv()

        for step in range(4):
            zz = z_order(step)
            rail = zz * 2 + 1 - y
            core_wait(rail)
            out_y[zz] = (part[2 * rail + core].astype(f32) + from_core[rail].astype(f32)).astype(bf16)
            y_copy(zz).start()

        @pl.loop(0, flat // BLOCK)
        def _(i):
            at = pl.ds(pl.multiple_of(i * BLOCK, BLOCK), BLOCK)
            dx_out[at, :] = input_part(flat + i * BLOCK).astype(bf16)

        exchange = send(dx_out, from_dx, d_send, d_recv, across)
        exchange.start()
        for step in range(4):
            zz = z_order(step)
            rail = zz * 2 + y
            core_wait(rail)
            held[zz] = part[2 * rail + core].astype(f32) + from_core[rail].astype(f32)
        for step in range(3):
            zz = z_order(step)
            y_copy(zz).wait_recv()
            out_z[zz] = (held[zz] + from_y[zz].astype(f32)).astype(bf16)
            z_copy(zz).start()

        @pl.loop(0, flat // BLOCK)
        def _(i):
            at = pl.ds(pl.multiple_of(i * BLOCK, BLOCK), BLOCK)
            dx_ref[at, :] = dh_ref[at, :] + input_part(i * BLOCK)

        y_copy(z).wait_recv()
        result = held[z] + from_y[z].astype(f32)
        for step in range(3):
            zz = z_order(step)
            send(out_z.at[zz], from_z.at[zz], z_send.at[zz], z_recv.at[zz], partner).wait_recv()
            result = result + from_z[zz].astype(f32)
        total[...] = result.astype(bf16)
        last = send(total, from_x, x_send, x_recv, across)
        last.start()
        exchange.wait()

        @pl.loop(0, flat // BLOCK)
        def _(i):
            at = pl.ds(pl.multiple_of(i * BLOCK, BLOCK), BLOCK)
            dx_ref[at, :] += from_dx[at, :].astype(f32)

        for chunk in range(3):
            for rail in range(8):
                core_copy(chunk, rail).wait_send()
        for step in range(4):
            y_copy(z_order(step)).wait_send()
        for step in range(3):
            z_copy(z_order(step)).wait_send()
        last.wait()
        first = x == 0
        lo = low_lanes((rows, 128))

        def ordered(start, size, at):
            own = total[start : start + size, at].astype(f32)
            other = from_x[start : start + size, at].astype(f32)
            return jnp.where(first, own, other), jnp.where(first, other, own)

        for e in range(2):
            for t in range(half // 128):
                evens = ordered(e * rows, rows, slice(256 * t, 256 * t + 128))
                odds = ordered(e * rows, rows, slice(256 * t + 128, 256 * t + 256))
                for s in range(2):
                    word = jnp.where(lo, evens[s], pltpu.roll(odds[s], 64, 1))
                    entity = jnp.where(lo, pltpu.roll(evens[s], 64, 1), odds[s])
                    base = 2 * e * width + s * half + 128 * t
                    gq_ref[:, base : base + 128] = word
                    gq_ref[:, base + width : base + width + 128] = entity
        for ref, base in ((gk_ref, 0), (gv_ref, half)):
            a, b = ordered(2 * rows, rows, slice(base, base + half))
            ref[:, :half] = a
            ref[:, half:] = b
        gvec_ref[...] = total[3 * rows :, :].astype(f32) + from_x[3 * rows :, :].astype(f32)


def scatter_attention(x, d, vectors, weights, dh):
    tokens, width = x.shape
    rows = width // GROUPS
    tall = 3 * rows + 16
    sem = pltpu.SemaphoreType.DMA

    def whole(*dims):
        return pl.BlockSpec(dims, lambda i: (0,) * len(dims), pipeline_mode=pl.Buffered(1))

    outs = (dh.shape, (rows, 4 * width), (rows, width), (rows, width), (16, width))
    return pl.pallas_call(
        scatter_kernel,
        grid=(3,),
        in_specs=[
            whole(tokens, width),
            whole(*d.shape),
            whole(GROUPS, 16, width),
            whole(*weights.shape),
            whole(*dh.shape),
        ],
        out_specs=[whole(*dims) for dims in outs],
        out_shape=[jax.ShapeDtypeStruct(dims, f32) for dims in outs],
        scratch_shapes=[
            pltpu.VMEM((GROUPS, tall, width), bf16),
            pltpu.VMEM((8, tall, width), bf16),
            pltpu.VMEM((4, tall, width), bf16),
            pltpu.VMEM((4, tall, width), bf16),
            pltpu.VMEM((tall, width), bf16),
            pltpu.VMEM((4, tall, width), bf16),
            pltpu.VMEM((4, tall, width), bf16),
            pltpu.VMEM((4, tall, width), f32),
            pltpu.VMEM((tall, width), bf16),
            pltpu.VMEM(dh.shape, bf16),
            pltpu.VMEM(dh.shape, bf16),
            sem,
            sem,
            sem((24,)),
            sem((24,)),
            sem((4,)),
            sem((4,)),
            sem((4,)),
            sem((4,)),
            sem,
            sem,
        ],
        compiler_params=pltpu.CompilerParams(
            collective_id=1, has_side_effects=True, vmem_limit_bytes=VMEM_LIMIT
        ),
        cost_estimate=cost(2 * tokens * width * width * 3, tokens * width * 8 + width * width * 6),
        name="scatter",
    )(x, d, vectors, weights, dh)


def input_grad_kernel(d_ref, w_ref, out_ref):
    width = out_ref.shape[1]
    rows = width // GROUPS
    total = None
    for i in range(3):
        part = nt(
            d_ref[:, i * width : i * width + width],
            w_ref[:, i * rows : i * rows + rows, :].reshape(width, width),
        )
        total = part if total is None else total + part
    out_ref[...] = total.astype(out_ref.dtype)


def input_grad_part(d, weights, side_at, kind):
    _, micro, local, wide = d.shape
    width = wide // 3
    sub = local // BLOCK
    return pl.pallas_call(
        input_grad_kernel,
        grid=(micro, sub),
        in_specs=[
            pl.BlockSpec((None, None, BLOCK, wide), lambda m, i: (side_at, m, i, 0)),
            pl.BlockSpec(weights.shape, lambda m, i: (0, 0, 0)),
        ],
        out_specs=pl.BlockSpec((None, BLOCK, width), lambda m, i: (m, i, 0)),
        out_shape=jax.ShapeDtypeStruct((micro, local, width), kind),
        compiler_params=pltpu.CompilerParams(vmem_limit_bytes=VMEM_LIMIT),
        cost_estimate=cost(2 * micro * local * wide * width, micro * local * wide * 2 + weights.size * 2),
        name="input_grad",
    )(d, weights)


def assemble(attn_own, attn_other, side, head_dim, rows, piece):
    attn_own, attn_other = attn_own.astype(f32), attn_other.astype(f32)
    width = attn_own.shape[1]
    half = width // 2
    vec_total = attn_own[3 * rows, :piece] + attn_other[3 * rows, :piece]

    def by_side(own, other, axis):
        return jnp.where(
            side == 0,
            jnp.concatenate([own, other], axis=axis),
            jnp.concatenate([other, own], axis=axis),
        )

    def query_parts(block):
        pairs = jnp.stack([block[:rows], block[rows : 2 * rows]], axis=1)
        return unpair_columns(pairs, head_dim)

    grad_query = by_side(query_parts(attn_own), query_parts(attn_other), 3).reshape(rows, 4 * width)
    kv_own, kv_other = attn_own[2 * rows : 3 * rows], attn_other[2 * rows : 3 * rows]
    grad_key = by_side(kv_own[:, :half], kv_other[:, :half], 1)
    grad_value = by_side(kv_own[:, half:], kv_other[:, half:], 1)
    return grad_query, grad_key, grad_value, vec_total


def on_device(
    tokens,
    kinds,
    groups,
    query_weight,
    query_bias,
    key_weight,
    key_bias,
    value_weight,
    value_bias,
    output_weight,
    output_bias,
    norm1_gain,
    norm1_shift,
    up_weight,
    up_bias,
    down_weight,
    down_bias,
    norm2_gain,
    norm2_shift,
    cotangent,
):
    micro, _, local, width = tokens.shape
    half = width // 2
    head_dim = width // HEADS
    devices = lax.axis_size("shard")
    rows = width // devices
    side = lax.axis_index("seq").astype(jnp.int32)

    vectors = (
        query_bias,
        key_bias,
        value_bias,
        output_bias,
        norm1_gain,
        norm1_shift,
        up_bias,
        down_bias,
        norm2_gain,
        norm2_shift,
    )
    piece = 16 * rows
    direct = devices == GROUPS
    attn_sizes = (rows, rows, rows)
    feed_sizes = (4 * rows,) + (rows,) * 5
    if not direct:
        vector_row = jnp.pad(jnp.concatenate(vectors), (0, width - piece))[None]
        packed = pack_attention(query_weight, key_weight, value_weight, vector_row, side, head_dim)
        attn_gathered = lax.all_gather(packed[None], "shard", axis=0, tiled=True)
        other_tokens, other_kinds, other_groups = swap(tokens), swap(kinds), swap(groups)
    feed_local = pack_feed(down_weight, output_weight, up_weight)
    feed_gathered = lax.all_gather(feed_local[None], "shard", axis=0, tiled=True)
    if direct:
        attn_gathered, other_tokens, other_kinds, other_groups = gather_attention(
            query_weight, key_weight, value_weight, vectors, tokens, kinds, groups
        )
    vectors = attn_gathered[:, 3 * rows, :piece]
    if direct:
        attn_w, feed_w = attn_gathered, feed_gathered
    else:
        attn_w = regroup(attn_gathered, attn_sizes)
        feed_w = regroup(feed_gathered, feed_sizes)

    def whole_vector(start, size):
        return vectors[:, start : start + size].reshape(-1).astype(f32)

    full_query_bias = whole_vector(0, 4 * rows)
    full_key_bias = whole_vector(4 * rows, rows)
    full_value_bias = whole_vector(5 * rows, rows)
    bias_rows = jnp.concatenate(
        [
            pair_columns(full_query_bias, side, head_dim),
            jnp.concatenate([own_half(full_key_bias, side), own_half(full_value_bias, side)])[None],
        ],
        axis=0,
    )
    full_up_bias = whole_vector(9 * rows, 4 * rows).reshape(4, width)
    chain_vectors = jnp.concatenate(
        [
            whole_vector(6 * rows, rows)[None],
            whole_vector(7 * rows, rows)[None],
            whole_vector(8 * rows, rows)[None],
            full_up_bias,
            whole_vector(13 * rows, rows)[None],
            whole_vector(14 * rows, rows)[None],
            whole_vector(15 * rows, rows)[None],
        ],
        axis=0,
    )

    own_tokens = tokens[:, 0]
    own_groups, far_groups = groups.reshape(micro, local), other_groups.reshape(micro, local)
    qp, km, kmt, v, vt, xs, kind_col, gk, gq = project(
        tokens, other_tokens, kinds, other_kinds, groups, other_groups, attn_w, bias_rows
    )
    c, ct, lse = attend(own_groups, far_groups, qp, km, vt, gk, gq)
    flat = micro * local
    mixed, dh1, left, right, dc_own, dc_other, sums = chain(
        side,
        own_tokens.reshape(flat, width),
        c,
        cotangent.reshape(flat, width),
        feed_w,
        chain_vectors,
    )

    dc_swapped = swap(dc_other)
    feed_part = feed_grad(left, right, direct)
    dc_swapped, feed_part = lax.optimization_barrier((dc_swapped, feed_part))
    dc = jnp.stack([dc_own, dc_swapped]).reshape(2, micro, local, half)

    def mix_back(micro_at, before):
        return attend_back(
            own_groups, far_groups, qp, km, kmt, v, dc, ct, lse, gk, gq, kind_col, micro_at, before
        )

    d, db = None, 0.0
    for m in range(micro - 1):
        d, part = mix_back(m, d)
        db = db + part
    rails = None
    if direct:
        rails = [[2 * rail + core for rail in range(8)] for core in range(2)]
        keep, give = feed_part
        taken, d = lax.optimization_barrier((swap(give), d))
        feed_part = (keep.astype(f32) + taken.astype(f32)).astype(bf16)
    else:
        feed_part = ungroup(feed_part[0], feed_sizes, devices)
    feed_sum = lax.psum_scatter(
        feed_part, "shard", scatter_dimension=0, axis_index_groups=rails, tiled=True
    )[0]
    d, part = mix_back(micro - 1, d)
    db = db + part

    query_own = unpair_columns(db[0, : 2 * width].reshape(2, width), head_dim)
    zero = jnp.zeros((half,), f32)

    def spread(own):
        return jnp.where(side == 0, jnp.concatenate([own, zero]), jnp.concatenate([zero, own]))

    query_spread = jnp.concatenate([spread(query_own[e, w]) for e in range(2) for w in range(2)])
    key_spread = spread(db[0, 2 * width : 2 * width + half])
    value_spread = spread(db[0, 2 * width + half :])
    grad_vectors = jnp.concatenate(
        [
            query_spread.reshape(devices, 4 * rows),
            key_spread.reshape(devices, rows),
            value_spread.reshape(devices, rows),
            sums[5].reshape(devices, rows),
            sums[3].reshape(devices, rows),
            sums[4].reshape(devices, rows),
            sums[8:12].reshape(devices, 4 * rows),
            sums[2].reshape(devices, rows),
            sums[0].reshape(devices, rows),
            sums[1].reshape(devices, rows),
        ],
        axis=1,
    ).astype(bf16)
    grad_vectors = jnp.pad(grad_vectors[:, None, :], ((0, 0), (0, 15), (0, width - piece)))
    flat_x = xs.reshape(2 * flat, width)
    flat_d = d.reshape(2 * flat, 3 * width)
    if direct:
        input_grad, grad_query, grad_key, grad_value, vec_rows = scatter_attention(
            flat_x, flat_d, grad_vectors, attn_w, dh1
        )
        input_grad = input_grad.reshape(micro, local, width)
        vec_total = vec_rows[0, :piece]
    else:
        zeros = jnp.zeros((GROUPS, 16, width), bf16)
        attn_part = attn_grad(flat_x, flat_d, zeros)
        attn_part = jnp.concatenate(
            [ungroup(attn_part[:, : 3 * (width // GROUPS)], attn_sizes, devices), grad_vectors], axis=1
        )
        attn_sum = lax.psum_scatter(attn_part, "shard", scatter_dimension=0, tiled=True)[0]
        attn_other = swap(attn_sum)
        grad_query, grad_key, grad_value, vec_total = assemble(
            attn_sum, attn_other, side, head_dim, rows, piece
        )
        dx_other = input_grad_part(d, attn_w, 1, bf16)
        dx_own = input_grad_part(d, attn_w, 0, f32)
        input_grad = dh1.reshape(micro, local, width) + dx_own + swap(dx_other).astype(f32)

    feed_other = swap(feed_sum)
    if direct:
        feed_total = jnp.where(
            side == 0,
            jnp.concatenate([feed_sum, feed_other], axis=1),
            jnp.concatenate([feed_other, feed_sum], axis=1),
        ).astype(f32)
    else:
        feed_total = feed_sum.astype(f32) + feed_other.astype(f32)
    grad_down = feed_total[: 4 * rows]
    grad_output = feed_total[4 * rows : 5 * rows]
    grad_up = jnp.concatenate(
        [feed_total[(5 + j) * rows : (6 + j) * rows] for j in range(4)], axis=1
    )

    def piece_of(start, size):
        return vec_total[start : start + size]

    return (
        mixed.reshape(micro, 1, local, width),
        input_grad[:, None],
        grad_query,
        piece_of(0, 4 * rows),
        grad_key,
        piece_of(4 * rows, rows),
        grad_value,
        piece_of(5 * rows, rows),
        grad_output,
        piece_of(6 * rows, rows),
        piece_of(7 * rows, rows),
        piece_of(8 * rows, rows),
        grad_up,
        piece_of(9 * rows, 4 * rows),
        grad_down,
        piece_of(13 * rows, rows),
        piece_of(14 * rows, rows),
        piece_of(15 * rows, rows),
    )


def solution(mesh):
    weight = P("shard", None)
    vector = P("shard")
    tokens = P(None, "shard", "seq", None)
    marks = P(None, "shard", "seq")
    return jax.shard_map(
        on_device,
        mesh=mesh,
        in_specs=(tokens, marks, marks)
        + (weight, vector) * 4
        + (vector, vector)
        + (weight, vector) * 2
        + (vector, vector)
        + (tokens,),
        out_specs=(tokens, tokens)
        + (weight, vector) * 4
        + (vector, vector)
        + (weight, vector) * 2
        + (vector, vector),
        check_vma=False,
    )
```

```python
import jax
import jax.numpy as jnp
from jax import lax
from jax.experimental import pallas as pl
from jax.experimental.pallas import tpu as pltpu
from jax.sharding import PartitionSpec as P


HEADS = 12
GROUPS = 16
BLOCK = 256
masked_score = -1e30
layer_eps = 1e-12
bf16 = jnp.bfloat16
f32 = jnp.float32
VMEM_LIMIT = 60 * 1024 * 1024


def nn(a, b):
    return lax.dot_general(a, b, (((1,), (0,)), ((), ())), preferred_element_type=f32)


def nt(a, b):
    return lax.dot_general(a, b, (((1,), (1,)), ((), ())), preferred_element_type=f32)


def tn(a, b):
    return lax.dot_general(a, b, (((0,), (0,)), ((), ())), preferred_element_type=f32)


def swap(value):
    return lax.ppermute(value, "seq", [(0, 1), (1, 0)])


def cost(flops, moved, trans=0):
    return pl.CostEstimate(flops=flops, bytes_accessed=moved, transcendentals=trans)


def low_lanes(shape):
    return lax.broadcasted_iota(jnp.int32, shape, len(shape) - 1) % 128 < 64


def pack_into(first, q_ref, k_ref, v_ref, vec, out_ref):
    rows, width = k_ref.shape
    half = width // 2

    def own(ref, base):
        return jnp.where(
            first,
            ref[:, base : base + half].astype(f32),
            ref[:, base + half : base + width].astype(f32),
        )

    lo = low_lanes((rows, 128))
    for e in range(2):
        word = own(q_ref, 2 * e * width)
        entity = own(q_ref, (2 * e + 1) * width)
        for t in range(half // 128):
            a = word[:, 128 * t : 128 * t + 128]
            b = entity[:, 128 * t : 128 * t + 128]
            even = jnp.where(lo, a, pltpu.roll(b, 64, 1))
            odd = jnp.where(lo, pltpu.roll(a, 64, 1), b)
            out_ref[e * rows : e * rows + rows, 256 * t : 256 * t + 128] = even.astype(bf16)
            out_ref[e * rows : e * rows + rows, 256 * t + 128 : 256 * t + 256] = odd.astype(bf16)
    out_ref[2 * rows : 3 * rows, :half] = own(k_ref, 0).astype(bf16)
    out_ref[2 * rows : 3 * rows, half:] = own(v_ref, 0).astype(bf16)
    out_ref[3 * rows :, :] = jnp.broadcast_to(vec, (16, width)).astype(bf16)


def spots():
    x = lax.axis_index("seq")
    me = lax.axis_index("shard")
    core = lax.rem(me, 2)
    y = lax.rem(me // 2, 2)
    z = me // 4
    return x, me, z, y, core


def slot_of(z, y, core):
    return z * 4 + y * 2 + core


def greet(peers):
    barrier = pltpu.get_barrier_semaphore()
    for peer in peers:
        pl.semaphore_signal(barrier, inc=1, device_id=peer, device_id_type=pl.DeviceIdType.MESH)
    pl.semaphore_wait(barrier, len(peers))


def all_peers():
    x, me, z, y, core = spots()
    peers = [(x, slot_of(z, y, 1 - core)), (x, slot_of(z, 1 - y, core)), (1 - x, me)]
    for step in range(1, 4):
        peers.append((x, slot_of(lax.rem(z + step, 4), y, core)))
    return peers


def send(src, dst, send_sem, recv_sem, device):
    return pltpu.make_async_remote_copy(
        src_ref=src,
        dst_ref=dst,
        send_sem=send_sem,
        recv_sem=recv_sem,
        device_id=device,
        device_id_type=pl.DeviceIdType.MESH,
    )


def gather_kernel(*refs):
    q_ref, k_ref, v_ref = refs[:3]
    vec_refs = refs[3:13]
    tok_ref, kinds_ref, groups_ref = refs[13:16]
    w_ref, tok_out, kinds_out, groups_out = refs[16:20]
    mine, keep_sem, x_send, x_recv, z_send, z_recv, y_send, y_recv, c_send, c_recv = refs[20:]
    x, me, z, y, core = spots()
    across = (1 - x, me)
    beside = (x, slot_of(z, 1 - y, core))
    partner = (x, slot_of(z, y, 1 - core))
    greet(all_peers())
    over = [
        send(src, dst, x_send.at[i], x_recv.at[i], across)
        for i, (src, dst) in enumerate(
            ((kinds_ref, kinds_out), (groups_ref, groups_out), (tok_ref, tok_out))
        )
    ]
    for copy in over:
        copy.start()
    vec = jnp.concatenate([r[...].astype(f32) for r in vec_refs], axis=1)
    pack_into(x == 0, q_ref, k_ref, v_ref, vec, mine)
    started = []
    for step in range(1, 4):
        copy = send(
            mine,
            w_ref.at[me],
            z_send.at[step - 1],
            z_recv.at[z],
            (x, slot_of(lax.rem(z + step, 4), y, core)),
        )
        copy.start()
        started.append(copy)
    copy = send(mine, w_ref.at[me], y_send.at[z], y_recv.at[z], beside)
    copy.start()
    started.append(copy)
    copy = send(mine, w_ref.at[me], c_send.at[z * 2 + y], c_recv.at[z * 2 + y], partner)
    copy.start()
    started.append(copy)
    keep = pltpu.make_async_copy(mine, w_ref.at[me], keep_sem)
    keep.start()
    for step in range(1, 4):
        zz = lax.rem(z + step, 4)
        at = slot_of(zz, y, core)
        held = w_ref.at[at]
        send(held, held, z_send.at[0], z_recv.at[zz], partner).wait_recv()
        for copy in (
            send(held, held, y_send.at[zz], y_recv.at[zz], beside),
            send(held, held, c_send.at[zz * 2 + y], c_recv.at[zz * 2 + y], partner),
        ):
            copy.start()
            started.append(copy)
    for step in range(4):
        zz = lax.rem(z + step, 4)
        rail = zz * 2 + 1 - y
        held = w_ref.at[slot_of(zz, 1 - y, core)]
        send(held, held, y_send.at[0], y_recv.at[zz], partner).wait_recv()
        copy = send(held, held, c_send.at[rail], c_recv.at[rail], partner)
        copy.start()
        started.append(copy)
    for rail in range(8):
        held = w_ref.at[2 * rail + 1 - core]
        send(held, held, c_send.at[0], c_recv.at[rail], partner).wait_recv()
    keep.wait()
    for copy in started:
        copy.wait_send()
    for copy in over:
        copy.wait()


def gather_attention(query_weight, key_weight, value_weight, vectors, tokens, kinds, groups):
    rows, width = key_weight.shape
    vmem = pl.BlockSpec(memory_space=pltpu.VMEM)
    anywhere = pl.BlockSpec(memory_space=pl.ANY)
    sem = pltpu.SemaphoreType.DMA
    return pl.pallas_call(
        gather_kernel,
        in_specs=[vmem] * 13 + [anywhere] * 3,
        out_specs=[anywhere] * 4,
        out_shape=[
            jax.ShapeDtypeStruct((GROUPS, 3 * rows + 16, width), bf16),
            jax.ShapeDtypeStruct(tokens.shape, tokens.dtype),
            jax.ShapeDtypeStruct(kinds.shape, kinds.dtype),
            jax.ShapeDtypeStruct(groups.shape, groups.dtype),
        ],
        scratch_shapes=[
            pltpu.VMEM((3 * rows + 16, width), bf16),
            sem,
            sem((3,)),
            sem((3,)),
            sem((3,)),
            sem((4,)),
            sem((4,)),
            sem((4,)),
            sem((8,)),
            sem((8,)),
        ],
        compiler_params=pltpu.CompilerParams(
            collective_id=0, has_side_effects=True, vmem_limit_bytes=VMEM_LIMIT
        ),
        name="gather",
    )(query_weight, key_weight, value_weight, *[v[None] for v in vectors], tokens, kinds, groups)


def pair_columns(columns, side, head_dim):
    lead = columns.shape[:-1]
    per = columns.shape[-1] // (8 * head_dim)
    view = columns.reshape(lead + (2, 2, 2, per, head_dim))
    view = jnp.where(side == 0, view[..., 0, :, :], view[..., 1, :, :])
    return jnp.swapaxes(view, -3, -2).reshape(lead + (2, -1))


def unpair_columns(pairs, head_dim):
    lead = pairs.shape[:-2]
    per = pairs.shape[-1] // (2 * head_dim)
    view = pairs.reshape(lead + (2, per, 2, head_dim))
    return jnp.swapaxes(view, -3, -2).reshape(lead + (2, 2, per * head_dim))


def own_half(columns, side):
    half = columns.shape[-1] // 2
    return jnp.where(side == 0, columns[..., :half], columns[..., half:])


def pack_attention(query_weight, key_weight, value_weight, vector, side, head_dim):
    width = key_weight.shape[1]
    pairs = pair_columns(query_weight, side, head_dim)
    key_value = jnp.concatenate([own_half(key_weight, side), own_half(value_weight, side)], axis=1)
    return jnp.concatenate(
        [pairs[:, 0], pairs[:, 1], key_value, jnp.broadcast_to(vector, (16, width))], axis=0
    )


def pack_feed_kernel(down_ref, output_ref, up_ref, out_ref):
    rows, width = output_ref.shape
    out_ref[0 : 4 * rows, :] = down_ref[...]
    out_ref[4 * rows : 5 * rows, :] = output_ref[...]
    for j in range(4):
        out_ref[(5 + j) * rows : (6 + j) * rows, :] = up_ref[:, j * width : j * width + width]


def pack_feed(down_weight, output_weight, up_weight):
    rows, width = output_weight.shape
    if rows % 16:
        return jnp.concatenate(
            [down_weight, output_weight]
            + [up_weight[:, j * width : j * width + width] for j in range(4)],
            axis=0,
        )
    vmem = pl.BlockSpec(memory_space=pltpu.VMEM)
    return pl.pallas_call(
        pack_feed_kernel,
        in_specs=[vmem] * 3,
        out_specs=vmem,
        out_shape=jax.ShapeDtypeStruct((9 * rows, width), bf16),
        name="pack_feed",
    )(down_weight, output_weight, up_weight)


def regroup(gathered, sizes):
    _, _, width = gathered.shape
    pieces = []
    start = 0
    for size in sizes:
        piece = gathered[:, start : start + size].reshape(GROUPS, -1, width)
        pieces.append(piece)
        start += size
    return jnp.concatenate(pieces, axis=1)


def ungroup(grouped, sizes, devices):
    _, _, width = grouped.shape
    pieces = []
    start = 0
    for size in sizes:
        wide = size * devices // GROUPS
        pieces.append(grouped[:, start : start + wide].reshape(devices, size, width))
        start += wide
    return jnp.concatenate(pieces, axis=1)


def project_kernel(
    own_ref,
    other_ref,
    own_kind_ref,
    other_kind_ref,
    own_group_ref,
    other_group_ref,
    w_ref,
    bias_ref,
    qp_ref,
    km_ref,
    kmt_ref,
    v_ref,
    vt_ref,
    xs_ref,
    kind_ref,
    gk_ref,
    gq_ref,
):
    width = own_ref.shape[1]
    half = width // 2
    rows = width // GROUPS
    mine = pl.program_id(0) == 0

    def column(row):
        return jnp.broadcast_to(row.astype(f32), (128, BLOCK)).T.astype(jnp.int32)

    x = jnp.where(mine, own_ref[...].astype(f32), other_ref[...].astype(f32)).astype(bf16)
    group = jnp.where(mine, own_group_ref[...], other_group_ref[...])
    kinds = column(jnp.where(mine, own_kind_ref[...], other_kind_ref[...]))
    kind = kinds[:, 0:1]
    xs_ref[...] = x
    kind_ref[...] = kind
    gk_ref[...] = column(group)[:, 0:1]
    gq_ref[...] = group
    wa = w_ref[:, 0:rows, :].reshape(width, width)
    wb = w_ref[:, rows : 2 * rows, :].reshape(width, width)
    wkv = w_ref[:, 2 * rows : 3 * rows, :].reshape(width, width)
    qa = nn(x, wa) + bias_ref[0:1, :]
    qb = nn(x, wb) + bias_ref[1:2, :]
    qp_ref[...] = (jnp.where(kind == 1, qb, qa) * 0.125).astype(bf16)
    kv = nn(x, wkv) + bias_ref[2:3, :]
    lane_high = (lax.broadcasted_iota(jnp.int32, (BLOCK, 128), 1) >= 64).astype(jnp.int32)
    keep = lane_high == kinds
    lo = lane_high == 0
    for t in range(half // 128):
        k = kv[:, 128 * t : 128 * t + 128]
        r = pltpu.roll(k, 64, 1)
        even = jnp.where(keep, jnp.where(lo, k, r), 0.0)
        odd = jnp.where(keep, jnp.where(lo, r, k), 0.0)
        km_ref[:, 256 * t : 256 * t + 128] = even.astype(bf16)
        km_ref[:, 256 * t + 128 : 256 * t + 256] = odd.astype(bf16)
        kmt_ref[256 * t : 256 * t + 128, :] = even.T.astype(bf16)
        kmt_ref[256 * t + 128 : 256 * t + 256, :] = odd.T.astype(bf16)
    v = kv[:, half:]
    v_ref[...] = v.astype(bf16)
    vt_ref[...] = v.T.astype(bf16)


def project(tokens, other_tokens, kinds, other_kinds, groups, other_groups, weights, bias_rows):
    micro, _, local, width = tokens.shape
    halves = 2
    half = width // 2
    sub = local // BLOCK

    def rows_spec(cols):
        return pl.BlockSpec((None, None, BLOCK, cols), lambda a, m, i: (a, m, i, 0))

    def cols_spec(count):
        return pl.BlockSpec((None, None, count, BLOCK), lambda a, m, i: (a, m, 0, i))

    def shape(*dims, kind=bf16):
        return jax.ShapeDtypeStruct((halves, micro) + dims, kind)

    def pick(own, a, index, stop):
        return jnp.where(a == 0, index, stop) if own else jnp.where(a == 0, 0, index)

    def token_spec(own):
        return pl.BlockSpec(
            (None, None, BLOCK, width),
            lambda a, m, i: (pick(own, a, m, micro - 1), 0, pick(own, a, i, sub - 1), 0),
        )

    def mark_spec(own):
        return pl.BlockSpec(
            (None, 1, BLOCK),
            lambda a, m, i: (pick(own, a, m, micro - 1), 0, pick(own, a, i, sub - 1)),
        )

    count = halves * micro * local
    return pl.pallas_call(
        project_kernel,
        grid=(halves, micro, sub),
        in_specs=[
            token_spec(True),
            token_spec(False),
            mark_spec(True),
            mark_spec(False),
            mark_spec(True),
            mark_spec(False),
            pl.BlockSpec(weights.shape, lambda a, m, i: (0, 0, 0)),
            pl.BlockSpec(bias_rows.shape, lambda a, m, i: (0, 0)),
        ],
        out_specs=[
            rows_spec(width),
            rows_spec(width),
            cols_spec(width),
            rows_spec(half),
            cols_spec(half),
            rows_spec(width),
            rows_spec(1),
            rows_spec(1),
            cols_spec(1),
        ],
        out_shape=[
            shape(local, width),
            shape(local, width),
            shape(width, local),
            shape(local, half),
            shape(half, local),
            shape(local, width),
            shape(local, 1, kind=jnp.int32),
            shape(local, 1, kind=jnp.int32),
            shape(1, local, kind=jnp.int32),
        ],
        compiler_params=pltpu.CompilerParams(vmem_limit_bytes=VMEM_LIMIT),
        cost_estimate=cost(2 * count * width * 3 * width, count * width * 10),
        name="project",
    )(tokens, other_tokens, kinds, other_kinds, groups, other_groups, weights, bias_rows)


def place(block, per):
    return block // per, pl.multiple_of(lax.rem(block, per) * BLOCK, BLOCK)


def ends_of(own_ref, other_ref, micro_at, block, per):
    at = lax.rem(block, per) * BLOCK
    mine = block < per
    first = jnp.where(mine, own_ref[micro_at, at], other_ref[micro_at, at])
    last_at = at + BLOCK - 1
    return first, jnp.where(mine, own_ref[micro_at, last_at], other_ref[micro_at, last_at])


def attend_kernel(
    own_ref, other_ref, qp_ref, km_ref, vt_ref, gk_ref, gq_ref, c_ref, ct_ref, lse_ref, m_sc, l_sc, acc_sc
):
    micro_at = pl.program_id(0)
    local = qp_ref.shape[1]
    per = local // BLOCK
    blocks = 2 * per
    heads = qp_ref.shape[2] // 128

    @pl.loop(0, blocks)
    def _(qb):
        qh, qo = place(qb, per)
        m_sc[...] = jnp.full_like(m_sc, masked_score)
        l_sc[...] = jnp.zeros_like(l_sc)
        acc_sc[...] = jnp.zeros_like(acc_sc)
        q_low, q_high = ends_of(own_ref, other_ref, micro_at, qb, per)

        @pl.loop(0, blocks)
        def _(kb):
            k_low, k_high = ends_of(own_ref, other_ref, micro_at, kb, per)

            @pl.when((q_low <= k_high) & (k_low <= q_high))
            def _():
                kh, ko = place(kb, per)
                same = gk_ref[kh, pl.ds(ko, BLOCK), :] == gq_ref[qh, :, pl.ds(qo, BLOCK)]
                bias = jnp.where(same, 0.0, masked_score)
                for h in range(heads):
                    at = slice(128 * h, 128 * h + 128)
                    vat = slice(64 * h, 64 * h + 64)
                    s = nt(km_ref[kh, pl.ds(ko, BLOCK), at], qp_ref[qh, pl.ds(qo, BLOCK), at]) + bias
                    m_old = m_sc[h : h + 1, :]
                    m_new = jnp.maximum(m_old, jnp.max(s, axis=0, keepdims=True))
                    alpha = jnp.exp(m_old - m_new)
                    p = jnp.exp(s - m_new)
                    m_sc[h : h + 1, :] = m_new
                    l_sc[h : h + 1, :] = alpha * l_sc[h : h + 1, :] + jnp.sum(p, axis=0, keepdims=True)
                    acc_sc[vat, :] = alpha * acc_sc[vat, :] + nn(
                        vt_ref[kh, vat, pl.ds(ko, BLOCK)], p.astype(bf16)
                    )

        cols = pl.ds(pl.multiple_of(qb * BLOCK, BLOCK), BLOCK)
        for h in range(heads):
            vat = slice(64 * h, 64 * h + 64)
            total = l_sc[h : h + 1, :]
            ct_ref[vat, cols] = acc_sc[vat, :] / total
            lse_ref[h : h + 1, cols] = m_sc[h : h + 1, :] + jnp.log(total)
        c_ref[qh, pl.ds(qo, BLOCK), :] = ct_ref[:, cols].T.astype(bf16)


def whole_micro(array):
    rest = array.shape[2:]
    return pl.BlockSpec((array.shape[0], None) + rest, lambda m, *_: (0, m) + (0,) * len(rest))


def attend(own_groups, other_groups, qp, km, vt, gk, gq):
    halves, micro, local, width = qp.shape
    half = width // 2
    heads = width // 128
    length = halves * local
    return pl.pallas_call(
        attend_kernel,
        grid_spec=pltpu.PrefetchScalarGridSpec(
            num_scalar_prefetch=2,
            grid=(micro,),
            in_specs=[whole_micro(a) for a in (qp, km, vt, gk, gq)],
            out_specs=[
                pl.BlockSpec((halves, None, local, half), lambda m, *_: (0, m, 0, 0)),
                pl.BlockSpec((None, half, length), lambda m, *_: (m, 0, 0)),
                pl.BlockSpec((None, 8, length), lambda m, *_: (m, 0, 0)),
            ],
            scratch_shapes=[
                pltpu.VMEM((8, BLOCK), f32),
                pltpu.VMEM((8, BLOCK), f32),
                pltpu.VMEM((half, BLOCK), f32),
            ],
        ),
        out_shape=[
            jax.ShapeDtypeStruct((halves, micro, local, half), bf16),
            jax.ShapeDtypeStruct((micro, half, length), f32),
            jax.ShapeDtypeStruct((micro, 8, length), f32),
        ],
        compiler_params=pltpu.CompilerParams(vmem_limit_bytes=VMEM_LIMIT),
        cost_estimate=cost(
            micro * heads * length * length * 512, micro * length * width * 8, micro * heads * length * length
        ),
        name="attend",
    )(own_groups, other_groups, qp, km, vt, gk, gq)


def attend_back_kernel(
    own_ref,
    other_ref,
    qp_ref,
    km_ref,
    kmt_ref,
    v_ref,
    dc_ref,
    ct_ref,
    lse_ref,
    gk_ref,
    gq_ref,
    kind_ref,
    d_ref,
    db_ref,
    dqt_sc,
    dk_sc,
    dv_sc,
    delta_sc,
):
    micro_at = pl.program_id(0)
    local, width = qp_ref.shape[1], qp_ref.shape[2]
    half = width // 2
    per = local // BLOCK
    blocks = 2 * per
    tiles = half // 128
    dk_sc[...] = jnp.zeros_like(dk_sc)
    dv_sc[...] = jnp.zeros_like(dv_sc)

    @pl.when(micro_at == 0)
    def _():
        db_ref[...] = jnp.zeros_like(db_ref)

    lo = low_lanes((BLOCK, 128))

    @pl.loop(0, blocks)
    def _(qb):
        qh, qo = place(qb, per)
        qrows = pl.ds(qo, BLOCK)
        cols = pl.ds(pl.multiple_of(qb * BLOCK, BLOCK), BLOCK)
        dct = dc_ref[qh, qrows, :].astype(f32).T
        inner = dct * ct_ref[:, cols]
        for h in range(2 * tiles):
            delta_sc[h : h + 1, :] = jnp.sum(inner[64 * h : 64 * h + 64, :], axis=0, keepdims=True)
        dqt_sc[...] = jnp.zeros_like(dqt_sc)
        q_low, q_high = ends_of(own_ref, other_ref, micro_at, qb, per)

        @pl.loop(0, blocks)
        def _(kb):
            k_low, k_high = ends_of(own_ref, other_ref, micro_at, kb, per)

            @pl.when((q_low <= k_high) & (k_low <= q_high))
            def _():
                kh, ko = place(kb, per)
                krows = pl.ds(ko, BLOCK)
                drows = pl.ds(pl.multiple_of(kb * BLOCK, BLOCK), BLOCK)
                same = gk_ref[kh, krows, :] == gq_ref[qh, :, qrows]
                bias = jnp.where(same, 0.0, masked_score)
                for t in range(tiles):
                    tat = slice(128 * t, 128 * t + 128)
                    v = v_ref[kh, krows, tat]
                    dc = dc_ref[qh, qrows, tat]
                    from_pair = []
                    for side in range(2):
                        h = 2 * t + side
                        at = slice(128 * h, 128 * h + 128)
                        q = qp_ref[qh, qrows, at]
                        s = nt(km_ref[kh, krows, at], q) + bias
                        p = jnp.exp(s - lse_ref[h : h + 1, cols])
                        zero = jnp.zeros_like(v)
                        vm = jnp.where(lo, v, zero) if side == 0 else jnp.where(lo, zero, v)
                        dp = nt(vm, dc)
                        ds = (p * (dp - delta_sc[h : h + 1, :])).astype(bf16)
                        dk_sc[drows, at] += nn(ds, q)
                        dqt_sc[at, :] += nn(kmt_ref[kh, at, krows], ds)
                        from_pair.append(nn(p.astype(bf16), dc))
                    dv_sc[drows, tat] += jnp.where(lo, from_pair[0], from_pair[1])

        dq = dqt_sc[...].T * 0.125
        entity = kind_ref[qh, qrows, :] == 1
        d_ref[qh, qrows, 0:width] = jnp.where(entity, 0.0, dq).astype(bf16)
        d_ref[qh, qrows, width : 2 * width] = jnp.where(entity, dq, 0.0).astype(bf16)

    @pl.loop(0, blocks)
    def _(kb):
        kh, ko = place(kb, per)
        krows = pl.ds(ko, BLOCK)
        drows = pl.ds(pl.multiple_of(kb * BLOCK, BLOCK), BLOCK)
        entity = kind_ref[kh, krows, :] == 1
        for t in range(tiles):
            even = dk_sc[drows, 256 * t : 256 * t + 128]
            odd = dk_sc[drows, 256 * t + 128 : 256 * t + 256]
            left = jnp.where(entity, pltpu.roll(even, 64, 1), even)
            right = jnp.where(entity, odd, pltpu.roll(odd, 64, 1))
            d_ref[kh, krows, 2 * width + 128 * t : 2 * width + 128 * t + 128] = jnp.where(
                lo, left, right
            ).astype(bf16)
        d_ref[kh, krows, 2 * width + half : 3 * width] = dv_sc[drows, :].astype(bf16)
        db_ref[0:1, :] += jnp.sum(d_ref[kh, krows, :].astype(f32), axis=0, keepdims=True)


def attend_back(own_groups, other_groups, qp, km, kmt, v, dc, ct, lse, gk, gq, kind_col):
    halves, micro, local, width = qp.shape
    half = width // 2
    heads = width // 128
    length = halves * local
    return pl.pallas_call(
        attend_back_kernel,
        grid_spec=pltpu.PrefetchScalarGridSpec(
            num_scalar_prefetch=2,
            grid=(micro,),
            in_specs=[whole_micro(a) for a in (qp, km, kmt, v, dc)]
            + [
                pl.BlockSpec((None, half, length), lambda m, *_: (m, 0, 0)),
                pl.BlockSpec((None, 8, length), lambda m, *_: (m, 0, 0)),
            ]
            + [whole_micro(a) for a in (gk, gq, kind_col)],
            out_specs=[
                pl.BlockSpec((halves, None, local, 3 * width), lambda m, *_: (0, m, 0, 0)),
                pl.BlockSpec((8, 3 * width), lambda m, *_: (0, 0)),
            ],
            scratch_shapes=[
                pltpu.VMEM((width, BLOCK), f32),
                pltpu.VMEM((length, width), f32),
                pltpu.VMEM((length, half), f32),
                pltpu.VMEM((8, BLOCK), f32),
            ],
        ),
        out_shape=[
            jax.ShapeDtypeStruct((halves, micro, local, 3 * width), bf16),
            jax.ShapeDtypeStruct((8, 3 * width), f32),
        ],
        compiler_params=pltpu.CompilerParams(vmem_limit_bytes=VMEM_LIMIT),
        cost_estimate=cost(
            micro * heads * length * length * 1280, micro * length * width * 16, micro * heads * length * length
        ),
        name="attend_back",
    )(own_groups, other_groups, qp, km, kmt, v, dc, ct, lse, gk, gq, kind_col)


def norm_forward(hidden):
    center = hidden - jnp.mean(hidden, axis=-1, keepdims=True)
    rescale = lax.rsqrt(jnp.mean(center * center, axis=-1, keepdims=True) + layer_eps)
    return center * rescale, rescale


def norm_backward(upstream, normed, rescale, gain):
    scaled = upstream * gain
    return rescale * (
        scaled
        - jnp.mean(scaled, axis=-1, keepdims=True)
        - normed * jnp.mean(scaled * normed, axis=-1, keepdims=True)
    )


def column_sum(values):
    return jnp.sum(values.astype(f32), axis=0, keepdims=True)


def chain_kernel(
    side_ref,
    x_ref,
    own_ref,
    far_ref,
    cot_ref,
    w_ref,
    vec_ref,
    mixed_ref,
    dh_ref,
    left_ref,
    right_ref,
    dco_ref,
    dcx_ref,
    sums_ref,
    slope_sc,
    z_sc,
    landed,
    c_send,
    c_recv,
):
    width = x_ref.shape[1]
    half = width // 2
    rows = width // GROUPS
    chunks = 4
    first = side_ref[0] == 0

    step_at = pl.program_id(0)
    blocks = landed.shape[0]
    per = far_ref.shape[2] // BLOCK
    across = (1 - lax.axis_index("seq"), lax.axis_index("shard"))

    def far_copy(i):
        return send(
            far_ref.at[1, i // per, pl.ds((i % per) * BLOCK, BLOCK), :],
            landed.at[i],
            c_send.at[i],
            c_recv.at[i],
            across,
        )

    @pl.when(step_at == 0)
    def _():
        sums_ref[...] = jnp.zeros_like(sums_ref)
        greet([across])
        for i in range(blocks):
            far_copy(i).start()

    for i in range(blocks):

        @pl.when(step_at == i)
        def _(i=i):
            far_copy(i).wait_recv()
            if i == blocks - 1:
                for k in range(blocks):
                    far_copy(k).wait_send()

    def vector(at):
        return vec_ref[at : at + 1, :]

    def up_chunk(j):
        at = pl.multiple_of(5 * rows + j * rows, 16)
        return w_ref[:, pl.ds(at, rows), :].reshape(width, width)

    def down_chunk(j):
        return w_ref[pl.ds(j * (GROUPS // chunks), GROUPS // chunks), 0 : 4 * rows, :].reshape(width, width)

    def out_weight():
        return w_ref[:, 4 * rows : 5 * rows, :].reshape(width, width)

    own = own_ref[...].astype(f32)
    other = landed[step_at].astype(f32)
    context = jnp.concatenate(
        [jnp.where(first, own, other), jnp.where(first, other, own)], axis=1
    ).astype(bf16)
    left_ref[:, 0:width] = context
    hidden = x_ref[...].astype(f32) + (nn(context, out_weight()) + vector(0))
    n1, r1 = norm_forward(hidden)
    y1 = n1 * vector(1) + vector(2)
    left_ref[:, width : 2 * width] = y1.astype(bf16)
    z_sc[...] = y1 + vector(7)

    @pl.loop(0, chunks)
    def _(j):
        u = nn(left_ref[:, width : 2 * width], up_chunk(j)) + vec_ref[pl.ds(j + 3, 1), :]
        cumulative = 0.5 * (1.0 + lax.erf(u * 0.7071067811865476))
        at = pl.multiple_of(j * width, 128)
        slope_sc[:, pl.ds(at, width)] = (
            cumulative + u * jnp.exp(-0.5 * u * u) * 0.3989422804014327
        )
        g = (u * cumulative).astype(bf16)
        left_ref[:, pl.ds(pl.multiple_of(at + 2 * width, 128), width)] = g
        z_sc[...] += nn(g, down_chunk(j))

    n2, r2 = norm_forward(z_sc[...])
    mixed_ref[...] = (n2 * vector(8) + vector(9)).astype(bf16)
    upstream = cot_ref[...].astype(f32)
    sums_ref[0:1, :] += column_sum(upstream * n2)
    sums_ref[1:2, :] += column_sum(upstream)
    dh2 = norm_backward(upstream, n2, r2, vector(8))
    dz = dh2.astype(bf16)
    right_ref[:, 5 * width :] = dz
    sums_ref[2:3, :] += column_sum(dz)
    z_sc[...] = dh2

    @pl.loop(0, chunks)
    def _(j):
        at = pl.multiple_of(j * width, 128)
        du = (
            nt(right_ref[:, 5 * width :], down_chunk(j)) * slope_sc[:, pl.ds(at, width)]
        ).astype(bf16)
        right_ref[:, pl.ds(pl.multiple_of(at + width, 128), width)] = du
        sums_ref[pl.ds(j + 8, 1), :] += column_sum(du)
        z_sc[...] += nt(du, up_chunk(j))

    dy1 = z_sc[...]
    hidden = x_ref[...].astype(f32) + (nn(left_ref[:, 0:width], out_weight()) + vector(0))
    n1, r1 = norm_forward(hidden)
    sums_ref[3:4, :] += column_sum(dy1 * n1)
    sums_ref[4:5, :] += column_sum(dy1)
    dh1 = norm_backward(dy1, n1, r1, vector(1))
    dh_ref[...] = dh1
    da = dh1.astype(bf16)
    right_ref[:, 0:width] = da
    sums_ref[5:6, :] += column_sum(da)
    dc = nt(da, out_weight())
    dco_ref[...] = jnp.where(first, dc[:, :half], dc[:, half:]).astype(bf16)
    dcx_ref[...] = jnp.where(first, dc[:, half:], dc[:, :half]).astype(bf16)


def chain(side, x, c, cot, weights, vectors):
    tokens, width = x.shape
    half = width // 2
    per = c.shape[2] // BLOCK
    blocks = tokens // BLOCK

    def rows_spec(cols):
        return pl.BlockSpec((BLOCK, cols), lambda i, *_: (i, 0))

    def shape(cols, kind):
        return jax.ShapeDtypeStruct((tokens, cols), kind)

    return pl.pallas_call(
        chain_kernel,
        grid_spec=pltpu.PrefetchScalarGridSpec(
            num_scalar_prefetch=1,
            grid=(tokens // BLOCK,),
            in_specs=[
                rows_spec(width),
                pl.BlockSpec((None, None, BLOCK, half), lambda i, *_: (0, i // per, i % per, 0)),
                pl.BlockSpec(memory_space=pl.ANY),
                rows_spec(width),
                pl.BlockSpec(weights.shape, lambda i, *_: (0, 0, 0), pipeline_mode=pl.Buffered(1)),
                pl.BlockSpec(vectors.shape, lambda i, *_: (0, 0)),
            ],
            out_specs=[
                rows_spec(width),
                rows_spec(width),
                rows_spec(6 * width),
                rows_spec(6 * width),
                rows_spec(half),
                rows_spec(half),
                pl.BlockSpec((16, width), lambda i, *_: (0, 0)),
            ],
            scratch_shapes=[
                pltpu.VMEM((BLOCK, 4 * width), f32),
                pltpu.VMEM((BLOCK, width), f32),
                pltpu.VMEM((blocks, BLOCK, half), bf16),
                pltpu.SemaphoreType.DMA((blocks,)),
                pltpu.SemaphoreType.DMA((blocks,)),
            ],
        ),
        out_shape=[
            shape(width, bf16),
            shape(width, f32),
            shape(6 * width, bf16),
            shape(6 * width, bf16),
            shape(half, bf16),
            shape(half, bf16),
            jax.ShapeDtypeStruct((16, width), f32),
        ],
        compiler_params=pltpu.CompilerParams(
            collective_id=3, has_side_effects=True, vmem_limit_bytes=VMEM_LIMIT
        ),
        cost_estimate=cost(2 * tokens * width * width * 19, tokens * width * 36 + weights.size * 2),
        name="chain",
    )(side[None], x, c, c, cot, weights, vectors)


def feed_grad_kernel(l_ref, r_ref, out_ref):
    width = l_ref.shape[1]
    rows = width // GROUPS
    at = pl.program_id(0)
    grad = tn(l_ref[...], r_ref[...]).astype(bf16)

    @pl.when(at == 0)
    def _():
        out_ref[:, 4 * rows : 5 * rows, :] = grad.reshape(GROUPS, rows, width)

    @pl.when((at >= 1) & (at < 5))
    def _():
        start = pl.multiple_of(5 * rows + (at - 1) * rows, 16)
        out_ref[:, pl.ds(start, rows), :] = grad.reshape(GROUPS, rows, width)

    @pl.when(at >= 5)
    def _():
        out_ref[pl.ds((at - 5) * 4, 4), 0 : 4 * rows, :] = grad.reshape(4, 4 * rows, width)


def chip_grad_kernel(l_ref, r_ref, keep_ref, give_ref, part, from_core, c_send, c_recv):
    width = l_ref.shape[1]
    rows = width // GROUPS
    at = pl.program_id(0)
    x, _, z, y, core = spots()
    partner = (x, slot_of(z, y, 1 - core))
    spans = [(slice(0, 8), 4 * rows + i * rows, rows) for i in range(5)]
    spans += [(slice(2 * j, 2 * j + 2), 0, 4 * rows) for j in range(4)]

    def copy_of(i):
        rails, start, size = spans[i]
        return send(
            part.at[rails, 1 - core, slice(start, start + size), :],
            from_core.at[rails, slice(start, start + size), :],
            c_send.at[i],
            c_recv.at[i],
            partner,
        )

    def add(i):
        rails, start, size = spans[i]
        copy_of(i).wait_recv()
        for rail in range(rails.start, rails.stop):
            mine = part[rail, core, start : start + size, :].astype(f32)
            theirs = from_core[rail, start : start + size, :].astype(f32)
            whole = mine + theirs
            left, right = whole[:, : width // 2], whole[:, width // 2 :]
            keep_ref[rail, start : start + size, :] = jnp.where(x == 0, left, right).astype(bf16)
            give_ref[rail, start : start + size, :] = jnp.where(x == 0, right, left).astype(bf16)

    @pl.when(at == 0)
    def _():
        greet([partner])

    grad = tn(l_ref[...], r_ref[...]).astype(bf16)
    for i in range(9):

        @pl.when(at == i)
        def _(i=i):
            rails, start, size = spans[i]
            count = rails.stop - rails.start
            part[rails, :, start : start + size, :] = grad.reshape(count, 2, size, width)
            copy_of(i).start()
            if i >= 2:
                add(i - 2)
            if i == 8:
                add(7)
                add(8)
                for k in range(9):
                    copy_of(k).wait_send()


def feed_grad(left, right, direct):
    tokens = left.shape[0]
    width = left.shape[1] // 6
    rows = width // GROUPS

    def left_at(i):
        return (0, jnp.where(i == 0, 0, jnp.where(i < 5, 1, i - 3)))

    def right_at(i):
        return (0, jnp.minimum(i, 5))

    out = (8, 9 * rows, width // 2) if direct else (GROUPS, 9 * rows, width)
    count = 2 if direct else 1
    scratch = [
        pltpu.VMEM((8, 2, 9 * rows, width), bf16),
        pltpu.VMEM((8, 9 * rows, width), bf16),
        pltpu.SemaphoreType.DMA((9,)),
        pltpu.SemaphoreType.DMA((9,)),
    ]
    extra = dict(collective_id=2, has_side_effects=True) if direct else {}
    return pl.pallas_call(
        chip_grad_kernel if direct else feed_grad_kernel,
        grid=(9,),
        in_specs=[
            pl.BlockSpec((tokens, width), left_at),
            pl.BlockSpec((tokens, width), right_at),
        ],
        out_specs=[pl.BlockSpec(out, lambda i: (0, 0, 0))] * count,
        out_shape=[jax.ShapeDtypeStruct(out, bf16)] * count,
        scratch_shapes=scratch if direct else (),
        compiler_params=pltpu.CompilerParams(vmem_limit_bytes=VMEM_LIMIT, **extra),
        cost_estimate=cost(2 * tokens * width * width * 9, tokens * width * 24 + width * width * 18),
        name="feed_grad",
    )(left, right)


def attn_grad_kernel(x_ref, d_ref, vec_ref, out_ref):
    width = x_ref.shape[1]
    rows = width // GROUPS
    at = pl.program_id(0)
    grad = tn(x_ref[...], d_ref[...]).astype(bf16)
    start = pl.multiple_of(at * rows, 16)
    out_ref[:, pl.ds(start, rows), :] = grad.reshape(GROUPS, rows, width)
    out_ref[:, 3 * rows :, :] = vec_ref[...]


def attn_grad(x, d, vectors):
    tokens, width = x.shape
    rows = width // GROUPS
    return pl.pallas_call(
        attn_grad_kernel,
        grid=(3,),
        in_specs=[
            pl.BlockSpec((tokens, width), lambda i: (0, 0)),
            pl.BlockSpec((tokens, width), lambda i: (0, i)),
            pl.BlockSpec((GROUPS, 16, width), lambda i: (0, 0, 0)),
        ],
        out_specs=pl.BlockSpec((GROUPS, 3 * rows + 16, width), lambda i: (0, 0, 0)),
        out_shape=jax.ShapeDtypeStruct((GROUPS, 3 * rows + 16, width), bf16),
        compiler_params=pltpu.CompilerParams(vmem_limit_bytes=VMEM_LIMIT),
        cost_estimate=cost(2 * tokens * width * width * 3, tokens * width * 8 + width * width * 6),
        name="attn_grad",
    )(x, d, vectors)


def scatter_kernel(
    x_ref,
    d_ref,
    vec_ref,
    w_ref,
    dh_ref,
    keep_ref,
    taken_ref,
    dx_ref,
    gq_ref,
    gk_ref,
    gv_ref,
    gvec_ref,
    feed_ref,
    part,
    from_core,
    from_y,
    from_z,
    from_x,
    out_y,
    out_z,
    total,
    feed_out_y,
    feed_from_y,
    feed_out_z,
    feed_from_z,
    feed_total,
    feed_from_x,
    fy_send,
    fy_recv,
    fz_send,
    fz_recv,
    fx_send,
    fx_recv,
    dx_out,
    from_dx,
    d_send,
    d_recv,
    c_send,
    c_recv,
    y_send,
    y_recv,
    z_send,
    z_recv,
    x_send,
    x_recv,
):
    width = x_ref.shape[1]
    half = width // 2
    rows = width // GROUPS
    step_at = pl.program_id(0)
    x, me, z, y, core = spots()
    across = (1 - x, me)
    beside = (x, slot_of(z, 1 - y, core))
    partner = (x, slot_of(z, y, 1 - core))
    spans = ((0, rows), (rows, rows), (2 * rows, rows + 16))

    def core_copy(chunk, rail):
        start, size = spans[chunk]
        return send(
            part.at[2 * rail + 1 - core, pl.ds(start, size), :],
            from_core.at[rail, pl.ds(start, size), :],
            c_send.at[chunk * 8 + rail],
            c_recv.at[chunk * 8 + rail],
            partner,
        )

    def z_order(step):
        return lax.rem(z + 1 + step, 4)

    def feed_chip(rail):
        return keep_ref[rail].astype(f32) + taken_ref[rail].astype(f32)

    def feed_y(zz):
        return send(feed_out_y.at[zz], feed_from_y.at[zz], fy_send.at[zz], fy_recv.at[zz], beside)

    def feed_z(zz):
        return send(
            feed_out_z.at[zz],
            feed_from_z.at[z],
            fz_send.at[zz],
            fz_recv.at[z],
            (x, slot_of(zz, y, core)),
        )

    @pl.when(step_at == 0)
    def _():
        greet(all_peers())
        for step in range(4):
            zz = z_order(step)
            feed_out_y[zz] = feed_chip(zz * 2 + 1 - y).astype(bf16)
            feed_y(zz).start()

    columns = pl.ds(pl.multiple_of(step_at * width, 128), width)
    grad = tn(x_ref[...], d_ref[:, columns]).astype(bf16)
    for chunk in range(3):

        @pl.when(step_at == chunk)
        def _(chunk=chunk):
            start = spans[chunk][0]
            part[:, start : start + rows, :] = grad.reshape(GROUPS, rows, width)
            if chunk == 2:
                part[:, 3 * rows :, :] = vec_ref[...]
            for rail in range(8):
                core_copy(chunk, rail).start()

    flat = dh_ref.shape[0]

    def input_part(start):
        found = None
        for i in range(3):
            piece = nt(
                d_ref[pl.ds(pl.multiple_of(start, BLOCK), BLOCK), i * width : i * width + width],
                w_ref[:, i * rows : i * rows + rows, :].reshape(width, width),
            )
            found = piece if found is None else found + piece
        return found

    @pl.when(step_at == 2)
    def _():
        def y_copy(zz):
            return send(out_y.at[zz], from_y.at[zz], y_send.at[zz], y_recv.at[zz], beside)

        def z_copy(zz):
            return send(
                out_z.at[zz], from_z.at[z], z_send.at[zz], z_recv.at[z], (x, slot_of(zz, y, core))
            )

        def core_wait(rail):
            for chunk in range(3):
                start, size = spans[chunk]
                send(
                    part.at[0, pl.ds(start, size), :],
                    from_core.at[rail, pl.ds(start, size), :],
                    c_send.at[0],
                    c_recv.at[chunk * 8 + rail],
                    partner,
                ).wait_recv()

        for step in range(4):
            zz = z_order(step)
            rail = zz * 2 + 1 - y
            core_wait(rail)
            out_y[zz] = (part[2 * rail + core].astype(f32) + from_core[rail].astype(f32)).astype(bf16)
            y_copy(zz).start()

        @pl.loop(0, flat // BLOCK)
        def _(i):
            at = pl.ds(pl.multiple_of(i * BLOCK, BLOCK), BLOCK)
            dx_out[at, :] = input_part(flat + i * BLOCK).astype(bf16)

        exchange = send(dx_out, from_dx, d_send, d_recv, across)
        exchange.start()
        for step in range(3):
            zz = z_order(step)
            feed_y(zz).wait_recv()
            feed_out_z[zz] = (feed_chip(zz * 2 + y) + feed_from_y[zz].astype(f32)).astype(bf16)
            feed_z(zz).start()
        for step in range(4):
            core_wait(z_order(step) * 2 + y)

        def chip(zz):
            rail = zz * 2 + y
            return part[2 * rail + core].astype(f32) + from_core[rail].astype(f32)

        @pl.loop(0, flat // BLOCK)
        def _(i):
            at = pl.ds(pl.multiple_of(i * BLOCK, BLOCK), BLOCK)
            dx_ref[at, :] = dh_ref[at, :] + input_part(i * BLOCK)

        for step in range(3):
            zz = z_order(step)
            y_copy(zz).wait_recv()
            out_z[zz] = (chip(zz) + from_y[zz].astype(f32)).astype(bf16)
            z_copy(zz).start()
        feed_y(z).wait_recv()
        feed_result = feed_chip(z * 2 + y) + feed_from_y[z].astype(f32)
        for step in range(3):
            zz = z_order(step)
            send(
                feed_out_z.at[zz], feed_from_z.at[zz], fz_send.at[zz], fz_recv.at[zz], partner
            ).wait_recv()
            feed_result = feed_result + feed_from_z[zz].astype(f32)
        feed_total[...] = feed_result.astype(bf16)
        feed_last = send(feed_total, feed_from_x, fx_send, fx_recv, across)
        feed_last.start()
        y_copy(z).wait_recv()
        result = chip(z) + from_y[z].astype(f32)
        for step in range(3):
            zz = z_order(step)
            send(out_z.at[zz], from_z.at[zz], z_send.at[zz], z_recv.at[zz], partner).wait_recv()
            result = result + from_z[zz].astype(f32)
        total[...] = result.astype(bf16)
        last = send(total, from_x, x_send, x_recv, across)
        last.start()
        exchange.wait()

        @pl.loop(0, flat // BLOCK)
        def _(i):
            at = pl.ds(pl.multiple_of(i * BLOCK, BLOCK), BLOCK)
            dx_ref[at, :] += from_dx[at, :].astype(f32)

        for chunk in range(3):
            for rail in range(8):
                core_copy(chunk, rail).wait_send()
        for step in range(4):
            y_copy(z_order(step)).wait_send()
            feed_y(z_order(step)).wait_send()
        for step in range(3):
            z_copy(z_order(step)).wait_send()
            feed_z(z_order(step)).wait_send()
        first = x == 0
        feed_last.wait()
        own_feed, far_feed = feed_total[...].astype(f32), feed_from_x[...].astype(f32)
        feed_ref[:, :half] = jnp.where(first, own_feed, far_feed)
        feed_ref[:, half:] = jnp.where(first, far_feed, own_feed)
        last.wait()
        lo = low_lanes((rows, 128))

        def ordered(start, size, at):
            own = total[start : start + size, at].astype(f32)
            other = from_x[start : start + size, at].astype(f32)
            return jnp.where(first, own, other), jnp.where(first, other, own)

        for e in range(2):
            for t in range(half // 128):
                evens = ordered(e * rows, rows, slice(256 * t, 256 * t + 128))
                odds = ordered(e * rows, rows, slice(256 * t + 128, 256 * t + 256))
                for s in range(2):
                    word = jnp.where(lo, evens[s], pltpu.roll(odds[s], 64, 1))
                    entity = jnp.where(lo, pltpu.roll(evens[s], 64, 1), odds[s])
                    base = 2 * e * width + s * half + 128 * t
                    gq_ref[:, base : base + 128] = word
                    gq_ref[:, base + width : base + width + 128] = entity
        for ref, base in ((gk_ref, 0), (gv_ref, half)):
            a, b = ordered(2 * rows, rows, slice(base, base + half))
            ref[:, :half] = a
            ref[:, half:] = b
        gvec_ref[...] = total[3 * rows :, :].astype(f32) + from_x[3 * rows :, :].astype(f32)


def scatter_attention(x, d, vectors, weights, dh, keep, taken):
    tokens, width = x.shape
    rows = width // GROUPS
    tall = 3 * rows + 16
    sem = pltpu.SemaphoreType.DMA

    def whole(*dims):
        return pl.BlockSpec(dims, lambda i: (0,) * len(dims), pipeline_mode=pl.Buffered(1))

    outs = (dh.shape, (rows, 4 * width), (rows, width), (rows, width), (16, width), (9 * rows, width))
    return pl.pallas_call(
        scatter_kernel,
        grid=(3,),
        in_specs=[
            whole(tokens, width),
            whole(*d.shape),
            whole(GROUPS, 16, width),
            whole(*weights.shape),
            whole(*dh.shape),
            whole(*keep.shape),
            whole(*keep.shape),
        ],
        out_specs=[whole(*dims) for dims in outs],
        out_shape=[jax.ShapeDtypeStruct(dims, f32) for dims in outs],
        scratch_shapes=[
            pltpu.VMEM((GROUPS, tall, width), bf16),
            pltpu.VMEM((8, tall, width), bf16),
            pltpu.VMEM((4, tall, width), bf16),
            pltpu.VMEM((4, tall, width), bf16),
            pltpu.VMEM((tall, width), bf16),
            pltpu.VMEM((4, tall, width), bf16),
            pltpu.VMEM((4, tall, width), bf16),
            pltpu.VMEM((tall, width), bf16),
            pltpu.VMEM((4,) + keep.shape[1:], bf16),
            pltpu.VMEM((4,) + keep.shape[1:], bf16),
            pltpu.VMEM((4,) + keep.shape[1:], bf16),
            pltpu.VMEM((4,) + keep.shape[1:], bf16),
            pltpu.VMEM(keep.shape[1:], bf16),
            pltpu.VMEM(keep.shape[1:], bf16),
            sem((4,)),
            sem((4,)),
            sem((4,)),
            sem((4,)),
            sem,
            sem,
            pltpu.VMEM(dh.shape, bf16),
            pltpu.VMEM(dh.shape, bf16),
            sem,
            sem,
            sem((24,)),
            sem((24,)),
            sem((4,)),
            sem((4,)),
            sem((4,)),
            sem((4,)),
            sem,
            sem,
        ],
        compiler_params=pltpu.CompilerParams(
            collective_id=1, has_side_effects=True, vmem_limit_bytes=VMEM_LIMIT
        ),
        cost_estimate=cost(2 * tokens * width * width * 3, tokens * width * 8 + width * width * 6),
        name="scatter",
    )(x, d, vectors, weights, dh, keep, taken)


def input_grad_kernel(d_ref, w_ref, out_ref):
    width = out_ref.shape[1]
    rows = width // GROUPS
    total = None
    for i in range(3):
        part = nt(
            d_ref[:, i * width : i * width + width],
            w_ref[:, i * rows : i * rows + rows, :].reshape(width, width),
        )
        total = part if total is None else total + part
    out_ref[...] = total.astype(out_ref.dtype)


def input_grad_part(d, weights, side_at, kind):
    _, micro, local, wide = d.shape
    width = wide // 3
    sub = local // BLOCK
    return pl.pallas_call(
        input_grad_kernel,
        grid=(micro, sub),
        in_specs=[
            pl.BlockSpec((None, None, BLOCK, wide), lambda m, i: (side_at, m, i, 0)),
            pl.BlockSpec(weights.shape, lambda m, i: (0, 0, 0)),
        ],
        out_specs=pl.BlockSpec((None, BLOCK, width), lambda m, i: (m, i, 0)),
        out_shape=jax.ShapeDtypeStruct((micro, local, width), kind),
        compiler_params=pltpu.CompilerParams(vmem_limit_bytes=VMEM_LIMIT),
        cost_estimate=cost(2 * micro * local * wide * width, micro * local * wide * 2 + weights.size * 2),
        name="input_grad",
    )(d, weights)


def assemble(attn_own, attn_other, side, head_dim, rows, piece):
    attn_own, attn_other = attn_own.astype(f32), attn_other.astype(f32)
    width = attn_own.shape[1]
    half = width // 2
    vec_total = attn_own[3 * rows, :piece] + attn_other[3 * rows, :piece]

    def by_side(own, other, axis):
        return jnp.where(
            side == 0,
            jnp.concatenate([own, other], axis=axis),
            jnp.concatenate([other, own], axis=axis),
        )

    def query_parts(block):
        pairs = jnp.stack([block[:rows], block[rows : 2 * rows]], axis=1)
        return unpair_columns(pairs, head_dim)

    grad_query = by_side(query_parts(attn_own), query_parts(attn_other), 3).reshape(rows, 4 * width)
    kv_own, kv_other = attn_own[2 * rows : 3 * rows], attn_other[2 * rows : 3 * rows]
    grad_key = by_side(kv_own[:, :half], kv_other[:, :half], 1)
    grad_value = by_side(kv_own[:, half:], kv_other[:, half:], 1)
    return grad_query, grad_key, grad_value, vec_total


def on_device(
    tokens,
    kinds,
    groups,
    query_weight,
    query_bias,
    key_weight,
    key_bias,
    value_weight,
    value_bias,
    output_weight,
    output_bias,
    norm1_gain,
    norm1_shift,
    up_weight,
    up_bias,
    down_weight,
    down_bias,
    norm2_gain,
    norm2_shift,
    cotangent,
):
    micro, _, local, width = tokens.shape
    half = width // 2
    head_dim = width // HEADS
    devices = lax.axis_size("shard")
    rows = width // devices
    side = lax.axis_index("seq").astype(jnp.int32)

    vectors = (
        query_bias,
        key_bias,
        value_bias,
        output_bias,
        norm1_gain,
        norm1_shift,
        up_bias,
        down_bias,
        norm2_gain,
        norm2_shift,
    )
    piece = 16 * rows
    direct = devices == GROUPS
    attn_sizes = (rows, rows, rows)
    feed_sizes = (4 * rows,) + (rows,) * 5
    if not direct:
        vector_row = jnp.pad(jnp.concatenate(vectors), (0, width - piece))[None]
        packed = pack_attention(query_weight, key_weight, value_weight, vector_row, side, head_dim)
        attn_gathered = lax.all_gather(packed[None], "shard", axis=0, tiled=True)
        other_tokens, other_kinds, other_groups = swap(tokens), swap(kinds), swap(groups)
    feed_local = pack_feed(down_weight, output_weight, up_weight)
    feed_gathered = lax.all_gather(feed_local[None], "shard", axis=0, tiled=True)
    if direct:
        attn_gathered, other_tokens, other_kinds, other_groups = gather_attention(
            query_weight, key_weight, value_weight, vectors, tokens, kinds, groups
        )
    vectors = attn_gathered[:, 3 * rows, :piece]
    if direct:
        attn_w, feed_w = attn_gathered, feed_gathered
    else:
        attn_w = regroup(attn_gathered, attn_sizes)
        feed_w = regroup(feed_gathered, feed_sizes)

    def whole_vector(start, size):
        return vectors[:, start : start + size].reshape(-1).astype(f32)

    full_query_bias = whole_vector(0, 4 * rows)
    full_key_bias = whole_vector(4 * rows, rows)
    full_value_bias = whole_vector(5 * rows, rows)
    bias_rows = jnp.concatenate(
        [
            pair_columns(full_query_bias, side, head_dim),
            jnp.concatenate([own_half(full_key_bias, side), own_half(full_value_bias, side)])[None],
        ],
        axis=0,
    )
    full_up_bias = whole_vector(9 * rows, 4 * rows).reshape(4, width)
    chain_vectors = jnp.concatenate(
        [
            whole_vector(6 * rows, rows)[None],
            whole_vector(7 * rows, rows)[None],
            whole_vector(8 * rows, rows)[None],
            full_up_bias,
            whole_vector(13 * rows, rows)[None],
            whole_vector(14 * rows, rows)[None],
            whole_vector(15 * rows, rows)[None],
        ],
        axis=0,
    )

    own_tokens = tokens[:, 0]
    own_groups, far_groups = groups.reshape(micro, local), other_groups.reshape(micro, local)
    qp, km, kmt, v, vt, xs, kind_col, gk, gq = project(
        tokens, other_tokens, kinds, other_kinds, groups, other_groups, attn_w, bias_rows
    )
    c, ct, lse = attend(own_groups, far_groups, qp, km, vt, gk, gq)
    flat = micro * local
    mixed, dh1, left, right, dc_own, dc_other, sums = chain(
        side,
        own_tokens.reshape(flat, width),
        c,
        cotangent.reshape(flat, width),
        feed_w,
        chain_vectors,
    )

    dc_swapped = swap(dc_other)
    feed_part = feed_grad(left, right, direct)
    dc_swapped, feed_part = lax.optimization_barrier((dc_swapped, feed_part))
    dc = jnp.stack([dc_own, dc_swapped]).reshape(2, micro, local, half)

    if direct:
        keep, give = feed_part
        taken = swap(give)
    else:
        feed_part = ungroup(feed_part[0], feed_sizes, devices)
        feed_sum = lax.psum_scatter(feed_part, "shard", scatter_dimension=0, tiled=True)[0]
    d, db = attend_back(own_groups, far_groups, qp, km, kmt, v, dc, ct, lse, gk, gq, kind_col)

    query_own = unpair_columns(db[0, : 2 * width].reshape(2, width), head_dim)
    zero = jnp.zeros((half,), f32)

    def spread(own):
        return jnp.where(side == 0, jnp.concatenate([own, zero]), jnp.concatenate([zero, own]))

    query_spread = jnp.concatenate([spread(query_own[e, w]) for e in range(2) for w in range(2)])
    key_spread = spread(db[0, 2 * width : 2 * width + half])
    value_spread = spread(db[0, 2 * width + half :])
    grad_vectors = jnp.concatenate(
        [
            query_spread.reshape(devices, 4 * rows),
            key_spread.reshape(devices, rows),
            value_spread.reshape(devices, rows),
            sums[5].reshape(devices, rows),
            sums[3].reshape(devices, rows),
            sums[4].reshape(devices, rows),
            sums[8:12].reshape(devices, 4 * rows),
            sums[2].reshape(devices, rows),
            sums[0].reshape(devices, rows),
            sums[1].reshape(devices, rows),
        ],
        axis=1,
    ).astype(bf16)
    grad_vectors = jnp.pad(grad_vectors[:, None, :], ((0, 0), (0, 15), (0, width - piece)))
    flat_x = xs.reshape(2 * flat, width)
    flat_d = d.reshape(2 * flat, 3 * width)
    if direct:
        input_grad, grad_query, grad_key, grad_value, vec_rows, feed_total = scatter_attention(
            flat_x, flat_d, grad_vectors, attn_w, dh1, keep, taken
        )
        input_grad = input_grad.reshape(micro, local, width)
        vec_total = vec_rows[0, :piece]
    else:
        zeros = jnp.zeros((GROUPS, 16, width), bf16)
        attn_part = attn_grad(flat_x, flat_d, zeros)
        attn_part = jnp.concatenate(
            [ungroup(attn_part[:, : 3 * (width // GROUPS)], attn_sizes, devices), grad_vectors], axis=1
        )
        attn_sum = lax.psum_scatter(attn_part, "shard", scatter_dimension=0, tiled=True)[0]
        attn_other = swap(attn_sum)
        grad_query, grad_key, grad_value, vec_total = assemble(
            attn_sum, attn_other, side, head_dim, rows, piece
        )
        dx_other = input_grad_part(d, attn_w, 1, bf16)
        dx_own = input_grad_part(d, attn_w, 0, f32)
        input_grad = dh1.reshape(micro, local, width) + dx_own + swap(dx_other).astype(f32)

    if not direct:
        feed_total = feed_sum.astype(f32) + swap(feed_sum).astype(f32)
    grad_down = feed_total[: 4 * rows]
    grad_output = feed_total[4 * rows : 5 * rows]
    grad_up = jnp.concatenate(
        [feed_total[(5 + j) * rows : (6 + j) * rows] for j in range(4)], axis=1
    )

    def piece_of(start, size):
        return vec_total[start : start + size]

    return (
        mixed.reshape(micro, 1, local, width),
        input_grad[:, None],
        grad_query,
        piece_of(0, 4 * rows),
        grad_key,
        piece_of(4 * rows, rows),
        grad_value,
        piece_of(5 * rows, rows),
        grad_output,
        piece_of(6 * rows, rows),
        piece_of(7 * rows, rows),
        piece_of(8 * rows, rows),
        grad_up,
        piece_of(9 * rows, 4 * rows),
        grad_down,
        piece_of(13 * rows, rows),
        piece_of(14 * rows, rows),
        piece_of(15 * rows, rows),
    )


def solution(mesh):
    weight = P("shard", None)
    vector = P("shard")
    tokens = P(None, "shard", "seq", None)
    marks = P(None, "shard", "seq")
    return jax.shard_map(
        on_device,
        mesh=mesh,
        in_specs=(tokens, marks, marks)
        + (weight, vector) * 4
        + (vector, vector)
        + (weight, vector) * 2
        + (vector, vector)
        + (tokens,),
        out_specs=(tokens, tokens)
        + (weight, vector) * 4
        + (vector, vector)
        + (weight, vector) * 2
        + (vector, vector),
        check_vma=False,
    )
```

```python
import jax
import jax.numpy as jnp
from jax import lax
from jax.experimental import pallas as pl
from jax.experimental.pallas import tpu as pltpu
from jax.sharding import PartitionSpec as P


HEADS = 12
GROUPS = 16
BLOCK = 256
masked_score = -1e30
layer_eps = 1e-12
bf16 = jnp.bfloat16
f32 = jnp.float32
VMEM_LIMIT = 60 * 1024 * 1024


def nn(a, b):
    return lax.dot_general(a, b, (((1,), (0,)), ((), ())), preferred_element_type=f32)


def nt(a, b):
    return lax.dot_general(a, b, (((1,), (1,)), ((), ())), preferred_element_type=f32)


def tn(a, b):
    return lax.dot_general(a, b, (((0,), (0,)), ((), ())), preferred_element_type=f32)


def swap(value):
    return lax.ppermute(value, "seq", [(0, 1), (1, 0)])


def cost(flops, moved, trans=0):
    return pl.CostEstimate(flops=flops, bytes_accessed=moved, transcendentals=trans)


def low_lanes(shape):
    return lax.broadcasted_iota(jnp.int32, shape, len(shape) - 1) % 128 < 64


def pack_into(first, q_ref, k_ref, v_ref, vec, out_ref):
    rows, width = k_ref.shape
    half = width // 2

    def own(ref, base):
        return jnp.where(
            first,
            ref[:, base : base + half].astype(f32),
            ref[:, base + half : base + width].astype(f32),
        )

    lo = low_lanes((rows, 128))
    for e in range(2):
        word = own(q_ref, 2 * e * width)
        entity = own(q_ref, (2 * e + 1) * width)
        for t in range(half // 128):
            a = word[:, 128 * t : 128 * t + 128]
            b = entity[:, 128 * t : 128 * t + 128]
            even = jnp.where(lo, a, pltpu.roll(b, 64, 1))
            odd = jnp.where(lo, pltpu.roll(a, 64, 1), b)
            out_ref[e * rows : e * rows + rows, 256 * t : 256 * t + 128] = even.astype(bf16)
            out_ref[e * rows : e * rows + rows, 256 * t + 128 : 256 * t + 256] = odd.astype(bf16)
    out_ref[2 * rows : 3 * rows, :half] = own(k_ref, 0).astype(bf16)
    out_ref[2 * rows : 3 * rows, half:] = own(v_ref, 0).astype(bf16)
    out_ref[3 * rows :, :] = jnp.broadcast_to(vec, (16, width)).astype(bf16)


def spots():
    x = lax.axis_index("seq")
    me = lax.axis_index("shard")
    core = lax.rem(me, 2)
    y = lax.rem(me // 2, 2)
    z = me // 4
    return x, me, z, y, core


def slot_of(z, y, core):
    return z * 4 + y * 2 + core


def greet(peers):
    barrier = pltpu.get_barrier_semaphore()
    for peer in peers:
        pl.semaphore_signal(barrier, inc=1, device_id=peer, device_id_type=pl.DeviceIdType.MESH)
    pl.semaphore_wait(barrier, len(peers))


def all_peers():
    x, me, z, y, core = spots()
    peers = [(x, slot_of(z, y, 1 - core)), (x, slot_of(z, 1 - y, core)), (1 - x, me)]
    for step in range(1, 4):
        peers.append((x, slot_of(lax.rem(z + step, 4), y, core)))
    return peers


def send(src, dst, send_sem, recv_sem, device):
    return pltpu.make_async_remote_copy(
        src_ref=src,
        dst_ref=dst,
        send_sem=send_sem,
        recv_sem=recv_sem,
        device_id=device,
        device_id_type=pl.DeviceIdType.MESH,
    )


def gather_kernel(*refs):
    q_ref, k_ref, v_ref = refs[:3]
    vec_refs = refs[3:13]
    tok_ref, kinds_ref, groups_ref = refs[13:16]
    w_ref, tok_out, kinds_out, groups_out = refs[16:20]
    mine, keep_sem, x_send, x_recv, z_send, z_recv, y_send, y_recv, c_send, c_recv = refs[20:]
    x, me, z, y, core = spots()
    across = (1 - x, me)
    beside = (x, slot_of(z, 1 - y, core))
    partner = (x, slot_of(z, y, 1 - core))
    greet(all_peers())
    over = [
        send(src, dst, x_send.at[i], x_recv.at[i], across)
        for i, (src, dst) in enumerate(
            ((kinds_ref, kinds_out), (groups_ref, groups_out), (tok_ref, tok_out))
        )
    ]
    for copy in over:
        copy.start()
    vec = jnp.concatenate([r[...].astype(f32) for r in vec_refs], axis=1)
    pack_into(x == 0, q_ref, k_ref, v_ref, vec, mine)
    started = []
    copy = send(mine, w_ref.at[me], y_send.at[z], y_recv.at[z], beside)
    copy.start()
    started.append(copy)
    copy = send(mine, w_ref.at[me], c_send.at[z * 2 + y], c_recv.at[z * 2 + y], partner)
    copy.start()
    started.append(copy)
    keep = pltpu.make_async_copy(mine, w_ref.at[me], keep_sem)
    keep.start()
    for step in range(1, 4):
        copy = send(
            mine,
            w_ref.at[me],
            z_send.at[step - 1],
            z_recv.at[z],
            (x, slot_of(lax.rem(z + step, 4), y, core)),
        )
        copy.start()
        started.append(copy)
        zz = lax.rem(z + 4 - step, 4)
        at = slot_of(zz, y, core)
        held = w_ref.at[at]
        send(held, held, z_send.at[0], z_recv.at[zz], partner).wait_recv()
        for copy in (
            send(held, held, y_send.at[zz], y_recv.at[zz], beside),
            send(held, held, c_send.at[zz * 2 + y], c_recv.at[zz * 2 + y], partner),
        ):
            copy.start()
            started.append(copy)
    for step in range(4):
        zz = lax.rem(z + 4 - step, 4)
        rail = zz * 2 + 1 - y
        held = w_ref.at[slot_of(zz, 1 - y, core)]
        send(held, held, y_send.at[0], y_recv.at[zz], partner).wait_recv()
        copy = send(held, held, c_send.at[rail], c_recv.at[rail], partner)
        copy.start()
        started.append(copy)
    for rail in range(8):
        held = w_ref.at[2 * rail + 1 - core]
        send(held, held, c_send.at[0], c_recv.at[rail], partner).wait_recv()
    keep.wait()
    for copy in started:
        copy.wait_send()
    for copy in over:
        copy.wait()


def gather_attention(query_weight, key_weight, value_weight, vectors, tokens, kinds, groups):
    rows, width = key_weight.shape
    vmem = pl.BlockSpec(memory_space=pltpu.VMEM)
    anywhere = pl.BlockSpec(memory_space=pl.ANY)
    sem = pltpu.SemaphoreType.DMA
    return pl.pallas_call(
        gather_kernel,
        in_specs=[vmem] * 13 + [anywhere] * 3,
        out_specs=[anywhere] * 4,
        out_shape=[
            jax.ShapeDtypeStruct((GROUPS, 3 * rows + 16, width), bf16),
            jax.ShapeDtypeStruct(tokens.shape, tokens.dtype),
            jax.ShapeDtypeStruct(kinds.shape, kinds.dtype),
            jax.ShapeDtypeStruct(groups.shape, groups.dtype),
        ],
        scratch_shapes=[
            pltpu.VMEM((3 * rows + 16, width), bf16),
            sem,
            sem((3,)),
            sem((3,)),
            sem((3,)),
            sem((4,)),
            sem((4,)),
            sem((4,)),
            sem((8,)),
            sem((8,)),
        ],
        compiler_params=pltpu.CompilerParams(
            collective_id=0, has_side_effects=True, vmem_limit_bytes=VMEM_LIMIT
        ),
        name="gather",
    )(query_weight, key_weight, value_weight, *[v[None] for v in vectors], tokens, kinds, groups)


def pair_columns(columns, side, head_dim):
    lead = columns.shape[:-1]
    per = columns.shape[-1] // (8 * head_dim)
    view = columns.reshape(lead + (2, 2, 2, per, head_dim))
    view = jnp.where(side == 0, view[..., 0, :, :], view[..., 1, :, :])
    return jnp.swapaxes(view, -3, -2).reshape(lead + (2, -1))


def unpair_columns(pairs, head_dim):
    lead = pairs.shape[:-2]
    per = pairs.shape[-1] // (2 * head_dim)
    view = pairs.reshape(lead + (2, per, 2, head_dim))
    return jnp.swapaxes(view, -3, -2).reshape(lead + (2, 2, per * head_dim))


def own_half(columns, side):
    half = columns.shape[-1] // 2
    return jnp.where(side == 0, columns[..., :half], columns[..., half:])


def pack_attention(query_weight, key_weight, value_weight, vector, side, head_dim):
    width = key_weight.shape[1]
    pairs = pair_columns(query_weight, side, head_dim)
    key_value = jnp.concatenate([own_half(key_weight, side), own_half(value_weight, side)], axis=1)
    return jnp.concatenate(
        [pairs[:, 0], pairs[:, 1], key_value, jnp.broadcast_to(vector, (16, width))], axis=0
    )


def pack_feed_kernel(down_ref, output_ref, up_ref, out_ref):
    rows, width = output_ref.shape
    out_ref[0 : 4 * rows, :] = down_ref[...]
    out_ref[4 * rows : 5 * rows, :] = output_ref[...]
    for j in range(4):
        out_ref[(5 + j) * rows : (6 + j) * rows, :] = up_ref[:, j * width : j * width + width]


def pack_feed(down_weight, output_weight, up_weight):
    rows, width = output_weight.shape
    if rows % 16:
        return jnp.concatenate(
            [down_weight, output_weight]
            + [up_weight[:, j * width : j * width + width] for j in range(4)],
            axis=0,
        )
    vmem = pl.BlockSpec(memory_space=pltpu.VMEM)
    return pl.pallas_call(
        pack_feed_kernel,
        in_specs=[vmem] * 3,
        out_specs=vmem,
        out_shape=jax.ShapeDtypeStruct((9 * rows, width), bf16),
        name="pack_feed",
    )(down_weight, output_weight, up_weight)


def regroup(gathered, sizes):
    _, _, width = gathered.shape
    pieces = []
    start = 0
    for size in sizes:
        piece = gathered[:, start : start + size].reshape(GROUPS, -1, width)
        pieces.append(piece)
        start += size
    return jnp.concatenate(pieces, axis=1)


def ungroup(grouped, sizes, devices):
    _, _, width = grouped.shape
    pieces = []
    start = 0
    for size in sizes:
        wide = size * devices // GROUPS
        pieces.append(grouped[:, start : start + wide].reshape(devices, size, width))
        start += wide
    return jnp.concatenate(pieces, axis=1)


def project_kernel(
    own_ref,
    other_ref,
    own_kind_ref,
    other_kind_ref,
    own_group_ref,
    other_group_ref,
    w_ref,
    bias_ref,
    qp_ref,
    km_ref,
    kmt_ref,
    v_ref,
    vt_ref,
    xs_ref,
    kind_ref,
    gk_ref,
    gq_ref,
):
    width = own_ref.shape[1]
    half = width // 2
    rows = width // GROUPS
    mine = pl.program_id(0) == 0

    def column(row):
        return jnp.broadcast_to(row.astype(f32), (128, BLOCK)).T.astype(jnp.int32)

    x = jnp.where(mine, own_ref[...].astype(f32), other_ref[...].astype(f32)).astype(bf16)
    group = jnp.where(mine, own_group_ref[...], other_group_ref[...])
    kinds = column(jnp.where(mine, own_kind_ref[...], other_kind_ref[...]))
    kind = kinds[:, 0:1]
    xs_ref[...] = x
    kind_ref[...] = kind
    gk_ref[...] = column(group)[:, 0:1]
    gq_ref[...] = group
    wa = w_ref[:, 0:rows, :].reshape(width, width)
    wb = w_ref[:, rows : 2 * rows, :].reshape(width, width)
    wkv = w_ref[:, 2 * rows : 3 * rows, :].reshape(width, width)
    qa = nn(x, wa) + bias_ref[0:1, :]
    qb = nn(x, wb) + bias_ref[1:2, :]
    qp_ref[...] = (jnp.where(kind == 1, qb, qa) * 0.125).astype(bf16)
    kv = nn(x, wkv) + bias_ref[2:3, :]
    lane_high = (lax.broadcasted_iota(jnp.int32, (BLOCK, 128), 1) >= 64).astype(jnp.int32)
    keep = lane_high == kinds
    lo = lane_high == 0
    for t in range(half // 128):
        k = kv[:, 128 * t : 128 * t + 128]
        r = pltpu.roll(k, 64, 1)
        even = jnp.where(keep, jnp.where(lo, k, r), 0.0)
        odd = jnp.where(keep, jnp.where(lo, r, k), 0.0)
        km_ref[:, 256 * t : 256 * t + 128] = even.astype(bf16)
        km_ref[:, 256 * t + 128 : 256 * t + 256] = odd.astype(bf16)
        kmt_ref[256 * t : 256 * t + 128, :] = even.T.astype(bf16)
        kmt_ref[256 * t + 128 : 256 * t + 256, :] = odd.T.astype(bf16)
    v = kv[:, half:]
    v_ref[...] = v.astype(bf16)
    vt_ref[...] = v.T.astype(bf16)


def project(tokens, other_tokens, kinds, other_kinds, groups, other_groups, weights, bias_rows):
    micro, _, local, width = tokens.shape
    halves = 2
    half = width // 2
    sub = local // BLOCK

    def rows_spec(cols):
        return pl.BlockSpec((None, None, BLOCK, cols), lambda a, m, i: (a, m, i, 0))

    def cols_spec(count):
        return pl.BlockSpec((None, None, count, BLOCK), lambda a, m, i: (a, m, 0, i))

    def shape(*dims, kind=bf16):
        return jax.ShapeDtypeStruct((halves, micro) + dims, kind)

    def pick(own, a, index, stop):
        return jnp.where(a == 0, index, stop) if own else jnp.where(a == 0, 0, index)

    def token_spec(own):
        return pl.BlockSpec(
            (None, None, BLOCK, width),
            lambda a, m, i: (pick(own, a, m, micro - 1), 0, pick(own, a, i, sub - 1), 0),
        )

    def mark_spec(own):
        return pl.BlockSpec(
            (None, 1, BLOCK),
            lambda a, m, i: (pick(own, a, m, micro - 1), 0, pick(own, a, i, sub - 1)),
        )

    count = halves * micro * local
    return pl.pallas_call(
        project_kernel,
        grid=(halves, micro, sub),
        in_specs=[
            token_spec(True),
            token_spec(False),
            mark_spec(True),
            mark_spec(False),
            mark_spec(True),
            mark_spec(False),
            pl.BlockSpec(weights.shape, lambda a, m, i: (0, 0, 0)),
            pl.BlockSpec(bias_rows.shape, lambda a, m, i: (0, 0)),
        ],
        out_specs=[
            rows_spec(width),
            rows_spec(width),
            cols_spec(width),
            rows_spec(half),
            cols_spec(half),
            rows_spec(width),
            rows_spec(1),
            rows_spec(1),
            cols_spec(1),
        ],
        out_shape=[
            shape(local, width),
            shape(local, width),
            shape(width, local),
            shape(local, half),
            shape(half, local),
            shape(local, width),
            shape(local, 1, kind=jnp.int32),
            shape(local, 1, kind=jnp.int32),
            shape(1, local, kind=jnp.int32),
        ],
        compiler_params=pltpu.CompilerParams(vmem_limit_bytes=VMEM_LIMIT),
        cost_estimate=cost(2 * count * width * 3 * width, count * width * 10),
        name="project",
    )(tokens, other_tokens, kinds, other_kinds, groups, other_groups, weights, bias_rows)


def place(block, per):
    return block // per, pl.multiple_of(lax.rem(block, per) * BLOCK, BLOCK)


def ends_of(own_ref, other_ref, micro_at, block, per):
    at = lax.rem(block, per) * BLOCK
    mine = block < per
    first = jnp.where(mine, own_ref[micro_at, at], other_ref[micro_at, at])
    last_at = at + BLOCK - 1
    return first, jnp.where(mine, own_ref[micro_at, last_at], other_ref[micro_at, last_at])


def attend_kernel(
    own_ref, other_ref, qp_ref, km_ref, vt_ref, gk_ref, gq_ref, c_ref, ct_ref, lse_ref, m_sc, l_sc, acc_sc
):
    micro_at = pl.program_id(0)
    local = qp_ref.shape[1]
    per = local // BLOCK
    blocks = 2 * per
    heads = qp_ref.shape[2] // 128

    @pl.loop(0, blocks)
    def _(qb):
        qh, qo = place(qb, per)
        m_sc[...] = jnp.full_like(m_sc, masked_score)
        l_sc[...] = jnp.zeros_like(l_sc)
        acc_sc[...] = jnp.zeros_like(acc_sc)
        q_low, q_high = ends_of(own_ref, other_ref, micro_at, qb, per)

        @pl.loop(0, blocks)
        def _(kb):
            k_low, k_high = ends_of(own_ref, other_ref, micro_at, kb, per)

            @pl.when((q_low <= k_high) & (k_low <= q_high))
            def _():
                kh, ko = place(kb, per)
                same = gk_ref[kh, pl.ds(ko, BLOCK), :] == gq_ref[qh, :, pl.ds(qo, BLOCK)]
                bias = jnp.where(same, 0.0, masked_score)
                for h in range(heads):
                    at = slice(128 * h, 128 * h + 128)
                    vat = slice(64 * h, 64 * h + 64)
                    s = nt(km_ref[kh, pl.ds(ko, BLOCK), at], qp_ref[qh, pl.ds(qo, BLOCK), at]) + bias
                    m_old = m_sc[h : h + 1, :]
                    m_new = jnp.maximum(m_old, jnp.max(s, axis=0, keepdims=True))
                    alpha = jnp.exp(m_old - m_new)
                    p = jnp.exp(s - m_new)
                    m_sc[h : h + 1, :] = m_new
                    l_sc[h : h + 1, :] = alpha * l_sc[h : h + 1, :] + jnp.sum(p, axis=0, keepdims=True)
                    acc_sc[vat, :] = alpha * acc_sc[vat, :] + nn(
                        vt_ref[kh, vat, pl.ds(ko, BLOCK)], p.astype(bf16)
                    )

        cols = pl.ds(pl.multiple_of(qb * BLOCK, BLOCK), BLOCK)
        for h in range(heads):
            vat = slice(64 * h, 64 * h + 64)
            total = l_sc[h : h + 1, :]
            ct_ref[vat, cols] = acc_sc[vat, :] / total
            lse_ref[h : h + 1, cols] = m_sc[h : h + 1, :] + jnp.log(total)
        c_ref[qh, pl.ds(qo, BLOCK), :] = ct_ref[:, cols].T.astype(bf16)


def whole_micro(array):
    rest = array.shape[2:]
    return pl.BlockSpec((array.shape[0], None) + rest, lambda m, *_: (0, m) + (0,) * len(rest))


def attend(own_groups, other_groups, qp, km, vt, gk, gq):
    halves, micro, local, width = qp.shape
    half = width // 2
    heads = width // 128
    length = halves * local
    return pl.pallas_call(
        attend_kernel,
        grid_spec=pltpu.PrefetchScalarGridSpec(
            num_scalar_prefetch=2,
            grid=(micro,),
            in_specs=[whole_micro(a) for a in (qp, km, vt, gk, gq)],
            out_specs=[
                pl.BlockSpec((halves, None, local, half), lambda m, *_: (0, m, 0, 0)),
                pl.BlockSpec((None, half, length), lambda m, *_: (m, 0, 0)),
                pl.BlockSpec((None, 8, length), lambda m, *_: (m, 0, 0)),
            ],
            scratch_shapes=[
                pltpu.VMEM((8, BLOCK), f32),
                pltpu.VMEM((8, BLOCK), f32),
                pltpu.VMEM((half, BLOCK), f32),
            ],
        ),
        out_shape=[
            jax.ShapeDtypeStruct((halves, micro, local, half), bf16),
            jax.ShapeDtypeStruct((micro, half, length), f32),
            jax.ShapeDtypeStruct((micro, 8, length), f32),
        ],
        compiler_params=pltpu.CompilerParams(vmem_limit_bytes=VMEM_LIMIT),
        cost_estimate=cost(
            micro * heads * length * length * 512, micro * length * width * 8, micro * heads * length * length
        ),
        name="attend",
    )(own_groups, other_groups, qp, km, vt, gk, gq)


def attend_back_kernel(
    own_ref,
    other_ref,
    qp_ref,
    km_ref,
    kmt_ref,
    v_ref,
    dc_ref,
    ct_ref,
    lse_ref,
    gk_ref,
    gq_ref,
    kind_ref,
    d_ref,
    db_ref,
    dqt_sc,
    dk_sc,
    dv_sc,
    delta_sc,
):
    micro_at = pl.program_id(0)
    local, width = qp_ref.shape[1], qp_ref.shape[2]
    half = width // 2
    per = local // BLOCK
    blocks = 2 * per
    tiles = half // 128
    dk_sc[...] = jnp.zeros_like(dk_sc)
    dv_sc[...] = jnp.zeros_like(dv_sc)

    @pl.when(micro_at == 0)
    def _():
        db_ref[...] = jnp.zeros_like(db_ref)

    lo = low_lanes((BLOCK, 128))

    @pl.loop(0, blocks)
    def _(qb):
        qh, qo = place(qb, per)
        qrows = pl.ds(qo, BLOCK)
        cols = pl.ds(pl.multiple_of(qb * BLOCK, BLOCK), BLOCK)
        dct = dc_ref[qh, qrows, :].astype(f32).T
        inner = dct * ct_ref[:, cols]
        for h in range(2 * tiles):
            delta_sc[h : h + 1, :] = jnp.sum(inner[64 * h : 64 * h + 64, :], axis=0, keepdims=True)
        dqt_sc[...] = jnp.zeros_like(dqt_sc)
        q_low, q_high = ends_of(own_ref, other_ref, micro_at, qb, per)

        @pl.loop(0, blocks)
        def _(kb):
            k_low, k_high = ends_of(own_ref, other_ref, micro_at, kb, per)

            @pl.when((q_low <= k_high) & (k_low <= q_high))
            def _():
                kh, ko = place(kb, per)
                krows = pl.ds(ko, BLOCK)
                drows = pl.ds(pl.multiple_of(kb * BLOCK, BLOCK), BLOCK)
                same = gk_ref[kh, krows, :] == gq_ref[qh, :, qrows]
                bias = jnp.where(same, 0.0, masked_score)
                for t in range(tiles):
                    tat = slice(128 * t, 128 * t + 128)
                    v = v_ref[kh, krows, tat]
                    dc = dc_ref[qh, qrows, tat]
                    from_pair = []
                    for side in range(2):
                        h = 2 * t + side
                        at = slice(128 * h, 128 * h + 128)
                        q = qp_ref[qh, qrows, at]
                        s = nt(km_ref[kh, krows, at], q) + bias
                        p = jnp.exp(s - lse_ref[h : h + 1, cols])
                        zero = jnp.zeros_like(v)
                        vm = jnp.where(lo, v, zero) if side == 0 else jnp.where(lo, zero, v)
                        dp = nt(vm, dc)
                        ds = (p * (dp - delta_sc[h : h + 1, :])).astype(bf16)
                        dk_sc[drows, at] += nn(ds, q)
                        dqt_sc[at, :] += nn(kmt_ref[kh, at, krows], ds)
                        from_pair.append(nn(p.astype(bf16), dc))
                    dv_sc[drows, tat] += jnp.where(lo, from_pair[0], from_pair[1])

        dq = dqt_sc[...].T * 0.125
        entity = kind_ref[qh, qrows, :] == 1
        d_ref[qh, qrows, 0:width] = jnp.where(entity, 0.0, dq).astype(bf16)
        d_ref[qh, qrows, width : 2 * width] = jnp.where(entity, dq, 0.0).astype(bf16)

    @pl.loop(0, blocks)
    def _(kb):
        kh, ko = place(kb, per)
        krows = pl.ds(ko, BLOCK)
        drows = pl.ds(pl.multiple_of(kb * BLOCK, BLOCK), BLOCK)
        entity = kind_ref[kh, krows, :] == 1
        for t in range(tiles):
            even = dk_sc[drows, 256 * t : 256 * t + 128]
            odd = dk_sc[drows, 256 * t + 128 : 256 * t + 256]
            left = jnp.where(entity, pltpu.roll(even, 64, 1), even)
            right = jnp.where(entity, odd, pltpu.roll(odd, 64, 1))
            d_ref[kh, krows, 2 * width + 128 * t : 2 * width + 128 * t + 128] = jnp.where(
                lo, left, right
            ).astype(bf16)
        d_ref[kh, krows, 2 * width + half : 3 * width] = dv_sc[drows, :].astype(bf16)
        db_ref[0:1, :] += jnp.sum(d_ref[kh, krows, :].astype(f32), axis=0, keepdims=True)


def attend_back(own_groups, other_groups, qp, km, kmt, v, dc, ct, lse, gk, gq, kind_col):
    halves, micro, local, width = qp.shape
    half = width // 2
    heads = width // 128
    length = halves * local
    return pl.pallas_call(
        attend_back_kernel,
        grid_spec=pltpu.PrefetchScalarGridSpec(
            num_scalar_prefetch=2,
            grid=(micro,),
            in_specs=[whole_micro(a) for a in (qp, km, kmt, v, dc)]
            + [
                pl.BlockSpec((None, half, length), lambda m, *_: (m, 0, 0)),
                pl.BlockSpec((None, 8, length), lambda m, *_: (m, 0, 0)),
            ]
            + [whole_micro(a) for a in (gk, gq, kind_col)],
            out_specs=[
                pl.BlockSpec((halves, None, local, 3 * width), lambda m, *_: (0, m, 0, 0)),
                pl.BlockSpec((8, 3 * width), lambda m, *_: (0, 0)),
            ],
            scratch_shapes=[
                pltpu.VMEM((width, BLOCK), f32),
                pltpu.VMEM((length, width), f32),
                pltpu.VMEM((length, half), f32),
                pltpu.VMEM((8, BLOCK), f32),
            ],
        ),
        out_shape=[
            jax.ShapeDtypeStruct((halves, micro, local, 3 * width), bf16),
            jax.ShapeDtypeStruct((8, 3 * width), f32),
        ],
        compiler_params=pltpu.CompilerParams(vmem_limit_bytes=VMEM_LIMIT),
        cost_estimate=cost(
            micro * heads * length * length * 1280, micro * length * width * 16, micro * heads * length * length
        ),
        name="attend_back",
    )(own_groups, other_groups, qp, km, kmt, v, dc, ct, lse, gk, gq, kind_col)


def norm_forward(hidden):
    center = hidden - jnp.mean(hidden, axis=-1, keepdims=True)
    rescale = lax.rsqrt(jnp.mean(center * center, axis=-1, keepdims=True) + layer_eps)
    return center * rescale, rescale


def norm_backward(upstream, normed, rescale, gain):
    scaled = upstream * gain
    return rescale * (
        scaled
        - jnp.mean(scaled, axis=-1, keepdims=True)
        - normed * jnp.mean(scaled * normed, axis=-1, keepdims=True)
    )


def column_sum(values):
    return jnp.sum(values.astype(f32), axis=0, keepdims=True)


def chain_kernel(
    side_ref,
    x_ref,
    own_ref,
    far_ref,
    cot_ref,
    w_ref,
    vec_ref,
    mixed_ref,
    dh_ref,
    left_ref,
    right_ref,
    dco_ref,
    dcx_ref,
    sums_ref,
    slope_sc,
    z_sc,
    landed,
    c_send,
    c_recv,
):
    width = x_ref.shape[1]
    half = width // 2
    rows = width // GROUPS
    chunks = 4
    first = side_ref[0] == 0

    step_at = pl.program_id(0)
    blocks = landed.shape[0]
    per = far_ref.shape[2] // BLOCK
    across = (1 - lax.axis_index("seq"), lax.axis_index("shard"))

    def far_copy(i):
        return send(
            far_ref.at[1, i // per, pl.ds((i % per) * BLOCK, BLOCK), :],
            landed.at[i],
            c_send.at[i],
            c_recv.at[i],
            across,
        )

    @pl.when(step_at == 0)
    def _():
        sums_ref[...] = jnp.zeros_like(sums_ref)
        greet([across])
        for i in range(blocks):
            far_copy(i).start()

    for i in range(blocks):

        @pl.when(step_at == i)
        def _(i=i):
            far_copy(i).wait_recv()
            if i == blocks - 1:
                for k in range(blocks):
                    far_copy(k).wait_send()

    def vector(at):
        return vec_ref[at : at + 1, :]

    def up_chunk(j):
        at = pl.multiple_of(5 * rows + j * rows, 16)
        return w_ref[:, pl.ds(at, rows), :].reshape(width, width)

    def down_chunk(j):
        return w_ref[pl.ds(j * (GROUPS // chunks), GROUPS // chunks), 0 : 4 * rows, :].reshape(width, width)

    def out_weight():
        return w_ref[:, 4 * rows : 5 * rows, :].reshape(width, width)

    own = own_ref[...].astype(f32)
    other = landed[step_at].astype(f32)
    context = jnp.concatenate(
        [jnp.where(first, own, other), jnp.where(first, other, own)], axis=1
    ).astype(bf16)
    left_ref[:, 0:width] = context
    hidden = x_ref[...].astype(f32) + (nn(context, out_weight()) + vector(0))
    n1, r1 = norm_forward(hidden)
    y1 = n1 * vector(1) + vector(2)
    left_ref[:, width : 2 * width] = y1.astype(bf16)
    z_sc[...] = y1 + vector(7)

    @pl.loop(0, chunks)
    def _(j):
        u = nn(left_ref[:, width : 2 * width], up_chunk(j)) + vec_ref[pl.ds(j + 3, 1), :]
        cumulative = 0.5 * (1.0 + lax.erf(u * 0.7071067811865476))
        at = pl.multiple_of(j * width, 128)
        slope_sc[:, pl.ds(at, width)] = (
            cumulative + u * jnp.exp(-0.5 * u * u) * 0.3989422804014327
        )
        g = (u * cumulative).astype(bf16)
        left_ref[:, pl.ds(pl.multiple_of(at + 2 * width, 128), width)] = g
        z_sc[...] += nn(g, down_chunk(j))

    n2, r2 = norm_forward(z_sc[...])
    mixed_ref[...] = (n2 * vector(8) + vector(9)).astype(bf16)
    upstream = cot_ref[...].astype(f32)
    sums_ref[0:1, :] += column_sum(upstream * n2)
    sums_ref[1:2, :] += column_sum(upstream)
    dh2 = norm_backward(upstream, n2, r2, vector(8))
    dz = dh2.astype(bf16)
    right_ref[:, 5 * width :] = dz
    sums_ref[2:3, :] += column_sum(dz)
    z_sc[...] = dh2

    @pl.loop(0, chunks)
    def _(j):
        at = pl.multiple_of(j * width, 128)
        du = (
            nt(right_ref[:, 5 * width :], down_chunk(j)) * slope_sc[:, pl.ds(at, width)]
        ).astype(bf16)
        right_ref[:, pl.ds(pl.multiple_of(at + width, 128), width)] = du
        sums_ref[pl.ds(j + 8, 1), :] += column_sum(du)
        z_sc[...] += nt(du, up_chunk(j))

    dy1 = z_sc[...]
    hidden = x_ref[...].astype(f32) + (nn(left_ref[:, 0:width], out_weight()) + vector(0))
    n1, r1 = norm_forward(hidden)
    sums_ref[3:4, :] += column_sum(dy1 * n1)
    sums_ref[4:5, :] += column_sum(dy1)
    dh1 = norm_backward(dy1, n1, r1, vector(1))
    dh_ref[...] = dh1
    da = dh1.astype(bf16)
    right_ref[:, 0:width] = da
    sums_ref[5:6, :] += column_sum(da)
    dc = nt(da, out_weight())
    dco_ref[...] = jnp.where(first, dc[:, :half], dc[:, half:]).astype(bf16)
    dcx_ref[...] = jnp.where(first, dc[:, half:], dc[:, :half]).astype(bf16)


def chain(side, x, c, cot, weights, vectors):
    tokens, width = x.shape
    half = width // 2
    per = c.shape[2] // BLOCK
    blocks = tokens // BLOCK

    def rows_spec(cols):
        return pl.BlockSpec((BLOCK, cols), lambda i, *_: (i, 0))

    def shape(cols, kind):
        return jax.ShapeDtypeStruct((tokens, cols), kind)

    return pl.pallas_call(
        chain_kernel,
        grid_spec=pltpu.PrefetchScalarGridSpec(
            num_scalar_prefetch=1,
            grid=(tokens // BLOCK,),
            in_specs=[
                rows_spec(width),
                pl.BlockSpec((None, None, BLOCK, half), lambda i, *_: (0, i // per, i % per, 0)),
                pl.BlockSpec(memory_space=pl.ANY),
                rows_spec(width),
                pl.BlockSpec(weights.shape, lambda i, *_: (0, 0, 0), pipeline_mode=pl.Buffered(1)),
                pl.BlockSpec(vectors.shape, lambda i, *_: (0, 0)),
            ],
            out_specs=[
                rows_spec(width),
                rows_spec(width),
                rows_spec(6 * width),
                rows_spec(6 * width),
                rows_spec(half),
                rows_spec(half),
                pl.BlockSpec((16, width), lambda i, *_: (0, 0)),
            ],
            scratch_shapes=[
                pltpu.VMEM((BLOCK, 4 * width), f32),
                pltpu.VMEM((BLOCK, width), f32),
                pltpu.VMEM((blocks, BLOCK, half), bf16),
                pltpu.SemaphoreType.DMA((blocks,)),
                pltpu.SemaphoreType.DMA((blocks,)),
            ],
        ),
        out_shape=[
            shape(width, bf16),
            shape(width, f32),
            shape(6 * width, bf16),
            shape(6 * width, bf16),
            shape(half, bf16),
            shape(half, bf16),
            jax.ShapeDtypeStruct((16, width), f32),
        ],
        compiler_params=pltpu.CompilerParams(
            collective_id=3, has_side_effects=True, vmem_limit_bytes=VMEM_LIMIT
        ),
        cost_estimate=cost(2 * tokens * width * width * 19, tokens * width * 36 + weights.size * 2),
        name="chain",
    )(side[None], x, c, c, cot, weights, vectors)


def feed_grad_kernel(l_ref, r_ref, out_ref):
    width = l_ref.shape[1]
    rows = width // GROUPS
    at = pl.program_id(0)
    grad = tn(l_ref[...], r_ref[...]).astype(bf16)

    @pl.when(at == 0)
    def _():
        out_ref[:, 4 * rows : 5 * rows, :] = grad.reshape(GROUPS, rows, width)

    @pl.when((at >= 1) & (at < 5))
    def _():
        start = pl.multiple_of(5 * rows + (at - 1) * rows, 16)
        out_ref[:, pl.ds(start, rows), :] = grad.reshape(GROUPS, rows, width)

    @pl.when(at >= 5)
    def _():
        out_ref[pl.ds((at - 5) * 4, 4), 0 : 4 * rows, :] = grad.reshape(4, 4 * rows, width)


def chip_grad_kernel(l_ref, r_ref, keep_ref, give_ref, part, from_core, c_send, c_recv):
    width = l_ref.shape[1]
    rows = width // GROUPS
    at = pl.program_id(0)
    x, _, z, y, core = spots()
    partner = (x, slot_of(z, y, 1 - core))
    spans = [(slice(0, 8), 4 * rows + i * rows, rows) for i in range(5)]
    spans += [(slice(2 * j, 2 * j + 2), 0, 4 * rows) for j in range(4)]

    def copy_of(i):
        rails, start, size = spans[i]
        return send(
            part.at[rails, 1 - core, slice(start, start + size), :],
            from_core.at[rails, slice(start, start + size), :],
            c_send.at[i],
            c_recv.at[i],
            partner,
        )

    def add(i):
        rails, start, size = spans[i]
        copy_of(i).wait_recv()
        for rail in range(rails.start, rails.stop):
            mine = part[rail, core, start : start + size, :].astype(f32)
            theirs = from_core[rail, start : start + size, :].astype(f32)
            whole = mine + theirs
            left, right = whole[:, : width // 2], whole[:, width // 2 :]
            keep_ref[rail, start : start + size, :] = jnp.where(x == 0, left, right).astype(bf16)
            give_ref[rail, start : start + size, :] = jnp.where(x == 0, right, left).astype(bf16)

    @pl.when(at == 0)
    def _():
        greet([partner])

    grad = tn(l_ref[...], r_ref[...]).astype(bf16)
    for i in range(9):

        @pl.when(at == i)
        def _(i=i):
            rails, start, size = spans[i]
            count = rails.stop - rails.start
            part[rails, :, start : start + size, :] = grad.reshape(count, 2, size, width)
            copy_of(i).start()
            if i >= 2:
                add(i - 2)
            if i == 8:
                add(7)
                add(8)
                for k in range(9):
                    copy_of(k).wait_send()


def feed_grad(left, right, direct):
    tokens = left.shape[0]
    width = left.shape[1] // 6
    rows = width // GROUPS

    def left_at(i):
        return (0, jnp.where(i == 0, 0, jnp.where(i < 5, 1, i - 3)))

    def right_at(i):
        return (0, jnp.minimum(i, 5))

    out = (8, 9 * rows, width // 2) if direct else (GROUPS, 9 * rows, width)
    count = 2 if direct else 1
    scratch = [
        pltpu.VMEM((8, 2, 9 * rows, width), bf16),
        pltpu.VMEM((8, 9 * rows, width), bf16),
        pltpu.SemaphoreType.DMA((9,)),
        pltpu.SemaphoreType.DMA((9,)),
    ]
    extra = dict(collective_id=2, has_side_effects=True) if direct else {}
    return pl.pallas_call(
        chip_grad_kernel if direct else feed_grad_kernel,
        grid=(9,),
        in_specs=[
            pl.BlockSpec((tokens, width), left_at),
            pl.BlockSpec((tokens, width), right_at),
        ],
        out_specs=[pl.BlockSpec(out, lambda i: (0, 0, 0))] * count,
        out_shape=[jax.ShapeDtypeStruct(out, bf16)] * count,
        scratch_shapes=scratch if direct else (),
        compiler_params=pltpu.CompilerParams(vmem_limit_bytes=VMEM_LIMIT, **extra),
        cost_estimate=cost(2 * tokens * width * width * 9, tokens * width * 24 + width * width * 18),
        name="feed_grad",
    )(left, right)


def attn_grad_kernel(x_ref, d_ref, vec_ref, out_ref):
    width = x_ref.shape[1]
    rows = width // GROUPS
    at = pl.program_id(0)
    grad = tn(x_ref[...], d_ref[...]).astype(bf16)
    start = pl.multiple_of(at * rows, 16)
    out_ref[:, pl.ds(start, rows), :] = grad.reshape(GROUPS, rows, width)
    out_ref[:, 3 * rows :, :] = vec_ref[...]


def attn_grad(x, d, vectors):
    tokens, width = x.shape
    rows = width // GROUPS
    return pl.pallas_call(
        attn_grad_kernel,
        grid=(3,),
        in_specs=[
            pl.BlockSpec((tokens, width), lambda i: (0, 0)),
            pl.BlockSpec((tokens, width), lambda i: (0, i)),
            pl.BlockSpec((GROUPS, 16, width), lambda i: (0, 0, 0)),
        ],
        out_specs=pl.BlockSpec((GROUPS, 3 * rows + 16, width), lambda i: (0, 0, 0)),
        out_shape=jax.ShapeDtypeStruct((GROUPS, 3 * rows + 16, width), bf16),
        compiler_params=pltpu.CompilerParams(vmem_limit_bytes=VMEM_LIMIT),
        cost_estimate=cost(2 * tokens * width * width * 3, tokens * width * 8 + width * width * 6),
        name="attn_grad",
    )(x, d, vectors)


def scatter_kernel(
    x_ref,
    d_ref,
    vec_ref,
    w_ref,
    dh_ref,
    keep_ref,
    taken_ref,
    dx_ref,
    gq_ref,
    gk_ref,
    gv_ref,
    gvec_ref,
    feed_ref,
    part,
    from_core,
    from_y,
    from_z,
    from_x,
    out_y,
    out_z,
    total,
    feed_out_y,
    feed_from_y,
    feed_out_z,
    feed_from_z,
    feed_total,
    feed_from_x,
    fy_send,
    fy_recv,
    fz_send,
    fz_recv,
    fx_send,
    fx_recv,
    dx_out,
    from_dx,
    d_send,
    d_recv,
    c_send,
    c_recv,
    y_send,
    y_recv,
    z_send,
    z_recv,
    x_send,
    x_recv,
):
    width = x_ref.shape[1]
    half = width // 2
    rows = width // GROUPS
    step_at = pl.program_id(0)
    x, me, z, y, core = spots()
    across = (1 - x, me)
    beside = (x, slot_of(z, 1 - y, core))
    partner = (x, slot_of(z, y, 1 - core))
    spans = ((0, rows), (rows, rows), (2 * rows, rows + 16))

    def core_copy(chunk, rail):
        start, size = spans[chunk]
        return send(
            part.at[2 * rail + 1 - core, pl.ds(start, size), :],
            from_core.at[rail, pl.ds(start, size), :],
            c_send.at[chunk * 8 + rail],
            c_recv.at[chunk * 8 + rail],
            partner,
        )

    def z_order(step):
        return lax.rem(z + 1 + step, 4)

    def feed_chip(rail):
        return keep_ref[rail].astype(f32) + taken_ref[rail].astype(f32)

    def feed_y(zz):
        return send(feed_out_y.at[zz], feed_from_y.at[zz], fy_send.at[zz], fy_recv.at[zz], beside)

    def feed_z(zz):
        return send(
            feed_out_z.at[zz],
            feed_from_z.at[z],
            fz_send.at[zz],
            fz_recv.at[z],
            (x, slot_of(zz, y, core)),
        )

    @pl.when(step_at == 0)
    def _():
        greet(all_peers())
        for step in range(4):
            zz = z_order(step)
            feed_out_y[zz] = feed_chip(zz * 2 + 1 - y).astype(bf16)
            if step < 2:
                feed_y(zz).start()

    columns = pl.ds(pl.multiple_of(step_at * width, 128), width)
    grad = tn(x_ref[...], d_ref[:, columns]).astype(bf16)
    for chunk in range(3):

        @pl.when(step_at == chunk)
        def _(chunk=chunk):
            start = spans[chunk][0]
            part[:, start : start + rows, :] = grad.reshape(GROUPS, rows, width)
            if chunk == 2:
                part[:, 3 * rows :, :] = vec_ref[...]
            for rail in range(8):
                core_copy(chunk, rail).start()

    flat = dh_ref.shape[0]

    def input_part(start):
        found = None
        for i in range(3):
            piece = nt(
                d_ref[pl.ds(pl.multiple_of(start, BLOCK), BLOCK), i * width : i * width + width],
                w_ref[:, i * rows : i * rows + rows, :].reshape(width, width),
            )
            found = piece if found is None else found + piece
        return found

    @pl.when(step_at == 2)
    def _():
        def y_copy(zz):
            return send(out_y.at[zz], from_y.at[zz], y_send.at[zz], y_recv.at[zz], beside)

        def z_copy(zz):
            return send(
                out_z.at[zz], from_z.at[z], z_send.at[zz], z_recv.at[z], (x, slot_of(zz, y, core))
            )

        def core_wait(rail):
            for chunk in range(3):
                start, size = spans[chunk]
                send(
                    part.at[0, pl.ds(start, size), :],
                    from_core.at[rail, pl.ds(start, size), :],
                    c_send.at[0],
                    c_recv.at[chunk * 8 + rail],
                    partner,
                ).wait_recv()

        def chip(zz, yy):
            rail = zz * 2 + yy
            return part[2 * rail + core].astype(f32) + from_core[rail].astype(f32)

        def feed_forward(zz):
            feed_y(zz).wait_recv()
            feed_out_z[zz] = (feed_chip(zz * 2 + y) + feed_from_y[zz].astype(f32)).astype(bf16)
            feed_z(zz).start()

        def forward(zz):
            y_copy(zz).wait_recv()
            out_z[zz] = (chip(zz, y) + from_y[zz].astype(f32)).astype(bf16)
            z_copy(zz).start()

        feed_forward(z_order(0))
        feed_forward(z_order(1))
        feed_y(z_order(2)).start()
        feed_y(z_order(3)).start()

        @pl.loop(0, flat // BLOCK)
        def _(i):
            at = pl.ds(pl.multiple_of(i * BLOCK, BLOCK), BLOCK)
            dx_out[at, :] = input_part(flat + i * BLOCK).astype(bf16)

        exchange = send(dx_out, from_dx, d_send, d_recv, across)
        exchange.start()
        for rail in range(8):
            core_wait(rail)
        for step in range(4):
            zz = z_order(step)
            out_y[zz] = chip(zz, 1 - y).astype(bf16)
        feed_forward(z_order(2))
        y_copy(z_order(0)).start()
        y_copy(z_order(1)).start()

        @pl.loop(0, flat // BLOCK)
        def _(i):
            at = pl.ds(pl.multiple_of(i * BLOCK, BLOCK), BLOCK)
            dx_ref[at, :] = dh_ref[at, :] + input_part(i * BLOCK)

        forward(z_order(0))
        forward(z_order(1))
        y_copy(z_order(2)).start()
        y_copy(z_order(3)).start()
        feed_y(z).wait_recv()
        feed_result = feed_chip(z * 2 + y) + feed_from_y[z].astype(f32)
        for step in range(3):
            zz = z_order(step)
            send(
                feed_out_z.at[zz], feed_from_z.at[zz], fz_send.at[zz], fz_recv.at[zz], partner
            ).wait_recv()
            feed_result = feed_result + feed_from_z[zz].astype(f32)
        feed_total[...] = feed_result.astype(bf16)
        feed_last = send(feed_total, feed_from_x, fx_send, fx_recv, across)
        feed_last.start()
        forward(z_order(2))
        y_copy(z).wait_recv()
        result = chip(z, y) + from_y[z].astype(f32)
        for step in range(3):
            zz = z_order(step)
            send(out_z.at[zz], from_z.at[zz], z_send.at[zz], z_recv.at[zz], partner).wait_recv()
            result = result + from_z[zz].astype(f32)
        total[...] = result.astype(bf16)
        last = send(total, from_x, x_send, x_recv, across)
        last.start()
        exchange.wait()

        @pl.loop(0, flat // BLOCK)
        def _(i):
            at = pl.ds(pl.multiple_of(i * BLOCK, BLOCK), BLOCK)
            dx_ref[at, :] += from_dx[at, :].astype(f32)

        for chunk in range(3):
            for rail in range(8):
                core_copy(chunk, rail).wait_send()
        for step in range(4):
            y_copy(z_order(step)).wait_send()
            feed_y(z_order(step)).wait_send()
        for step in range(3):
            z_copy(z_order(step)).wait_send()
            feed_z(z_order(step)).wait_send()
        first = x == 0
        feed_last.wait()
        own_feed, far_feed = feed_total[...].astype(f32), feed_from_x[...].astype(f32)
        feed_ref[:, :half] = jnp.where(first, own_feed, far_feed)
        feed_ref[:, half:] = jnp.where(first, far_feed, own_feed)
        last.wait()
        lo = low_lanes((rows, 128))

        def ordered(start, size, at):
            own = total[start : start + size, at].astype(f32)
            other = from_x[start : start + size, at].astype(f32)
            return jnp.where(first, own, other), jnp.where(first, other, own)

        for e in range(2):
            for t in range(half // 128):
                evens = ordered(e * rows, rows, slice(256 * t, 256 * t + 128))
                odds = ordered(e * rows, rows, slice(256 * t + 128, 256 * t + 256))
                for s in range(2):
                    word = jnp.where(lo, evens[s], pltpu.roll(odds[s], 64, 1))
                    entity = jnp.where(lo, pltpu.roll(evens[s], 64, 1), odds[s])
                    base = 2 * e * width + s * half + 128 * t
                    gq_ref[:, base : base + 128] = word
                    gq_ref[:, base + width : base + width + 128] = entity
        for ref, base in ((gk_ref, 0), (gv_ref, half)):
            a, b = ordered(2 * rows, rows, slice(base, base + half))
            ref[:, :half] = a
            ref[:, half:] = b
        gvec_ref[...] = total[3 * rows :, :].astype(f32) + from_x[3 * rows :, :].astype(f32)


def scatter_attention(x, d, vectors, weights, dh, keep, taken):
    tokens, width = x.shape
    rows = width // GROUPS
    tall = 3 * rows + 16
    sem = pltpu.SemaphoreType.DMA

    def whole(*dims):
        return pl.BlockSpec(dims, lambda i: (0,) * len(dims), pipeline_mode=pl.Buffered(1))

    outs = (dh.shape, (rows, 4 * width), (rows, width), (rows, width), (16, width), (9 * rows, width))
    return pl.pallas_call(
        scatter_kernel,
        grid=(3,),
        in_specs=[
            whole(tokens, width),
            whole(*d.shape),
            whole(GROUPS, 16, width),
            whole(*weights.shape),
            whole(*dh.shape),
            whole(*keep.shape),
            whole(*keep.shape),
        ],
        out_specs=[whole(*dims) for dims in outs],
        out_shape=[jax.ShapeDtypeStruct(dims, f32) for dims in outs],
        scratch_shapes=[
            pltpu.VMEM((GROUPS, tall, width), bf16),
            pltpu.VMEM((8, tall, width), bf16),
            pltpu.VMEM((4, tall, width), bf16),
            pltpu.VMEM((4, tall, width), bf16),
            pltpu.VMEM((tall, width), bf16),
            pltpu.VMEM((4, tall, width), bf16),
            pltpu.VMEM((4, tall, width), bf16),
            pltpu.VMEM((tall, width), bf16),
            pltpu.VMEM((4,) + keep.shape[1:], bf16),
            pltpu.VMEM((4,) + keep.shape[1:], bf16),
            pltpu.VMEM((4,) + keep.shape[1:], bf16),
            pltpu.VMEM((4,) + keep.shape[1:], bf16),
            pltpu.VMEM(keep.shape[1:], bf16),
            pltpu.VMEM(keep.shape[1:], bf16),
            sem((4,)),
            sem((4,)),
            sem((4,)),
            sem((4,)),
            sem,
            sem,
            pltpu.VMEM(dh.shape, bf16),
            pltpu.VMEM(dh.shape, bf16),
            sem,
            sem,
            sem((24,)),
            sem((24,)),
            sem((4,)),
            sem((4,)),
            sem((4,)),
            sem((4,)),
            sem,
            sem,
        ],
        compiler_params=pltpu.CompilerParams(
            collective_id=1, has_side_effects=True, vmem_limit_bytes=VMEM_LIMIT
        ),
        cost_estimate=cost(2 * tokens * width * width * 3, tokens * width * 8 + width * width * 6),
        name="scatter",
    )(x, d, vectors, weights, dh, keep, taken)


def input_grad_kernel(d_ref, w_ref, out_ref):
    width = out_ref.shape[1]
    rows = width // GROUPS
    total = None
    for i in range(3):
        part = nt(
            d_ref[:, i * width : i * width + width],
            w_ref[:, i * rows : i * rows + rows, :].reshape(width, width),
        )
        total = part if total is None else total + part
    out_ref[...] = total.astype(out_ref.dtype)


def input_grad_part(d, weights, side_at, kind):
    _, micro, local, wide = d.shape
    width = wide // 3
    sub = local // BLOCK
    return pl.pallas_call(
        input_grad_kernel,
        grid=(micro, sub),
        in_specs=[
            pl.BlockSpec((None, None, BLOCK, wide), lambda m, i: (side_at, m, i, 0)),
            pl.BlockSpec(weights.shape, lambda m, i: (0, 0, 0)),
        ],
        out_specs=pl.BlockSpec((None, BLOCK, width), lambda m, i: (m, i, 0)),
        out_shape=jax.ShapeDtypeStruct((micro, local, width), kind),
        compiler_params=pltpu.CompilerParams(vmem_limit_bytes=VMEM_LIMIT),
        cost_estimate=cost(2 * micro * local * wide * width, micro * local * wide * 2 + weights.size * 2),
        name="input_grad",
    )(d, weights)


def assemble(attn_own, attn_other, side, head_dim, rows, piece):
    attn_own, attn_other = attn_own.astype(f32), attn_other.astype(f32)
    width = attn_own.shape[1]
    half = width // 2
    vec_total = attn_own[3 * rows, :piece] + attn_other[3 * rows, :piece]

    def by_side(own, other, axis):
        return jnp.where(
            side == 0,
            jnp.concatenate([own, other], axis=axis),
            jnp.concatenate([other, own], axis=axis),
        )

    def query_parts(block):
        pairs = jnp.stack([block[:rows], block[rows : 2 * rows]], axis=1)
        return unpair_columns(pairs, head_dim)

    grad_query = by_side(query_parts(attn_own), query_parts(attn_other), 3).reshape(rows, 4 * width)
    kv_own, kv_other = attn_own[2 * rows : 3 * rows], attn_other[2 * rows : 3 * rows]
    grad_key = by_side(kv_own[:, :half], kv_other[:, :half], 1)
    grad_value = by_side(kv_own[:, half:], kv_other[:, half:], 1)
    return grad_query, grad_key, grad_value, vec_total


def on_device(
    tokens,
    kinds,
    groups,
    query_weight,
    query_bias,
    key_weight,
    key_bias,
    value_weight,
    value_bias,
    output_weight,
    output_bias,
    norm1_gain,
    norm1_shift,
    up_weight,
    up_bias,
    down_weight,
    down_bias,
    norm2_gain,
    norm2_shift,
    cotangent,
):
    micro, _, local, width = tokens.shape
    half = width // 2
    head_dim = width // HEADS
    devices = lax.axis_size("shard")
    rows = width // devices
    side = lax.axis_index("seq").astype(jnp.int32)

    vectors = (
        query_bias,
        key_bias,
        value_bias,
        output_bias,
        norm1_gain,
        norm1_shift,
        up_bias,
        down_bias,
        norm2_gain,
        norm2_shift,
    )
    piece = 16 * rows
    direct = devices == GROUPS
    attn_sizes = (rows, rows, rows)
    feed_sizes = (4 * rows,) + (rows,) * 5
    if not direct:
        vector_row = jnp.pad(jnp.concatenate(vectors), (0, width - piece))[None]
        packed = pack_attention(query_weight, key_weight, value_weight, vector_row, side, head_dim)
        attn_gathered = lax.all_gather(packed[None], "shard", axis=0, tiled=True)
        other_tokens, other_kinds, other_groups = swap(tokens), swap(kinds), swap(groups)
    feed_local = pack_feed(down_weight, output_weight, up_weight)
    feed_gathered = lax.all_gather(feed_local[None], "shard", axis=0, tiled=True)
    if direct:
        attn_gathered, other_tokens, other_kinds, other_groups = gather_attention(
            query_weight, key_weight, value_weight, vectors, tokens, kinds, groups
        )
    vectors = attn_gathered[:, 3 * rows, :piece]
    if direct:
        attn_w, feed_w = attn_gathered, feed_gathered
    else:
        attn_w = regroup(attn_gathered, attn_sizes)
        feed_w = regroup(feed_gathered, feed_sizes)

    def whole_vector(start, size):
        return vectors[:, start : start + size].reshape(-1).astype(f32)

    full_query_bias = whole_vector(0, 4 * rows)
    full_key_bias = whole_vector(4 * rows, rows)
    full_value_bias = whole_vector(5 * rows, rows)
    bias_rows = jnp.concatenate(
        [
            pair_columns(full_query_bias, side, head_dim),
            jnp.concatenate([own_half(full_key_bias, side), own_half(full_value_bias, side)])[None],
        ],
        axis=0,
    )
    full_up_bias = whole_vector(9 * rows, 4 * rows).reshape(4, width)
    chain_vectors = jnp.concatenate(
        [
            whole_vector(6 * rows, rows)[None],
            whole_vector(7 * rows, rows)[None],
            whole_vector(8 * rows, rows)[None],
            full_up_bias,
            whole_vector(13 * rows, rows)[None],
            whole_vector(14 * rows, rows)[None],
            whole_vector(15 * rows, rows)[None],
        ],
        axis=0,
    )

    own_tokens = tokens[:, 0]
    own_groups, far_groups = groups.reshape(micro, local), other_groups.reshape(micro, local)
    qp, km, kmt, v, vt, xs, kind_col, gk, gq = project(
        tokens, other_tokens, kinds, other_kinds, groups, other_groups, attn_w, bias_rows
    )
    c, ct, lse = attend(own_groups, far_groups, qp, km, vt, gk, gq)
    flat = micro * local
    mixed, dh1, left, right, dc_own, dc_other, sums = chain(
        side,
        own_tokens.reshape(flat, width),
        c,
        cotangent.reshape(flat, width),
        feed_w,
        chain_vectors,
    )

    dc_swapped = swap(dc_other)
    feed_part = feed_grad(left, right, direct)
    dc_swapped, feed_part = lax.optimization_barrier((dc_swapped, feed_part))
    dc = jnp.stack([dc_own, dc_swapped]).reshape(2, micro, local, half)

    if direct:
        keep, give = feed_part
        taken = swap(give)
    else:
        feed_part = ungroup(feed_part[0], feed_sizes, devices)
        feed_sum = lax.psum_scatter(feed_part, "shard", scatter_dimension=0, tiled=True)[0]
    d, db = attend_back(own_groups, far_groups, qp, km, kmt, v, dc, ct, lse, gk, gq, kind_col)

    query_own = unpair_columns(db[0, : 2 * width].reshape(2, width), head_dim)
    zero = jnp.zeros((half,), f32)

    def spread(own):
        return jnp.where(side == 0, jnp.concatenate([own, zero]), jnp.concatenate([zero, own]))

    query_spread = jnp.concatenate([spread(query_own[e, w]) for e in range(2) for w in range(2)])
    key_spread = spread(db[0, 2 * width : 2 * width + half])
    value_spread = spread(db[0, 2 * width + half :])
    grad_vectors = jnp.concatenate(
        [
            query_spread.reshape(devices, 4 * rows),
            key_spread.reshape(devices, rows),
            value_spread.reshape(devices, rows),
            sums[5].reshape(devices, rows),
            sums[3].reshape(devices, rows),
            sums[4].reshape(devices, rows),
            sums[8:12].reshape(devices, 4 * rows),
            sums[2].reshape(devices, rows),
            sums[0].reshape(devices, rows),
            sums[1].reshape(devices, rows),
        ],
        axis=1,
    ).astype(bf16)
    grad_vectors = jnp.pad(grad_vectors[:, None, :], ((0, 0), (0, 15), (0, width - piece)))
    flat_x = xs.reshape(2 * flat, width)
    flat_d = d.reshape(2 * flat, 3 * width)
    if direct:
        input_grad, grad_query, grad_key, grad_value, vec_rows, feed_total = scatter_attention(
            flat_x, flat_d, grad_vectors, attn_w, dh1, keep, taken
        )
        input_grad = input_grad.reshape(micro, local, width)
        vec_total = vec_rows[0, :piece]
    else:
        zeros = jnp.zeros((GROUPS, 16, width), bf16)
        attn_part = attn_grad(flat_x, flat_d, zeros)
        attn_part = jnp.concatenate(
            [ungroup(attn_part[:, : 3 * (width // GROUPS)], attn_sizes, devices), grad_vectors], axis=1
        )
        attn_sum = lax.psum_scatter(attn_part, "shard", scatter_dimension=0, tiled=True)[0]
        attn_other = swap(attn_sum)
        grad_query, grad_key, grad_value, vec_total = assemble(
            attn_sum, attn_other, side, head_dim, rows, piece
        )
        dx_other = input_grad_part(d, attn_w, 1, bf16)
        dx_own = input_grad_part(d, attn_w, 0, f32)
        input_grad = dh1.reshape(micro, local, width) + dx_own + swap(dx_other).astype(f32)

    if not direct:
        feed_total = feed_sum.astype(f32) + swap(feed_sum).astype(f32)
    grad_down = feed_total[: 4 * rows]
    grad_output = feed_total[4 * rows : 5 * rows]
    grad_up = jnp.concatenate(
        [feed_total[(5 + j) * rows : (6 + j) * rows] for j in range(4)], axis=1
    )

    def piece_of(start, size):
        return vec_total[start : start + size]

    return (
        mixed.reshape(micro, 1, local, width),
        input_grad[:, None],
        grad_query,
        piece_of(0, 4 * rows),
        grad_key,
        piece_of(4 * rows, rows),
        grad_value,
        piece_of(5 * rows, rows),
        grad_output,
        piece_of(6 * rows, rows),
        piece_of(7 * rows, rows),
        piece_of(8 * rows, rows),
        grad_up,
        piece_of(9 * rows, 4 * rows),
        grad_down,
        piece_of(13 * rows, rows),
        piece_of(14 * rows, rows),
        piece_of(15 * rows, rows),
    )


def solution(mesh):
    weight = P("shard", None)
    vector = P("shard")
    tokens = P(None, "shard", "seq", None)
    marks = P(None, "shard", "seq")
    return jax.shard_map(
        on_device,
        mesh=mesh,
        in_specs=(tokens, marks, marks)
        + (weight, vector) * 4
        + (vector, vector)
        + (weight, vector) * 2
        + (vector, vector)
        + (tokens,),
        out_specs=(tokens, tokens)
        + (weight, vector) * 4
        + (vector, vector)
        + (weight, vector) * 2
        + (vector, vector),
        check_vma=False,
    )
```
